256 devices in a mesh: leaf: 64 (over x, y_lo, z), sub: 4 (over y_hi, core).
Axes of the slice: x: 4, y: 4 (y_hi: 2, y_lo: 2; y = y_hi * 2 + y_lo), z: 8, core: 2. Of those that a mesh axis runs over, the one named last changes fastest.
Arguments:
- field_in: float32 [2, 16, 393216], P(None, None, ('leaf', 'sub')), may hold values from -6 to 6
- compress: float32 [3072, 2, 64, 128], P(('leaf', 'sub')), may hold values from -0.375 to 0.375
- coupling: float32 [8, 3072, 2, 64, 128], P(None, ('leaf', 'sub')), may hold values from -0.375 to 0.375
- roster: int32 [8, 256, 12], P(None, ('leaf', 'sub')), may hold values from 0 to 11, each once within a row
- expand: float32 [3072, 2, 64, 128], P(('leaf', 'sub')), may hold values from -0.5 to 0.5
- nearfield_dense_blocks: float32 [3072, 2, 2, 128, 128], P(('leaf', 'sub')), may hold values from -0.25 to 0.25
- slot_owner_index: int32 [3072, 2], P(('leaf', 'sub')), may hold values from 0 to 3
- slot_source_position: int32 [3072, 2], P(('leaf', 'sub')), may hold values from 0 to 3
- slot_valid_mask: int32 [3072, 2], P(('leaf', 'sub')), may hold values 0 or 1
- near_pick: int32 [256, 4, 4], P(('leaf', 'sub')), may hold values from 0 to 11, as said below
Outputs:
- field_out: float32 [2, 16, 393216], P(None, None, ('leaf', 'sub'))
The draws below stay inside these ranges and needn't reach their ends.
Inputs may be any that keep to these rules, and one draw needn't show every extreme that they name: Each row of near_pick holds 4 distinct local leaf indices.
All inputs are finite; a program needn't handle non-finite values. No bound on the sum of `slot_valid_mask` on one device may be relied on, other than what follows from the above.
Results may differ from the reference program's by a relative error of at most 0.0001.
Values sent between devices are 32-bit elements; how exact they have to be, the bound alone decides.
No kernel may reach another device: no remote copies, remote signals or barrier semaphores. Data moves between devices by JAX's collectives and lax.ppermute only.
A program may use at most 64 MiB of HBM per device.

```python
import jax
import jax.numpy as jnp
from jax import lax

LEAF_ROW_COUNT = 128
RANK = 64
RHS = 16
DEVICE_LEAVES = 12
NEAR_SLOTS = 2
PEER_LEAF_LIMIT = 4
LEVELS = 8
TOTAL_LEAVES = 3072
ROWS = 393216
N_LEAF = 64
N_SUB = 4


def draw_near_pick(key, part):
    row_count = N_LEAF * N_SUB * N_SUB
    keys = jax.random.split(key, row_count)

    def one_row(row_key):
        return jax.random.permutation(row_key, DEVICE_LEAVES)
    shuffled = jax.vmap(one_row)(keys)
    return shuffled[:, :PEER_LEAF_LIMIT].reshape(N_LEAF * N_SUB, N_SUB, PEER_LEAF_LIMIT).astype(jnp.int32)


def with_ends(result, key, low, high):
    spot = [jax.random.randint(jax.random.fold_in(key, axis), (), 0, length) for axis, length in enumerate(result.shape)]
    longest = result.shape.index(max(result.shape))
    next_to = spot[:longest] + [(spot[longest] + 1) % result.shape[longest]] + spot[longest + 1:]
    return result.at[tuple(spot)].set(low).at[tuple(next_to)].set(high)


def shard_levels(key, dims, cuts, least, high):
    level = 1.0
    for axis_at, blocks in cuts:
        draws = jax.random.uniform(jax.random.fold_in(jax.random.fold_in(key, 6), axis_at), (blocks,), jnp.float32, least / len(cuts), high / len(cuts))
        level = level * jnp.repeat(jnp.exp(draws), dims[axis_at] // blocks).reshape((-1,) + (1,) * (len(dims) - 1 - axis_at))
    return level


def centred(stream_key, extent, width, reach, pieces=(), kind=jnp.bfloat16):
    result = jax.random.normal(stream_key, extent, jnp.float32) * width
    if len(pieces) > 0:
        result = shard_levels(stream_key, extent, pieces, -0.22, 0.18) * result
    return jnp.clip(result, min=-reach, max=reach).astype(kind)


def setup_inputs(seed: int = 0) -> dict:
    key_of = jax.random.split(jax.random.key(seed), 11)
    return {
        "field_in": centred(key_of[0], (2, RHS, ROWS), 1.0, 6.0, ((2, 256),), jnp.float32),
        "compress": centred(key_of[1], (TOTAL_LEAVES, 2, RANK, LEAF_ROW_COUNT), (2 * LEAF_ROW_COUNT) ** -0.5, 0.375, ((0, 256),), jnp.float32),
        "coupling": centred(key_of[2], (LEVELS, TOTAL_LEAVES, 2, RANK, 2 * RANK), (4 * RANK) ** -0.5, 0.375, ((1, 256),), jnp.float32),
        "roster": jax.vmap(lambda own: jax.random.permutation(own, DEVICE_LEAVES))(jax.random.split(key_of[3], LEVELS * (N_LEAF * N_SUB))).reshape((LEVELS, N_LEAF * N_SUB, DEVICE_LEAVES)).astype(jnp.int32),
        "expand": centred(key_of[4], (TOTAL_LEAVES, 2, RANK, LEAF_ROW_COUNT), (2 * RANK) ** -0.5, 0.5, ((0, 256),), jnp.float32),
        "nearfield_dense_blocks": centred(key_of[5], (TOTAL_LEAVES, NEAR_SLOTS, 2, LEAF_ROW_COUNT, LEAF_ROW_COUNT), (2 * LEAF_ROW_COUNT * NEAR_SLOTS) ** -0.5, 0.25, ((0, 256),), jnp.float32),
        "slot_owner_index": with_ends(jax.random.randint(key_of[6], (TOTAL_LEAVES, NEAR_SLOTS), 0, N_SUB), jax.random.fold_in(key_of[6], 1), 0, N_SUB - 1).astype(jnp.int32),
        "slot_source_position": with_ends(jax.random.randint(key_of[7], (TOTAL_LEAVES, NEAR_SLOTS), 0, PEER_LEAF_LIMIT), jax.random.fold_in(key_of[7], 1), 0, PEER_LEAF_LIMIT - 1).astype(jnp.int32),
        "slot_valid_mask": with_ends((jax.random.randint(key_of[8], (TOTAL_LEAVES, NEAR_SLOTS), 0, 3) < 2).astype(jnp.int32), jax.random.fold_in(key_of[8], 1), 0, 1),
        "near_pick": draw_near_pick(jax.random.fold_in(key_of[10], 71), 0),
    }


def complex_product(factor, stacked, pattern):
    products = jnp.einsum(pattern, factor, stacked, precision=lax.Precision.HIGHEST)
    return jnp.stack([products[0, 0] - products[1, 1], products[0, 1] + products[1, 0]])


def reference(field_in, compress, coupling, roster, expand, nearfield_dense_blocks, slot_owner_index, slot_source_position, slot_valid_mask, near_pick):
    device_total = N_LEAF * N_SUB
    columns = field_in.reshape(2, RHS, device_total, DEVICE_LEAVES, LEAF_ROW_COUNT).transpose(0, 2, 1, 3, 4)
    bases = compress.reshape(device_total, DEVICE_LEAVES, 2, RANK, LEAF_ROW_COUNT)
    coeffs = complex_product(bases, columns, "bkcij,dbskj->cdbski")
    logl = N_LEAF.bit_length() - 1
    flips = [logl + 1, logl, logl - 1, 0, 1, logl - 1, logl, logl + 1]
    numbers = jnp.arange(device_total, dtype=jnp.int32)
    for position in range(LEVELS):
        partner = coeffs[:, numbers ^ (1 << flips[position])]
        pairing = roster[position]
        aligned = jnp.take_along_axis(partner, pairing[None, :, None, :, None], axis=3)
        stacked = jnp.concatenate([coeffs, aligned], axis=-1)
        factor = coupling[position].reshape(device_total, DEVICE_LEAVES, 2, RANK, 2 * RANK)
        coeffs = complex_product(factor, stacked, "bkcij,dbskj->cdbski")
    rows_basis = expand.reshape(device_total, DEVICE_LEAVES, 2, RANK, LEAF_ROW_COUNT)
    far = complex_product(rows_basis, coeffs, "bkcji,dbskj->cdbski")
    holder_index = slot_owner_index.reshape(device_total, DEVICE_LEAVES, NEAR_SLOTS)
    list_position = slot_source_position.reshape(device_total, DEVICE_LEAVES, NEAR_SLOTS)
    slot_is_valid = slot_valid_mask.reshape(device_total, DEVICE_LEAVES, NEAR_SLOTS).astype(jnp.float32)
    number_grid = numbers[:, None, None]
    source_device = (number_grid // N_SUB) * N_SUB + holder_index
    source_leaf = near_pick[number_grid, holder_index, list_position]
    sources = columns[:, source_device, :, source_leaf, :]
    sources = sources * slot_is_valid[:, :, :, None, None, None]
    leaf_blocks = nearfield_dense_blocks.reshape(device_total, DEVICE_LEAVES, NEAR_SLOTS, 2, LEAF_ROW_COUNT, LEAF_ROW_COUNT)
    near = complex_product(leaf_blocks, sources, "bktcij,bktdsj->cdbski")
    total = far + near
    return total.transpose(0, 2, 1, 3, 4).reshape(2, RHS, device_total * DEVICE_LEAVES * LEAF_ROW_COUNT)
```

```python
import functools

import jax
import jax.numpy as jnp
from jax import lax
from jax.experimental import pallas as pl
from jax.experimental.pallas import tpu as pltpu
from jax.sharding import PartitionSpec as P

VMEM = pltpu.VMEM
SMEM = pltpu.SMEM
BF = jnp.bfloat16
F32 = jnp.float32
NT = (((1,), (1,)), ((), ()))
NN = (((1,), (0,)), ((), ()))


def split(value):
    high = value.astype(BF)
    return high, (value - high.astype(F32)).astype(BF)


def product(rows, weights, dims):
    count = rows.shape[0]
    rows_high, rows_low = split(rows)
    w_high, w_low = split(weights)
    both = jnp.concatenate([rows_high, rows_low], axis=0)
    first = lax.dot_general(both, w_high, dims, preferred_element_type=F32)
    second = lax.dot_general(rows_high, w_low, dims, preferred_element_type=F32)
    return first[:count] + first[count:] + second


def lane_low(shape):
    return lax.broadcasted_iota(jnp.int32, shape, 1) < 64


def joined(result):
    rhs = result.shape[0] // 2
    turned = pltpu.roll(result[rhs:], 64, axis=1)
    return result[:rhs] + jnp.where(lane_low(turned.shape), -turned, turned)


def compress_kernel(field_ref, weight_ref, out_ref):
    for k in range(out_ref.shape[0]):
        rows = jnp.concatenate(
            [field_ref[0, :, pl.ds(128 * k, 128)], field_ref[1, :, pl.ds(128 * k, 128)]], axis=0
        )
        out_ref[k] = joined(product(rows, weight_ref[k].reshape(128, 128), NT))


def stacked_rows(own, other):
    low = lane_low(own.shape)
    real = jnp.where(low, own, pltpu.roll(other, 64, axis=1))
    imag = jnp.where(low, pltpu.roll(own, 64, axis=1), other)
    return jnp.concatenate([real, imag], axis=0)


def level_kernel(level, roster_ref, own_ref, other_ref, weight_ref, *rest):
    out_ref = rest[-1]
    for k in range(out_ref.shape[0]):
        rows = stacked_rows(own_ref[k], other_ref[roster_ref[level, k]])
        out_ref[k] = joined(product(rows, weight_ref[level, k].reshape(128, 128), NT))


def last_kernel(level, roster_ref, own_ref, other_ref, weight_ref, expand_ref, *rest):
    near_refs, out_ref = rest[:-1], rest[-1]
    each = near_refs[0].shape[0]
    for k in range(own_ref.shape[0]):
        rows = stacked_rows(own_ref[k], other_ref[roster_ref[level, k]])
        coeffs = joined(product(rows, weight_ref[level, k].reshape(128, 128), NT))
        signed = jnp.where(lane_low(coeffs.shape), coeffs, -coeffs)
        turned = pltpu.roll(coeffs, 64, axis=1)
        far = product(jnp.concatenate([signed, turned], axis=0), expand_ref[k].reshape(128, 128), NN)
        total = far + near_refs[k // each][k % each]
        half = total.shape[0] // 2
        out_ref[0, :, pl.ds(128 * k, 128)] = total[:half]
        out_ref[1, :, pl.ds(128 * k, 128)] = total[half:]


def near_kernel(first, me_ref, owner_ref, place_ref, valid_ref, pick_ref, own_ref, core_ref, far_ref, both_ref, weight_ref, *rest):
    out_ref = rest[-1]
    me = me_ref[0]
    for n in range(out_ref.shape[0]):
        k = first + n
        total = None
        for t in range(weight_ref.shape[1]):
            owner = owner_ref[k, t]
            leaf = pick_ref[owner, place_ref[k, t]]
            lanes = pl.ds(pl.multiple_of(leaf * 128, 128), 128)
            which = owner ^ me
            parts = []
            for d in range(2):
                low = jnp.where(which == 1, core_ref[d, :, lanes], own_ref[d, :, lanes])
                high = jnp.where(which == 3, both_ref[d, :, lanes], far_ref[d, :, lanes])
                parts.append(jnp.where(which >= 2, high, low))
            rows = jnp.concatenate(parts, axis=0) * valid_ref[k, t].astype(F32)
            result = product(rows, weight_ref[k, t].reshape(256, 128), NT)
            half = result.shape[0] // 2
            term = jnp.concatenate(
                [result[:half, :128] - result[half:, 128:], result[half:, :128] + result[:half, 128:]], axis=0
            )
            total = term if total is None else total + term
        out_ref[n] = total


def spec(space):
    return pl.BlockSpec(memory_space=space)


def call(kernel, out, spaces, name, flops=2_000_000):
    return pl.pallas_call(
        kernel,
        out_shape=out,
        in_specs=[spec(space) for space in spaces],
        out_specs=spec(VMEM),
        compiler_params=pltpu.CompilerParams(vmem_limit_bytes=8 << 20),
        cost_estimate=pl.CostEstimate(flops=flops, bytes_accessed=1 << 20, transcendentals=0),
        name=name,
    )


def flipped(value, axis, mask):
    pairs = [(source, source ^ mask) for source in range(lax.axis_size(axis))]
    return lax.ppermute(value, axis, pairs)


def on_device(
    field_in,
    compress,
    coupling,
    roster,
    expand,
    nearfield_dense_blocks,
    slot_owner_index,
    slot_source_position,
    slot_valid_mask,
    near_pick,
):
    blocks = compress.shape[0]
    rhs = field_in.shape[1]
    leaf_count = lax.axis_size("leaf")
    top = leaf_count // 2
    plan = [
        ("leaf", top),
        ("leaf", top // 2),
        ("leaf", top // 4),
        ("sub", 1),
        ("sub", 2),
        ("leaf", top // 4),
        ("leaf", top // 2),
        ("leaf", top),
    ]
    me = lax.axis_index("sub").astype(jnp.int32).reshape(1)
    names = roster[:, 0]
    pick = near_pick[0]
    state = jax.ShapeDtypeStruct((blocks, rhs, 128), F32)
    field = pltpu.with_memory_space_constraint(field_in, VMEM)
    weights = pltpu.with_memory_space_constraint(coupling, VMEM)
    first = pltpu.with_memory_space_constraint(compress, VMEM)
    last = pltpu.with_memory_space_constraint(expand, VMEM)
    dense = pltpu.with_memory_space_constraint(nearfield_dense_blocks, VMEM)

    coeffs = call(compress_kernel, state, [VMEM, VMEM], "compress")(field, first)
    each = 2
    near_at = {2: 1, 3: 0, 4: 1, 5: 1, 6: 1, 7: 2}
    pieces = []
    for position, (axis, mask) in enumerate(plan):
        other = flipped(coeffs, axis, mask)
        if position == 0:
            far = flipped(field_in, "sub", 2)
            core = flipped(field_in, "sub", 1)
        if position == 1:
            both = flipped(far, "sub", 1)
        extra = []
        for _ in range(near_at.get(position, 0)):
            kernel = functools.partial(near_kernel, each * len(pieces))
            piece = call(
                kernel,
                jax.ShapeDtypeStruct((each, 2 * rhs, 128), F32),
                [SMEM] * 5 + [VMEM] * 5 + [pl.ANY],
                "near",
            )(me, slot_owner_index, slot_source_position, slot_valid_mask, pick, field, core, far, both, dense, coeffs)
            pieces.append(piece)
            extra.append(piece)
        if position < len(plan) - 1:
            coeffs = call(
                functools.partial(level_kernel, position),
                state,
                [SMEM, VMEM, VMEM, VMEM] + [pl.ANY] * len(extra),
                "level",
            )(names, coeffs, other, weights, *extra)
        else:
            total = call(
                functools.partial(last_kernel, position),
                jax.ShapeDtypeStruct(field_in.shape, F32),
                [SMEM] + [VMEM] * (4 + len(pieces)),
                "last",
            )(names, coeffs, other, weights, last, *pieces)
    return total


def solution(mesh):
    return jax.shard_map(
        on_device,
        mesh=mesh,
        in_specs=(
            P(None, None, ("leaf", "sub")),
            P(("leaf", "sub"), None, None, None),
            P(None, ("leaf", "sub"), None, None, None),
            P(None, ("leaf", "sub"), None),
            P(("leaf", "sub"), None, None, None),
            P(("leaf", "sub"), None, None, None, None),
            P(("leaf", "sub"), None),
            P(("leaf", "sub"), None),
            P(("leaf", "sub"), None),
            P(("leaf", "sub"), None, None),
        ),
        out_specs=P(None, None, ("leaf", "sub")),
        check_vma=False,
    )
```

```python
import functools

import jax
import jax.numpy as jnp
from jax import lax
from jax.experimental import pallas as pl
from jax.experimental.pallas import tpu as pltpu
from jax.sharding import PartitionSpec as P

VMEM = pltpu.VMEM
SMEM = pltpu.SMEM
ANY = pl.ANY
HBM = pltpu.HBM
DMA = pltpu.SemaphoreType.DMA
BF = jnp.bfloat16
F32 = jnp.float32
NT = (((1,), (1,)), ((), ()))
NN = (((1,), (0,)), ((), ()))
NEAR_EACH = 3
NEAR_AT = {4: 1, 5: 1, 6: 1, 7: 1}


def split(value):
    high = value.astype(BF)
    return high, (value - high.astype(F32)).astype(BF)


def product(rows, weights, dims):
    count = rows.shape[0]
    high, low = split(rows)
    stacked = jnp.concatenate(
        [
            jnp.concatenate([high, high], axis=1),
            jnp.concatenate([low, jnp.zeros_like(low)], axis=1),
        ],
        axis=0,
    )
    wide = jnp.concatenate(split(weights), axis=dims[0][1][0])
    result = lax.dot_general(stacked, wide, dims, preferred_element_type=F32)
    return result[:count] + result[count:]


def lane_low(shape):
    return lax.broadcasted_iota(jnp.int32, shape, 1) < 64


def joined(result):
    rhs = result.shape[0] // 2
    turned = pltpu.roll(result[rhs:], 64, axis=1)
    return result[:rhs] + jnp.where(lane_low(turned.shape), -turned, turned)


def compress_kernel(field_hbm, weight_hbm, out_ref, field_ref, weight_ref, sems):
    blocks = out_ref.shape[0]
    chunk = blocks // 3
    field_copy = pltpu.make_async_copy(field_hbm, field_ref, sems.at[3])
    field_copy.start()
    copies = []
    for n in range(3):
        part = pl.ds(n * chunk, chunk)
        copy = pltpu.make_async_copy(weight_hbm.at[part], weight_ref.at[part], sems.at[n])
        copy.start()
        copies.append(copy)
    field_copy.wait()
    for k in range(blocks):
        if k % chunk == 0:
            copies[k // chunk].wait()
        lanes = pl.ds(128 * k, 128)
        rows = jnp.concatenate([field_ref[0, :, lanes], field_ref[1, :, lanes]], axis=0)
        out_ref[k] = joined(product(rows, weight_ref[k].reshape(128, 128), NT))


def stacked_rows(own, other):
    low = lane_low(own.shape)
    real = jnp.where(low, own, pltpu.roll(other, 64, axis=1))
    imag = jnp.where(low, pltpu.roll(own, 64, axis=1), other)
    return jnp.concatenate([real, imag], axis=0)


def level_block(level, k, row, own_ref, other_ref, weight_ref):
    rows = stacked_rows(own_ref[k], other_ref[row[0, k]])
    return joined(product(rows, weight_ref[level, k].reshape(128, 128), NT))


def level_kernel(level, roster_ref, own_ref, other_ref, weight_ref, *rest):
    out_ref = rest[-1]
    row = roster_ref[level]
    for k in range(out_ref.shape[0]):
        out_ref[k] = level_block(level, k, row, own_ref, other_ref, weight_ref)


def last_kernel(level, roster_ref, own_ref, other_ref, weight_ref, expand_ref, *rest):
    near_refs, (out_hbm, state_ref, out_ref, sems) = rest[:-4], rest[-4:]
    row = roster_ref[level]
    blocks = own_ref.shape[0]
    each = near_refs[0].shape[0]
    for k in range(blocks):
        state_ref[k] = level_block(level, k, row, own_ref, other_ref, weight_ref)
    copies = []
    for k in range(blocks):
        coeffs = state_ref[k]
        signed = jnp.where(lane_low(coeffs.shape), coeffs, -coeffs)
        turned = pltpu.roll(coeffs, 64, axis=1)
        far = product(jnp.concatenate([signed, turned], axis=0), expand_ref[k].reshape(128, 128), NN)
        total = far + near_refs[k // each][k % each]
        half = total.shape[0] // 2
        lanes = pl.ds(128 * k, 128)
        out_ref[0, :, lanes] = total[:half]
        out_ref[1, :, lanes] = total[half:]
        if k % 4 == 3:
            part = pl.ds(128 * (k - 3), 512)
            copy = pltpu.make_async_copy(out_ref.at[:, :, part], out_hbm.at[:, :, part], sems.at[k // 4])
            copy.start()
            copies.append(copy)
    for copy in copies:
        copy.wait()


def near_kernel(first, owner_ref, place_ref, valid_ref, pick_ref, own_ref, core_ref, far_ref, both_ref, weight_ref, *rest):
    out_ref = rest[-1]
    me = lax.axis_index("sub")
    for n in range(out_ref.shape[0]):
        k = first + n
        total = None
        for t in range(weight_ref.shape[1]):
            owner = owner_ref[t, k]
            leaf = pick_ref[owner, place_ref[t, k]]
            lanes = pl.ds(pl.multiple_of(leaf * 128, 128), 128)
            which = owner ^ me
            parts = []
            for d in range(2):
                low = jnp.where(which == 1, core_ref[d, :, lanes], own_ref[d, :, lanes])
                high = jnp.where(which == 3, both_ref[d, :, lanes], far_ref[d, :, lanes])
                parts.append(jnp.where(which >= 2, high, low))
            rows = jnp.concatenate(parts, axis=0) * valid_ref[t, k].astype(F32)
            result = product(rows, weight_ref[k, t].reshape(256, 128), NT)
            half = result.shape[0] // 2
            term = jnp.concatenate(
                [result[:half, :128] - result[half:, 128:], result[half:, :128] + result[:half, 128:]], axis=0
            )
            total = term if total is None else total + term
        out_ref[n] = total


def fetch_kernel(*refs):
    count = (len(refs) - 2) // 2
    sources, outs, sem = refs[:count], refs[count + 1 : -1], refs[-1]
    copies = [pltpu.make_async_copy(s, o, sem.at[n]) for n, (s, o) in enumerate(zip(sources, outs))]
    for copy in copies:
        copy.start()
    for copy in copies:
        copy.wait()


def spec(space):
    return pl.BlockSpec(memory_space=space)


def call(kernel, out, spaces, name, out_spaces=VMEM, scratch=(), flops=2_000_000):
    single = not isinstance(out_spaces, (list, tuple))
    return pl.pallas_call(
        kernel,
        out_shape=out,
        in_specs=[spec(space) for space in spaces],
        out_specs=spec(out_spaces) if single else [spec(space) for space in out_spaces],
        scratch_shapes=list(scratch),
        compiler_params=pltpu.CompilerParams(vmem_limit_bytes=8 << 20),
        cost_estimate=pl.CostEstimate(flops=flops, bytes_accessed=1 << 20, transcendentals=0),
        name=name,
    )


def fetch(arrays, after, name):
    return call(
        fetch_kernel,
        [VMEM(a.shape, a.dtype) for a in arrays],
        [HBM] * len(arrays) + [ANY],
        name,
        [VMEM] * len(arrays),
        [DMA((len(arrays),))],
    )(*[pltpu.with_memory_space_constraint(a, HBM) for a in arrays], after)


def flipped(value, axis, mask):
    pairs = [(source, source ^ mask) for source in range(lax.axis_size(axis))]
    return lax.ppermute(value, axis, pairs)


def tied(value, after):
    return lax.optimization_barrier((value, after))[0]


def on_device(
    field_in,
    compress,
    coupling,
    roster,
    expand,
    nearfield_dense_blocks,
    slot_owner_index,
    slot_source_position,
    slot_valid_mask,
    near_pick,
):
    blocks = compress.shape[0]
    rhs = field_in.shape[1]
    leaf_count = lax.axis_size("leaf")
    top = leaf_count // 2
    plan = [
        ("leaf", top),
        ("leaf", top // 2),
        ("leaf", top // 4),
        ("sub", 1),
        ("sub", 2),
        ("leaf", top // 4),
        ("leaf", top // 2),
        ("leaf", top),
    ]
    pick = near_pick[0]
    indices = (slot_owner_index.T, slot_source_position.T, slot_valid_mask.T, pick)
    state = VMEM((blocks, rhs, 128), F32)

    coeffs = call(
        compress_kernel,
        state,
        [HBM, HBM],
        "compress",
        scratch=[VMEM(field_in.shape, F32), VMEM(compress.shape, F32), DMA((4,))],
    )(pltpu.with_memory_space_constraint(field_in, HBM), pltpu.with_memory_space_constraint(compress, HBM))
    pieces = []
    for position, (axis, mask) in enumerate(plan):
        other = flipped(coeffs, axis, mask)
        extra = []
        if position == 0:
            far = flipped(tied(field_in, coeffs), "sub", 2)
            core = flipped(tied(field_in, coeffs), "sub", 1)
            weights, names = fetch([coupling, roster], coeffs, "fetch_coupling")
        if position == 1:
            dense, last, field = fetch([nearfield_dense_blocks, expand, field_in], coeffs, "fetch_near")
            extra.append(field)
        if position == 2:
            both = flipped(tied(far, coeffs), "sub", 1)
        for _ in range(NEAR_AT.get(position, 0)):
            piece = call(
                functools.partial(near_kernel, NEAR_EACH * len(pieces)),
                VMEM((NEAR_EACH, 2 * rhs, 128), F32),
                [SMEM] * 4 + [VMEM] * 5 + [ANY],
                "near",
            )(*indices, field, core, far, both, dense, coeffs)
            pieces.append(piece)
            extra.append(piece)
        if position < len(plan) - 1:
            coeffs = call(
                functools.partial(level_kernel, position),
                state,
                [VMEM] * 4 + [ANY] * len(extra),
                "level",
            )(names, coeffs, other, weights, *extra)
        else:
            total = call(
                functools.partial(last_kernel, position),
                jax.ShapeDtypeStruct(field_in.shape, F32),
                [VMEM] * (5 + len(pieces)),
                "last",
                HBM,
                [VMEM((blocks, rhs, 128), F32), VMEM(field_in.shape, F32), DMA((3,))],
            )(names, coeffs, other, weights, last, *pieces)
    return total


def solution(mesh):
    return jax.shard_map(
        on_device,
        mesh=mesh,
        in_specs=(
            P(None, None, ("leaf", "sub")),
            P(("leaf", "sub"), None, None, None),
            P(None, ("leaf", "sub"), None, None, None),
            P(None, ("leaf", "sub"), None),
            P(("leaf", "sub"), None, None, None),
            P(("leaf", "sub"), None, None, None, None),
            P(("leaf", "sub"), None),
            P(("leaf", "sub"), None),
            P(("leaf", "sub"), None),
            P(("leaf", "sub"), None, None),
        ),
        out_specs=P(None, None, ("leaf", "sub")),
        check_vma=False,
    )
```

```python
import functools

import jax
import jax.numpy as jnp
from jax import lax
from jax.experimental import pallas as pl
from jax.experimental.pallas import tpu as pltpu
from jax.sharding import PartitionSpec as P


VMEM = pltpu.VMEM
SMEM = pltpu.SMEM
ANY = pl.ANY
HBM = pltpu.HBM
DMA = pltpu.SemaphoreType.DMA
BF = jnp.bfloat16
F32 = jnp.float32
NT = (((1,), (1,)), ((), ()))
NN = (((1,), (0,)), ((), ()))
NEAR_EACH = 4
HALF = 8
NEAR_AT = {5: 1, 6: 1, 7: 1}


def split(value):
    high = value.astype(BF)
    return high, (value - high.astype(F32)).astype(BF)


def product(rows, weights, dims):
    count = rows.shape[0]
    high, low = split(rows)
    stacked = jnp.concatenate(
        [
            jnp.concatenate([high, high], axis=1),
            jnp.concatenate([low, jnp.zeros_like(low)], axis=1),
        ],
        axis=0,
    )
    wide = jnp.concatenate(split(weights), axis=dims[0][1][0])
    result = lax.dot_general(stacked, wide, dims, preferred_element_type=F32)
    return result[:count] + result[count:]


def lane_low(shape):
    return lax.broadcasted_iota(jnp.int32, shape, 1) < 64


def joined(result):
    rhs = result.shape[0] // 2
    turned = pltpu.roll(result[rhs:], 64, axis=1)
    return result[:rhs] + jnp.where(lane_low(turned.shape), -turned, turned)


def compress_block(half, k, field_ref, weight_ref, out_ref):
    part = pl.ds(half * HALF, HALF)
    lanes = pl.ds(128 * k, 128)
    rows = jnp.concatenate([field_ref[0, part, lanes], field_ref[1, part, lanes]], axis=0)
    out_ref[k] = joined(product(rows, weight_ref[k].reshape(128, 128), NT))


def compress_kernel(field_hbm, weight_hbm, coupling_hbm, roster_hbm, out_ref, field_ref, weight_ref, coupling_ref, roster_ref, sems):
    blocks = out_ref.shape[0]
    chunk = blocks // 3
    field_copy = pltpu.make_async_copy(field_hbm, field_ref, sems.at[3])
    field_copy.start()
    copies = []
    for n in range(3):
        part = pl.ds(n * chunk, chunk)
        copy = pltpu.make_async_copy(weight_hbm.at[part], weight_ref.at[part], sems.at[n])
        copy.start()
        copies.append(copy)
    later = [
        pltpu.make_async_copy(coupling_hbm.at[0], coupling_ref, sems.at[4]),
        pltpu.make_async_copy(roster_hbm, roster_ref, sems.at[5]),
    ]
    for copy in later:
        copy.start()
    field_copy.wait()
    for k in range(blocks):
        if k % chunk == 0:
            copies[k // chunk].wait()
        compress_block(0, k, field_ref, weight_ref, out_ref)
    for copy in later:
        copy.wait()


def compress_again(field_ref, weight_ref, coupling_hbm, out_ref, coupling_ref, sem):
    copy = pltpu.make_async_copy(coupling_hbm.at[1], coupling_ref, sem)
    copy.start()
    for k in range(out_ref.shape[0]):
        compress_block(1, k, field_ref, weight_ref, out_ref)
    copy.wait()


def stacked_rows(own, other):
    low = lane_low(own.shape)
    real = jnp.where(low, own, pltpu.roll(other, 64, axis=1))
    imag = jnp.where(low, pltpu.roll(own, 64, axis=1), other)
    return jnp.concatenate([real, imag], axis=0)


def level_block(k, row, own_ref, other_ref, weight_ref):
    rows = stacked_rows(own_ref[k], other_ref[row[0, k]])
    return joined(product(rows, weight_ref[k].reshape(128, 128), NT))


def level_kernel(level, at, roster_ref, own_ref, other_ref, weight_ref, *rest):
    out_ref = rest[-1]
    row = roster_ref[level]
    for k in range(out_ref.shape[0]):
        out_ref[k] = level_block(k, row, own_ref, other_ref, weight_ref.at[at])


def last_rows(half, level, at, roster_ref, own_ref, other_ref, weight_ref, expand_ref, near_refs, state_ref, out_ref, done):
    row = roster_ref[level]
    blocks = own_ref.shape[0]
    each = near_refs[0].shape[0]
    rhs = near_refs[0].shape[1] // 2
    here = pl.ds(half * HALF, HALF)
    there = pl.ds(rhs + half * HALF, HALF)
    for k in range(blocks):
        state_ref[k] = level_block(k, row, own_ref, other_ref, weight_ref.at[at])
    for k in range(blocks):
        coeffs = state_ref[k]
        signed = jnp.where(lane_low(coeffs.shape), coeffs, -coeffs)
        turned = pltpu.roll(coeffs, 64, axis=1)
        far = product(jnp.concatenate([signed, turned], axis=0), expand_ref[k].reshape(128, 128), NN)
        near_ref = near_refs[k // each]
        lanes = pl.ds(128 * k, 128)
        out_ref[0, :, lanes] = far[:HALF] + near_ref[k % each, here]
        out_ref[1, :, lanes] = far[HALF:] + near_ref[k % each, there]
        done(k)


def last_first(level, at, roster_ref, own_ref, other_ref, weight_ref, expand_ref, *rest):
    near_refs, (out_ref, state_ref) = rest[:-2], rest[-2:]
    last_rows(0, level, at, roster_ref, own_ref, other_ref, weight_ref, expand_ref, near_refs, state_ref, out_ref, lambda k: None)


def last_second(level, at, roster_ref, own_ref, other_ref, weight_ref, expand_ref, ready_ref, *rest):
    near_refs, (out_hbm, state_ref, out_ref, sems) = rest[:-4], rest[-4:]
    copies = [pltpu.make_async_copy(ready_ref, out_hbm.at[:, pl.ds(0, HALF)], sems.at[3])]
    copies[0].start()

    def done(k):
        if k % 4 == 3:
            part = pl.ds(128 * (k - 3), 512)
            copy = pltpu.make_async_copy(
                out_ref.at[:, :, part], out_hbm.at[:, pl.ds(HALF, HALF), part], sems.at[k // 4]
            )
            copy.start()
            copies.append(copy)

    last_rows(1, level, at, roster_ref, own_ref, other_ref, weight_ref, expand_ref, near_refs, state_ref, out_ref, done)
    for copy in copies:
        copy.wait()


def near_kernel(first, owner_ref, place_ref, valid_ref, pick_ref, own_ref, core_ref, far_ref, both_ref, weight_ref, *rest):
    out_ref = rest[-1]
    me = lax.axis_index("sub")
    for n in range(out_ref.shape[0]):
        k = first + n
        total = None
        for t in range(weight_ref.shape[1]):
            owner = owner_ref[t, k]
            leaf = pick_ref[owner, place_ref[t, k]]
            lanes = pl.ds(pl.multiple_of(leaf * 128, 128), 128)
            which = owner ^ me
            parts = []
            for d in range(2):
                low = jnp.where(which == 1, core_ref[d, :, lanes], own_ref[d, :, lanes])
                high = jnp.where(which == 3, both_ref[d, :, lanes], far_ref[d, :, lanes])
                parts.append(jnp.where(which >= 2, high, low))
            rows = jnp.concatenate(parts, axis=0) * valid_ref[t, k].astype(F32)
            result = product(rows, weight_ref[k, t].reshape(256, 128), NT)
            half = result.shape[0] // 2
            term = jnp.concatenate(
                [result[:half, :128] - result[half:, 128:], result[half:, :128] + result[:half, 128:]], axis=0
            )
            total = term if total is None else total + term
        out_ref[n] = total


def fetch_kernel(parts, *refs):
    count = len(parts)
    sources, outs, sem = refs[:count], refs[count + 1 : -1], refs[-1]
    copies = []
    for n, (part, source, out) in enumerate(zip(parts, sources, outs)):
        source = source if part is None else source.at[pl.ds(*part)]
        copies.append(pltpu.make_async_copy(source, out, sem.at[n]))
    for copy in copies:
        copy.start()
    for copy in copies:
        copy.wait()


def spec(space):
    return pl.BlockSpec(memory_space=space)


def call(kernel, out, spaces, out_spaces=VMEM, scratch=(), flops=2_000_000):
    single = not isinstance(out_spaces, (list, tuple))
    return pl.pallas_call(
        kernel,
        out_shape=out,
        in_specs=[spec(space) for space in spaces],
        out_specs=spec(out_spaces) if single else [spec(space) for space in out_spaces],
        scratch_shapes=list(scratch),
        compiler_params=pltpu.CompilerParams(vmem_limit_bytes=8 << 20),
        cost_estimate=pl.CostEstimate(flops=flops, bytes_accessed=1 << 20, transcendentals=0),
    )


def in_hbm(*arrays):
    return [pltpu.with_memory_space_constraint(array, HBM) for array in arrays]


def fetch(arrays, parts, after):
    shapes = [a.shape if p is None else (p[1],) + a.shape[1:] for a, p in zip(arrays, parts)]
    return call(
        functools.partial(fetch_kernel, parts),
        [VMEM(shape, a.dtype) for shape, a in zip(shapes, arrays)],
        [HBM] * len(arrays) + [ANY],
        [VMEM] * len(arrays),
        [DMA((len(arrays),))],
    )(*in_hbm(*arrays), after)


def flipped(value, axis, mask):
    pairs = [(source, source ^ mask) for source in range(lax.axis_size(axis))]
    return lax.ppermute(value, axis, pairs)


def tied(value, after):
    return lax.optimization_barrier((value, after))[0]


def on_device(
    field_in,
    compress,
    coupling,
    roster,
    expand,
    nearfield_dense_blocks,
    slot_owner_index,
    slot_source_position,
    slot_valid_mask,
    near_pick,
):
    blocks = compress.shape[0]
    rhs = field_in.shape[1]
    leaf_count = lax.axis_size("leaf")
    top = leaf_count // 2
    plan = [
        ("leaf", top),
        ("leaf", top // 2),
        ("leaf", top // 4),
        ("sub", 1),
        ("sub", 2),
        ("leaf", top // 4),
        ("leaf", top // 2),
        ("leaf", top),
    ]
    pick = near_pick[0]
    indices = (slot_owner_index.T, slot_source_position.T, slot_valid_mask.T, pick)
    state = VMEM((blocks, HALF, 128), F32)
    field_shape, base_shape = VMEM(field_in.shape, F32), VMEM(compress.shape, F32)

    coeffs = [None, None]
    weights = {}
    coeffs[0], field, base, weights[0], names = call(
        compress_kernel,
        [state, field_shape, base_shape, VMEM(coupling.shape[1:], F32), VMEM(roster.shape, jnp.int32)],
        [HBM] * 4,
        [VMEM] * 5,
        scratch=[DMA((6,))],
    )(*in_hbm(field_in, compress, coupling, roster))
    coeffs[1], weights[1] = call(
        compress_again, [state, VMEM(coupling.shape[1:], F32)], [VMEM, VMEM, HBM], [VMEM] * 2, scratch=[DMA]
    )(field, base, *in_hbm(coupling))
    weights = {level: (weights[level][None], 0) for level in weights}
    pieces = []
    for position, (axis, mask) in enumerate(plan):
        other = [flipped(c, axis, mask) for c in coeffs]
        extra = []
        if position == 0:
            far = flipped(tied(field_in, coeffs[1]), "sub", 2)
        if position in (1, 2):
            begin = 3 * position - 1
            (some,) = fetch([coupling], [(begin, 3)], coeffs[1])
            weights.update({begin + n: (some, n) for n in range(3)})
            extra.append(some)
        if position == 4:
            core = flipped(tied(field_in, coeffs[1]), "sub", 1)
            both = flipped(tied(far, coeffs[1]), "sub", 1)
            dense, last = fetch([nearfield_dense_blocks, expand], [None, None], coeffs[1])
            extra.append(last)
        for _ in range(NEAR_AT.get(position, 0)):
            piece = call(
                functools.partial(near_kernel, NEAR_EACH * len(pieces)),
                VMEM((NEAR_EACH, 2 * rhs, 128), F32),
                [SMEM] * 4 + [VMEM] * 5 + [ANY],
            )(*indices, field, core, far, both, dense, coeffs[1])
            pieces.append(piece)
            extra.append(piece)
        if position < len(plan) - 1:
            fresh = []
            for half in range(2):
                after = extra + fresh
                fresh.append(
                    call(
                        functools.partial(level_kernel, position, weights[position][1]),
                        state,
                        [VMEM] * 4 + [ANY] * len(after),
                    )(names, coeffs[half], other[half], weights[position][0], *after)
                )
            coeffs = fresh
        else:
            ready = call(
                functools.partial(last_first, position, weights[position][1]),
                VMEM((2, HALF, field_in.shape[2]), F32),
                [VMEM] * (5 + len(pieces)),
                scratch=[state],
            )(names, coeffs[0], other[0], weights[position][0], last, *pieces)
            total = call(
                functools.partial(last_second, position, weights[position][1]),
                jax.ShapeDtypeStruct(field_in.shape, F32),
                [VMEM] * (6 + len(pieces)),
                HBM,
                [state, VMEM((2, HALF, field_in.shape[2]), F32), DMA((4,))],
            )(names, coeffs[1], other[1], weights[position][0], last, ready, *pieces)
    return total


def solution(mesh):
    return jax.shard_map(
        on_device,
        mesh=mesh,
        in_specs=(
            P(None, None, ("leaf", "sub")),
            P(("leaf", "sub"), None, None, None),
            P(None, ("leaf", "sub"), None, None, None),
            P(None, ("leaf", "sub"), None),
            P(("leaf", "sub"), None, None, None),
            P(("leaf", "sub"), None, None, None, None),
            P(("leaf", "sub"), None),
            P(("leaf", "sub"), None),
            P(("leaf", "sub"), None),
            P(("leaf", "sub"), None, None),
        ),
        out_specs=P(None, None, ("leaf", "sub")),
        check_vma=False,
    )
```

```python
import functools

import jax
import jax.numpy as jnp
from jax import lax
from jax.experimental import pallas as pl
from jax.experimental.pallas import tpu as pltpu
from jax.sharding import PartitionSpec as P


VMEM = pltpu.VMEM
SMEM = pltpu.SMEM
ANY = pl.ANY
HBM = pltpu.HBM
DMA = pltpu.SemaphoreType.DMA
BF = jnp.bfloat16
F32 = jnp.float32
NT = (((1,), (1,)), ((), ()))
NN = (((1,), (0,)), ((), ()))
NEAR_EACH = 4
NEAR_AT = {5: 1, 6: 2}


def split(value):
    high = value.astype(BF)
    return high, (value - high.astype(F32)).astype(BF)


def product(rows, weights, dims):
    count = rows.shape[0]
    high, low = split(rows)
    stacked = jnp.concatenate(
        [
            jnp.concatenate([high, high], axis=1),
            jnp.concatenate([low, jnp.zeros_like(low)], axis=1),
        ],
        axis=0,
    )
    wide = jnp.concatenate(split(weights), axis=dims[0][1][0])
    result = lax.dot_general(stacked, wide, dims, preferred_element_type=F32)
    return result[:count] + result[count:]


def lane_low(shape):
    return lax.broadcasted_iota(jnp.int32, shape, 1) < 64


def joined(result):
    rhs = result.shape[0] // 2
    turned = pltpu.roll(result[rhs:], 64, axis=1)
    return result[:rhs] + jnp.where(lane_low(turned.shape), -turned, turned)


def compress_kernel(field_hbm, weight_hbm, out_ref, field_ref, weight_ref, sems):
    blocks = out_ref.shape[0]
    chunk = blocks // 3
    field_copy = pltpu.make_async_copy(field_hbm, field_ref, sems.at[3])
    field_copy.start()
    copies = []
    for n in range(3):
        part = pl.ds(n * chunk, chunk)
        copy = pltpu.make_async_copy(weight_hbm.at[part], weight_ref.at[part], sems.at[n])
        copy.start()
        copies.append(copy)
    field_copy.wait()
    for k in range(blocks):
        if k % chunk == 0:
            copies[k // chunk].wait()
        lanes = pl.ds(128 * k, 128)
        rows = jnp.concatenate([field_ref[0, :, lanes], field_ref[1, :, lanes]], axis=0)
        out_ref[k] = joined(product(rows, weight_ref[k].reshape(128, 128), NT))


def stacked_rows(own, other):
    low = lane_low(own.shape)
    real = jnp.where(low, own, pltpu.roll(other, 64, axis=1))
    imag = jnp.where(low, pltpu.roll(own, 64, axis=1), other)
    return jnp.concatenate([real, imag], axis=0)


def level_block(k, row, own_ref, other_ref, weight_ref):
    rows = stacked_rows(own_ref[k], other_ref[row[0, k]])
    return joined(product(rows, weight_ref[k].reshape(128, 128), NT))


def level_kernel(level, at, roster_ref, own_ref, other_ref, weight_ref, *rest):
    out_ref = rest[-1]
    row = roster_ref[level]
    for k in range(out_ref.shape[0]):
        out_ref[k] = level_block(k, row, own_ref, other_ref, weight_ref.at[at])


def last_kernel(
    level, roster_ref, away_roster_ref, own_ref, cross_ref, corner_ref, away_ref, weight_ref, expand_ref, *rest
):
    near_refs, (out_hbm, there_ref, state_ref, out_ref, sems) = rest[:-5], rest[-5:]
    blocks = own_ref.shape[0]
    each = near_refs[0].shape[0]
    row = away_roster_ref[level - 1]
    for k in range(blocks):
        there_ref[k] = level_block(k, row, cross_ref, corner_ref, away_ref.at[0])
    row = roster_ref[level]
    for k in range(blocks):
        state_ref[k] = level_block(k, row, own_ref, there_ref, weight_ref.at[0])
    copies = []
    for k in range(blocks):
        coeffs = state_ref[k]
        signed = jnp.where(lane_low(coeffs.shape), coeffs, -coeffs)
        turned = pltpu.roll(coeffs, 64, axis=1)
        far = product(jnp.concatenate([signed, turned], axis=0), expand_ref[k].reshape(128, 128), NN)
        total = far + near_refs[k // each][k % each]
        half = total.shape[0] // 2
        lanes = pl.ds(128 * k, 128)
        out_ref[0, :, lanes] = total[:half]
        out_ref[1, :, lanes] = total[half:]
        if k % 4 == 3:
            part = pl.ds(128 * (k - 3), 512)
            copy = pltpu.make_async_copy(out_ref.at[:, :, part], out_hbm.at[:, :, part], sems.at[k // 4])
            copy.start()
            copies.append(copy)
    for copy in copies:
        copy.wait()


def near_kernel(first, owner_ref, place_ref, valid_ref, pick_ref, own_ref, core_ref, far_ref, both_ref, weight_ref, *rest):
    out_ref = rest[-1]
    me = lax.axis_index("sub")
    for n in range(out_ref.shape[0]):
        k = first + n
        total = None
        for t in range(weight_ref.shape[1]):
            owner = owner_ref[t, k]
            leaf = pick_ref[owner, place_ref[t, k]]
            lanes = pl.ds(pl.multiple_of(leaf * 128, 128), 128)
            which = owner ^ me
            parts = []
            for d in range(2):
                low = jnp.where(which == 1, core_ref[d, :, lanes], own_ref[d, :, lanes])
                high = jnp.where(which == 3, both_ref[d, :, lanes], far_ref[d, :, lanes])
                parts.append(jnp.where(which >= 2, high, low))
            rows = jnp.concatenate(parts, axis=0) * valid_ref[t, k].astype(F32)
            result = product(rows, weight_ref[k, t].reshape(256, 128), NT)
            half = result.shape[0] // 2
            term = jnp.concatenate(
                [result[:half, :128] - result[half:, 128:], result[half:, :128] + result[:half, 128:]], axis=0
            )
            total = term if total is None else total + term
        out_ref[n] = total


def fetch_kernel(parts, *refs):
    count = len(parts)
    sources, outs, sem = refs[:count], refs[count + 1 : -1], refs[-1]
    copies = []
    for n, (part, source, out) in enumerate(zip(parts, sources, outs)):
        source = source if part is None else source.at[pl.ds(*part)]
        copies.append(pltpu.make_async_copy(source, out, sem.at[n]))
    for copy in copies:
        copy.start()
    for copy in copies:
        copy.wait()


def spec(space):
    return pl.BlockSpec(memory_space=space)


def call(kernel, out, spaces, out_spaces=VMEM, scratch=(), flops=2_000_000):
    single = not isinstance(out_spaces, (list, tuple))
    return pl.pallas_call(
        kernel,
        out_shape=out,
        in_specs=[spec(space) for space in spaces],
        out_specs=spec(out_spaces) if single else [spec(space) for space in out_spaces],
        scratch_shapes=list(scratch),
        compiler_params=pltpu.CompilerParams(vmem_limit_bytes=8 << 20),
        cost_estimate=pl.CostEstimate(flops=flops, bytes_accessed=1 << 20, transcendentals=0),
    )


def in_hbm(*arrays):
    return [pltpu.with_memory_space_constraint(array, HBM) for array in arrays]


def fetch(arrays, parts, after):
    shapes = [a.shape if p is None else (p[1],) + a.shape[1:] for a, p in zip(arrays, parts)]
    return call(
        functools.partial(fetch_kernel, parts),
        [VMEM(shape, a.dtype) for shape, a in zip(shapes, arrays)],
        [HBM] * len(arrays) + [ANY],
        [VMEM] * len(arrays),
        [DMA((len(arrays),))],
    )(*in_hbm(*arrays), after)


def flipped(value, axis, mask):
    pairs = [(source, source ^ mask) for source in range(lax.axis_size(axis))]
    return lax.ppermute(value, axis, pairs)


def tied(value, after):
    return lax.optimization_barrier((value, after))[0]


def on_device(
    field_in,
    compress,
    coupling,
    roster,
    expand,
    nearfield_dense_blocks,
    slot_owner_index,
    slot_source_position,
    slot_valid_mask,
    near_pick,
):
    blocks = compress.shape[0]
    rhs = field_in.shape[1]
    leaf_count = lax.axis_size("leaf")
    top = leaf_count // 2
    plan = [
        ("leaf", top),
        ("leaf", top // 2),
        ("leaf", top // 4),
        ("sub", 1),
        ("sub", 2),
        ("leaf", top // 4),
        ("leaf", top // 2),
        ("leaf", top),
    ]
    pick = near_pick[0]
    indices = (slot_owner_index.T, slot_source_position.T, slot_valid_mask.T, pick)
    state = VMEM((blocks, rhs, 128), F32)

    coeffs = call(
        compress_kernel, state, [HBM, HBM], scratch=[VMEM(field_in.shape, F32), VMEM(compress.shape, F32), DMA((4,))]
    )(*in_hbm(field_in, compress))
    pieces = []

    def near_piece(field, core, far, both, dense, after):
        number = len(pieces)
        pieces.append(
            call(
                functools.partial(near_kernel, NEAR_EACH * number),
                VMEM((NEAR_EACH, 2 * rhs, 128), F32),
                [SMEM] * 4 + [VMEM] * 5 + [ANY],
            )(*indices, field, core, far, both, dense, after)
        )
        return pieces[-1]

    def level_of(position, own, other, extra):
        weight, at = weights[position]
        return call(
            functools.partial(level_kernel, position, at), state, [VMEM] * 4 + [ANY] * len(extra)
        )(names, own, other, weight, *extra)

    for position, (axis, mask) in enumerate(plan[:-2]):
        other = flipped(coeffs, axis, mask)
        extra = []
        if position == 0:
            far = flipped(tied(field_in, coeffs), "sub", 2)
            early, names = fetch([coupling, roster], [(0, 4), None], coeffs)
            weights = {level: (early, level) for level in range(4)}
        if position == 1:
            dense, last, field = fetch([nearfield_dense_blocks, expand, field_in], [None, None, None], coeffs)
            extra.append(field)
        if position == 2:
            middle, sixth, seventh = fetch([coupling] * 3, [(4, 2), (6, 1), (7, 1)], coeffs)
            weights |= {4: (middle, 0), 5: (middle, 1), 6: (sixth, 0), 7: (seventh, 0)}
            extra.append(seventh)
            away = flipped(tied(sixth, coeffs), "leaf", top)
        if position == 4:
            away_names = flipped(tied(names, coeffs), "leaf", top)
            core = flipped(tied(field_in, coeffs), "sub", 1)
            both = flipped(tied(far, coeffs), "sub", 1)
        for _ in range(NEAR_AT.get(position, 0)):
            extra.append(near_piece(field, core, far, both, dense, coeffs))
        coeffs = level_of(position, coeffs, other, extra)
    side = flipped(coeffs, "leaf", top // 2)
    corner = flipped(coeffs, "leaf", top // 2 + top)
    cross = flipped(coeffs, "leaf", top)
    for _ in range(NEAR_AT[6]):
        near_piece(field, core, far, both, dense, coeffs)
    own = level_of(6, coeffs, side, [pieces[-1]])
    return call(
        functools.partial(last_kernel, 7),
        jax.ShapeDtypeStruct(field_in.shape, F32),
        [VMEM] * (8 + len(pieces)),
        HBM,
        [state, state, VMEM(field_in.shape, F32), DMA((3,))],
    )(names, away_names, own, cross, corner, away, weights[7][0], last, *pieces)


def solution(mesh):
    return jax.shard_map(
        on_device,
        mesh=mesh,
        in_specs=(
            P(None, None, ("leaf", "sub")),
            P(("leaf", "sub"), None, None, None),
            P(None, ("leaf", "sub"), None, None, None),
            P(None, ("leaf", "sub"), None),
            P(("leaf", "sub"), None, None, None),
            P(("leaf", "sub"), None, None, None, None),
            P(("leaf", "sub"), None),
            P(("leaf", "sub"), None),
            P(("leaf", "sub"), None),
            P(("leaf", "sub"), None, None),
        ),
        out_specs=P(None, None, ("leaf", "sub")),
        check_vma=False,
    )
```

```python
import functools

import jax
import jax.numpy as jnp
from jax import lax
from jax.experimental import pallas as pl
from jax.experimental.pallas import tpu as pltpu
from jax.sharding import PartitionSpec as P


VMEM = pltpu.VMEM
SMEM = pltpu.SMEM
ANY = pl.ANY
HBM = pltpu.HBM
DMA = pltpu.SemaphoreType.DMA
BF = jnp.bfloat16
F32 = jnp.float32
NT = (((1,), (1,)), ((), ()))
NN = (((1,), (0,)), ((), ()))
NEAR_PARTS = ((0, 4), (4, 8))


def split(value):
    high = value.astype(BF)
    return high, (value - high.astype(F32)).astype(BF)


def widened(rows):
    high, low = split(rows)
    return jnp.concatenate(
        [
            jnp.concatenate([high, high], axis=1),
            jnp.concatenate([low, jnp.zeros_like(low)], axis=1),
        ],
        axis=0,
    )


def folded(result):
    count = result.shape[0] // 2
    return result[:count] + result[count:]


def product(rows, weights):
    wide = jnp.concatenate(split(weights), axis=1)
    return folded(lax.dot_general(widened(rows), wide, NT, preferred_element_type=F32))


def times(rows, wide):
    return folded(lax.dot_general(widened(rows), wide, NN, preferred_element_type=F32))


def lane_low(shape):
    return lax.broadcasted_iota(jnp.int32, shape, 1) < 64


def joined(result):
    rhs = result.shape[0] // 2
    turned = pltpu.roll(result[rhs:], 64, axis=1)
    return result[:rhs] + jnp.where(lane_low(turned.shape), -turned, turned)


def arranged(block):
    halves = []
    flat = block.T
    for half in range(2):
        upper = flat[64 * half : 64 * half + 64]
        turned = pltpu.roll(upper, 64, axis=1)
        lower = jnp.where(lane_low(turned.shape), -turned, turned)
        halves.append(jnp.concatenate(split(jnp.concatenate([upper, lower], axis=0)), axis=0))
    return halves


def started(pairs, sems):
    copies = [pltpu.make_async_copy(source, out, sems.at[n]) for n, (source, out) in enumerate(pairs)]
    for copy in copies:
        copy.start()
    return copies


def finish(copies):
    for copy in copies:
        copy.wait()


def compress_kernel(field_hbm, weight_hbm, coupling_hbm, roster_hbm, out_ref, coupling_ref, roster_ref, field_ref, weight_ref, sems):
    blocks = out_ref.shape[0]
    parts = [pl.ds(2 * n, 2) for n in range(blocks // 2)]
    copies = started(
        [(field_hbm, field_ref)]
        + [(weight_hbm.at[part], weight_ref.at[part]) for part in parts]
        + [(coupling_hbm.at[0], coupling_ref), (roster_hbm, roster_ref)],
        sems,
    )
    copies[0].wait()
    for k in range(blocks):
        if k % 2 == 0:
            copies[1 + k // 2].wait()
        lanes = pl.ds(128 * k, 128)
        rows = jnp.concatenate([field_ref[0, :, lanes], field_ref[1, :, lanes]], axis=0)
        out_ref[k] = joined(product(rows, weight_ref[k].reshape(128, 128)))
    finish(copies[-2:])


def ahead_kernel(parts, own_ref, weight_ref, *refs):
    count = len(parts)
    sources, own_out, other_out = refs[:count], refs[count], refs[count + 1]
    outs, sems = refs[count + 2 : -1], refs[-1]
    copies = started(
        [(source if part is None else source.at[part], out) for part, source, out in zip(parts, sources, outs)],
        sems,
    )
    for k in range(own_ref.shape[0]):
        own_wide, other_wide = arranged(weight_ref[k].reshape(128, 128))
        other_out[k] = other_wide
        own_out[k] = times(own_ref[k], own_wide)
    finish(copies)


def pack_kernel(level, weight_hbm, roster_ref, after_ref, out_ref, sem):
    count = out_ref.shape[0] - 1
    copy = pltpu.make_async_copy(weight_hbm.at[level], out_ref.at[pl.ds(0, count)], sem)
    copy.start()
    row = jnp.broadcast_to(roster_ref[level].astype(F32), (8, roster_ref.shape[2]))
    out_ref[count, 0, 0:8, 0 : roster_ref.shape[2]] = row
    copy.wait()


def prepare_kernel(weight_ref, after_ref, own_out, other_out):
    for k in range(own_out.shape[0]):
        own_out[k], other_out[k] = arranged(weight_ref[k].reshape(128, 128))


def spread_kernel(weight_ref, after_ref, out_ref):
    for k in range(out_ref.shape[0]):
        out_ref[k] = jnp.concatenate(split(weight_ref[k].reshape(128, 128)), axis=0)


def own_kernel(own_ref, wide_ref, out_ref):
    for k in range(out_ref.shape[0]):
        out_ref[k] = times(own_ref[k], wide_ref[k])


def level_kernel(level, roster_ref, other_ref, wide_ref, ready_ref, *rest):
    out_ref = rest[-1]
    row = roster_ref[level]
    places = [row[0, k] for k in range(out_ref.shape[0])]
    for k, place in enumerate(places):
        out_ref[k] = ready_ref[k] + times(other_ref[place], wide_ref[k])


def corner_kernel(packed_ref, other_ref, wide_ref, out_ref):
    blocks = out_ref.shape[0]
    row = packed_ref[blocks, 0, 0:8, 0:blocks]
    places = [row[0, k].astype(jnp.int32) for k in range(blocks)]
    for k, place in enumerate(places):
        out_ref[k] = times(other_ref[place], wide_ref[k])


def last_kernel(
    level, roster_ref, cross_ref, away_ref, corner_ref, wide_ref, ready_ref, expand_ref, *rest
):
    near_refs, (out_hbm, there_ref, out_ref, sems) = rest[:-4], rest[-4:]
    blocks = cross_ref.shape[0]
    row = roster_ref[level]
    places = [row[0, k] for k in range(blocks)]
    for k in range(blocks):
        there_ref[k] = corner_ref[k] + times(cross_ref[k], away_ref[k])
    copies = []
    for k, place in enumerate(places):
        coeffs = ready_ref[k] + times(there_ref[place], wide_ref[k])
        signed = jnp.where(lane_low(coeffs.shape), coeffs, -coeffs)
        turned = pltpu.roll(coeffs, 64, axis=1)
        far = times(jnp.concatenate([signed, turned], axis=0), expand_ref[k])
        which = [n for n, (begin, count) in enumerate(NEAR_PARTS) if begin <= k < begin + count][0]
        total = far + near_refs[which][k - NEAR_PARTS[which][0]]
        half = total.shape[0] // 2
        lanes = pl.ds(128 * k, 128)
        out_ref[0, :, lanes] = total[:half]
        out_ref[1, :, lanes] = total[half:]
        if k % 4 == 3:
            part = pl.ds(128 * (k - 3), 512)
            copy = pltpu.make_async_copy(out_ref.at[:, :, part], out_hbm.at[:, :, part], sems.at[k // 4])
            copy.start()
            copies.append(copy)
    finish(copies)


def near_kernel(first, owner_ref, place_ref, valid_ref, pick_ref, own_ref, core_ref, far_ref, both_ref, weight_ref, *rest):
    out_ref = rest[-1]
    me = lax.axis_index("sub")
    for n in range(out_ref.shape[0]):
        k = first + n
        total = None
        for t in range(weight_ref.shape[1]):
            owner = owner_ref[t, k]
            leaf = pick_ref[owner, place_ref[t, k]]
            lanes = pl.ds(pl.multiple_of(leaf * 128, 128), 128)
            which = owner ^ me
            parts = []
            for d in range(2):
                low = jnp.where(which == 1, core_ref[d, :, lanes], own_ref[d, :, lanes])
                high = jnp.where(which == 3, both_ref[d, :, lanes], far_ref[d, :, lanes])
                parts.append(jnp.where(which >= 2, high, low))
            rows = jnp.concatenate(parts, axis=0) * valid_ref[t, k].astype(F32)
            result = product(rows, weight_ref[k, t].reshape(256, 128))
            half = result.shape[0] // 2
            term = jnp.concatenate(
                [result[:half, :128] - result[half:, 128:], result[half:, :128] + result[:half, 128:]], axis=0
            )
            total = term if total is None else total + term
        out_ref[n] = total


def spec(space):
    return pl.BlockSpec(memory_space=space)


def call(kernel, out, spaces, out_spaces=VMEM, scratch=(), flops=2_000_000):
    single = not isinstance(out_spaces, (list, tuple))
    return pl.pallas_call(
        kernel,
        out_shape=out,
        in_specs=[spec(space) for space in spaces],
        out_specs=spec(out_spaces) if single else [spec(space) for space in out_spaces],
        scratch_shapes=list(scratch),
        compiler_params=pltpu.CompilerParams(vmem_limit_bytes=8 << 20),
        cost_estimate=pl.CostEstimate(flops=flops, bytes_accessed=1 << 20, transcendentals=0),
    )


def in_hbm(*arrays):
    return [pltpu.with_memory_space_constraint(array, HBM) for array in arrays]


def flipped(value, axis, mask):
    pairs = [(source, source ^ mask) for source in range(lax.axis_size(axis))]
    return lax.ppermute(value, axis, pairs)


def tied(value, after):
    return lax.optimization_barrier((value, after))[0]


def on_device(
    field_in,
    compress,
    coupling,
    roster,
    expand,
    nearfield_dense_blocks,
    slot_owner_index,
    slot_source_position,
    slot_valid_mask,
    near_pick,
):
    blocks = compress.shape[0]
    rhs = field_in.shape[1]
    leaf_count = lax.axis_size("leaf")
    top = leaf_count // 2
    plan = [
        ("leaf", top),
        ("leaf", top // 2),
        ("leaf", top // 4),
        ("sub", 1),
        ("sub", 2),
        ("leaf", top // 4),
        ("leaf", top // 2),
        ("leaf", top),
    ]
    pick = near_pick[0]
    indices = (slot_owner_index.T, slot_source_position.T, slot_valid_mask.T, pick)
    state = VMEM((blocks, rhs, 128), F32)
    wide = VMEM((blocks, 256, 128), BF)
    level_weights = VMEM(coupling.shape[1:], F32)
    coupling_hbm, near_hbm, expand_hbm, field_hbm = in_hbm(coupling, nearfield_dense_blocks, expand, field_in)

    coeffs, first, names = call(
        compress_kernel,
        [state, level_weights, VMEM(roster.shape, jnp.int32)],
        [HBM] * 4,
        [VMEM] * 3,
        scratch=[VMEM(field_in.shape, F32), VMEM(compress.shape, F32), DMA((3 + blocks // 2,))],
    )(*in_hbm(field_in, compress, coupling, roster))
    weights = {0: first}

    def ahead(position, coeffs, levels=(), whole=()):
        parts = list(levels) + [None] * len(whole)
        sources = [coupling_hbm] * len(levels) + list(whole)
        shapes = [level_weights] * len(levels) + [VMEM(array.shape, array.dtype) for array in whole]
        ready, other, *got = call(
            functools.partial(ahead_kernel, parts),
            [state, wide] + shapes,
            [VMEM] * 2 + [HBM] * len(sources),
            [VMEM] * (2 + len(shapes)),
            [DMA((len(parts),))],
        )(coeffs, weights[position], *sources)
        weights.update(dict(zip(levels, got)))
        return ready, other, got[len(levels) :]

    def prepared(weight, after):
        return call(prepare_kernel, [wide, wide], [VMEM, ANY], [VMEM] * 2)(weight, after)

    def near_piece(number, after):
        begin, count = NEAR_PARTS[number]
        return call(
            functools.partial(near_kernel, begin), VMEM((count, 2 * rhs, 128), F32), [SMEM] * 4 + [VMEM] * 5 + [ANY]
        )(*indices, field, core, far, both, dense, after)

    def own_part(own, wide_own):
        return call(own_kernel, state, [VMEM] * 2)(own, wide_own)

    def level_of(position, other, wide_other, ready, extra):
        return call(
            functools.partial(level_kernel, position), state, [VMEM] * 4 + [ANY] * len(extra)
        )(names, other, wide_other, ready, *extra)

    extra_levels = {0: (1,), 1: (2,), 2: (3, 7), 3: (4,), 4: (5,), 5: ()}
    extra_whole = {1: (near_hbm, field_hbm), 4: (expand_hbm,)}
    for position, (axis, mask) in enumerate(plan[:-2]):
        other = flipped(coeffs, axis, mask)
        extra = []
        ready, wide_other, got = ahead(position, coeffs, extra_levels[position], extra_whole.get(position, ()))
        if position == 0:
            far = flipped(tied(field_in, coeffs), "sub", 2)
        if position == 1:
            dense, field = got
            packed = call(
                functools.partial(pack_kernel, 6),
                VMEM((blocks + 1,) + coupling.shape[2:], F32),
                [HBM, VMEM, ANY],
                scratch=[DMA],
            )(coupling_hbm, names, coeffs)
            extra.append(packed)
        if position == 2:
            away = flipped(tied(packed, coeffs), "leaf", top)
        if position == 4:
            core = flipped(tied(field_in, coeffs), "sub", 1)
            both = flipped(tied(far, coeffs), "sub", 1)
            sixth = prepared(packed, coeffs)
            seventh = prepared(weights[7], coeffs)
            extra += [sixth[0], seventh[0]]
        if position == 5:
            last = call(spread_kernel, wide, [VMEM, ANY])(expand_ready, coeffs)
            pieces = [near_piece(0, coeffs)]
            extra += [last, pieces[0]]
        if position == 4:
            expand_ready = got[0]
        coeffs = level_of(position, other, wide_other, ready, extra)
    side = flipped(coeffs, "leaf", top // 2)
    corner = flipped(coeffs, "leaf", top // 2 + top)
    cross = flipped(coeffs, "leaf", top)
    pieces.append(near_piece(1, coeffs))
    ready = own_part(coeffs, sixth[0])
    here = level_of(6, side, sixth[1], ready, [pieces[1]])
    ready = own_part(here, seventh[0])
    away_wide = prepared(away, ready)
    beside = call(corner_kernel, state, [VMEM] * 3)(away, corner, away_wide[1])
    return call(
        functools.partial(last_kernel, 7),
        jax.ShapeDtypeStruct(field_in.shape, F32),
        [VMEM] * (7 + len(pieces)),
        HBM,
        [state, VMEM(field_in.shape, F32), DMA((3,))],
    )(names, cross, away_wide[0], beside, seventh[1], ready, last, *pieces)


def solution(mesh):
    return jax.shard_map(
        on_device,
        mesh=mesh,
        in_specs=(
            P(None, None, ("leaf", "sub")),
            P(("leaf", "sub"), None, None, None),
            P(None, ("leaf", "sub"), None, None, None),
            P(None, ("leaf", "sub"), None),
            P(("leaf", "sub"), None, None, None),
            P(("leaf", "sub"), None, None, None, None),
            P(("leaf", "sub"), None),
            P(("leaf", "sub"), None),
            P(("leaf", "sub"), None),
            P(("leaf", "sub"), None, None),
        ),
        out_specs=P(None, None, ("leaf", "sub")),
        check_vma=False,
    )
```

```python
import functools

import jax
import jax.numpy as jnp
from jax import lax
from jax.experimental import pallas as pl
from jax.experimental.pallas import tpu as pltpu
from jax.sharding import PartitionSpec as P


VMEM = pltpu.VMEM
SMEM = pltpu.SMEM
ANY = pl.ANY
HBM = pltpu.HBM
DMA = pltpu.SemaphoreType.DMA
BF = jnp.bfloat16
F32 = jnp.float32
NT = (((1,), (1,)), ((), ()))
NN = (((1,), (0,)), ((), ()))
NEAR_PARTS = ((0, 4), (4, 8))


def split(value):
    high = value.astype(BF)
    return high, (value - high.astype(F32)).astype(BF)


def widened(rows):
    high, low = split(rows)
    return jnp.concatenate(
        [
            jnp.concatenate([high, high], axis=1),
            jnp.concatenate([low, jnp.zeros_like(low)], axis=1),
        ],
        axis=0,
    )


def folded(result):
    count = result.shape[0] // 2
    return result[:count] + result[count:]


def product(rows, weights):
    wide = jnp.concatenate(split(weights), axis=1)
    return folded(lax.dot_general(widened(rows), wide, NT, preferred_element_type=F32))


def times(rows, wide):
    return folded(lax.dot_general(widened(rows), wide, NN, preferred_element_type=F32))


def lane_low(shape):
    return lax.broadcasted_iota(jnp.int32, shape, 1) < 64


def joined(result):
    rhs = result.shape[0] // 2
    turned = pltpu.roll(result[rhs:], 64, axis=1)
    return result[:rhs] + jnp.where(lane_low(turned.shape), -turned, turned)


def arranged(block):
    halves = []
    flat = block.T
    for half in range(2):
        upper = flat[64 * half : 64 * half + 64]
        turned = pltpu.roll(upper, 64, axis=1)
        lower = jnp.where(lane_low(turned.shape), -turned, turned)
        halves.append(jnp.concatenate(split(jnp.concatenate([upper, lower], axis=0)), axis=0))
    return halves


def started(pairs, sems):
    copies = [pltpu.make_async_copy(source, out, sems.at[n]) for n, (source, out) in enumerate(pairs)]
    for copy in copies:
        copy.start()
    return copies


def finish(copies):
    for copy in copies:
        copy.wait()


def compress_kernel(field_hbm, weight_hbm, out_ref, field_ref, weight_ref, sems):
    blocks = out_ref.shape[0]
    parts = [pl.ds(2 * n, 2) for n in range(blocks // 2)]
    copies = started(
        [(field_hbm, field_ref)] + [(weight_hbm.at[part], weight_ref.at[part]) for part in parts], sems
    )
    copies[0].wait()
    for k in range(blocks):
        if k % 2 == 0:
            copies[1 + k // 2].wait()
        lanes = pl.ds(128 * k, 128)
        rows = jnp.concatenate([field_ref[0, :, lanes], field_ref[1, :, lanes]], axis=0)
        out_ref[k] = joined(product(rows, weight_ref[k].reshape(128, 128)))


def slots(row, count, back_ref):
    places = [row[0, k] for k in range(count)]
    lane = lax.broadcasted_iota(jnp.int32, back_ref.shape, 1)
    back = jnp.zeros(back_ref.shape, jnp.int32)
    for k, place in enumerate(places):
        back = jnp.where(lane == place, k, back)
    back_ref[...] = back
    return places


def first_kernel(packed_level, own_ref, coupling_hbm, roster_hbm, *refs):
    own_out, other_out, back_ref, roster_ref, packed_ref, *outs, weight_ref, sems = refs
    blocks = own_ref.shape[0]
    parts = [pl.ds(4 * n, 4) for n in range(blocks // 4)]
    count = packed_ref.shape[0] - 1
    copies = started(
        [(roster_hbm, roster_ref)]
        + [(coupling_hbm.at[0, part], weight_ref.at[part]) for part in parts]
        + [(coupling_hbm.at[packed_level], packed_ref.at[pl.ds(0, count)])]
        + [(coupling_hbm.at[1 + n], out) for n, out in enumerate(outs)],
        sems,
    )
    copies[0].wait()
    packed_ref[count, 0, 0:8, 0:blocks] = jnp.broadcast_to(roster_ref[packed_level].astype(F32), (8, blocks))
    places = slots(roster_ref[0], blocks, back_ref)
    for k, place in enumerate(places):
        if k % 4 == 0:
            copies[1 + k // 4].wait()
        own_wide, other_wide = arranged(weight_ref[k].reshape(128, 128))
        other_out[place] = other_wide
        own_out[place] = times(own_ref[k], own_wide)
    finish(copies[1 + len(parts) :])


def ahead_kernel(level, parts, own_ref, weight_ref, roster_ref, *refs):
    count = len(parts)
    sources, own_out, other_out, back_ref = refs[:count], refs[count], refs[count + 1], refs[count + 2]
    outs, sems = refs[count + 3 : -1], refs[-1]
    copies = started(
        [(source if part is None else source.at[part], out) for part, source, out in zip(parts, sources, outs)],
        sems,
    )
    for k, place in enumerate(slots(roster_ref[level], own_ref.shape[0], back_ref)):
        own_wide, other_wide = arranged(weight_ref[k].reshape(128, 128))
        other_out[place] = other_wide
        own_out[place] = times(own_ref[k], own_wide)
    finish(copies)


def prepare_kernel(weight_ref, after_ref, own_out, other_out):
    for k in range(own_out.shape[0]):
        own_out[k], other_out[k] = arranged(weight_ref[k].reshape(128, 128))


def sorted_kernel(level, weight_ref, roster_ref, after_ref, own_out, other_out, back_ref):
    for k, place in enumerate(slots(roster_ref[level], own_out.shape[0], back_ref)):
        own_out[k], other_out[place] = arranged(weight_ref[k].reshape(128, 128))


def spread_kernel(weight_ref, after_ref, out_ref):
    for k in range(out_ref.shape[0]):
        out_ref[k] = jnp.concatenate(split(weight_ref[k].reshape(128, 128)), axis=0)


def own_kernel(own_ref, wide_ref, out_ref):
    for k in range(out_ref.shape[0]):
        out_ref[k] = times(own_ref[k], wide_ref[k])


def own_sorted_kernel(level, own_ref, wide_ref, roster_ref, out_ref):
    row = roster_ref[level]
    for k in range(out_ref.shape[0]):
        out_ref[row[0, k]] = times(own_ref[k], wide_ref[k])


def level_kernel(back_ref, other_ref, wide_ref, ready_ref, *rest):
    out_ref = rest[-1]
    row = back_ref[0:1, :]
    blocks = [row[0, place] for place in range(out_ref.shape[0])]
    for place, k in enumerate(blocks):
        out_ref[k] = ready_ref[place] + times(other_ref[place], wide_ref[place])


def corner_kernel(packed_ref, other_ref, wide_ref, out_ref):
    blocks = out_ref.shape[0]
    row = packed_ref[blocks, 0, 0:8, 0:blocks]
    places = [row[0, k].astype(jnp.int32) for k in range(blocks)]
    for k, place in enumerate(places):
        out_ref[k] = times(other_ref[place], wide_ref[k])


def last_kernel(
    level, roster_ref, cross_ref, away_ref, corner_ref, wide_ref, ready_ref, expand_ref, *rest
):
    near_refs, (out_hbm, there_ref, out_ref, sems) = rest[:-4], rest[-4:]
    blocks = cross_ref.shape[0]
    row = roster_ref[level]
    places = [row[0, k] for k in range(blocks)]
    for k in range(blocks):
        there_ref[k] = corner_ref[k] + times(cross_ref[k], away_ref[k])
    copies = []
    for k, place in enumerate(places):
        coeffs = ready_ref[k] + times(there_ref[place], wide_ref[k])
        signed = jnp.where(lane_low(coeffs.shape), coeffs, -coeffs)
        turned = pltpu.roll(coeffs, 64, axis=1)
        far = times(jnp.concatenate([signed, turned], axis=0), expand_ref[k])
        which = [n for n, (begin, count) in enumerate(NEAR_PARTS) if begin <= k < begin + count][0]
        total = far + near_refs[which][k - NEAR_PARTS[which][0]]
        half = total.shape[0] // 2
        lanes = pl.ds(128 * k, 128)
        out_ref[0, :, lanes] = total[:half]
        out_ref[1, :, lanes] = total[half:]
        if k % 4 == 3:
            part = pl.ds(128 * (k - 3), 512)
            copy = pltpu.make_async_copy(out_ref.at[:, :, part], out_hbm.at[:, :, part], sems.at[k // 4])
            copy.start()
            copies.append(copy)
    finish(copies)


def near_kernel(first, owner_ref, place_ref, valid_ref, pick_ref, own_ref, core_ref, far_ref, both_ref, weight_ref, *rest):
    out_ref = rest[-1]
    me = lax.axis_index("sub")
    for n in range(out_ref.shape[0]):
        k = first + n
        total = None
        for t in range(weight_ref.shape[1]):
            owner = owner_ref[t, k]
            leaf = pick_ref[owner, place_ref[t, k]]
            lanes = pl.ds(pl.multiple_of(leaf * 128, 128), 128)
            which = owner ^ me
            parts = []
            for d in range(2):
                low = jnp.where(which == 1, core_ref[d, :, lanes], own_ref[d, :, lanes])
                high = jnp.where(which == 3, both_ref[d, :, lanes], far_ref[d, :, lanes])
                parts.append(jnp.where(which >= 2, high, low))
            rows = jnp.concatenate(parts, axis=0) * valid_ref[t, k].astype(F32)
            result = product(rows, weight_ref[k, t].reshape(256, 128))
            half = result.shape[0] // 2
            term = jnp.concatenate(
                [result[:half, :128] - result[half:, 128:], result[half:, :128] + result[:half, 128:]], axis=0
            )
            total = term if total is None else total + term
        out_ref[n] = total


def spec(space):
    return pl.BlockSpec(memory_space=space)


def call(kernel, out, spaces, out_spaces=VMEM, scratch=(), flops=2_000_000):
    single = not isinstance(out_spaces, (list, tuple))
    return pl.pallas_call(
        kernel,
        out_shape=out,
        in_specs=[spec(space) for space in spaces],
        out_specs=spec(out_spaces) if single else [spec(space) for space in out_spaces],
        scratch_shapes=list(scratch),
        compiler_params=pltpu.CompilerParams(vmem_limit_bytes=8 << 20),
        cost_estimate=pl.CostEstimate(flops=flops, bytes_accessed=1 << 20, transcendentals=0),
    )


def in_hbm(*arrays):
    return [pltpu.with_memory_space_constraint(array, HBM) for array in arrays]


def flipped(value, axis, mask):
    pairs = [(source, source ^ mask) for source in range(lax.axis_size(axis))]
    return lax.ppermute(value, axis, pairs)


def tied(value, after):
    return lax.optimization_barrier((value, after))[0]


def on_device(
    field_in,
    compress,
    coupling,
    roster,
    expand,
    nearfield_dense_blocks,
    slot_owner_index,
    slot_source_position,
    slot_valid_mask,
    near_pick,
):
    blocks = compress.shape[0]
    rhs = field_in.shape[1]
    leaf_count = lax.axis_size("leaf")
    top = leaf_count // 2
    plan = [
        ("leaf", top),
        ("leaf", top // 2),
        ("leaf", top // 4),
        ("sub", 1),
        ("sub", 2),
        ("leaf", top // 4),
        ("leaf", top // 2),
        ("leaf", top),
    ]
    pick = near_pick[0]
    indices = (slot_owner_index.T, slot_source_position.T, slot_valid_mask.T, pick)
    state = VMEM((blocks, rhs, 128), F32)
    wide = VMEM((blocks, 256, 128), BF)
    level_weights = VMEM(coupling.shape[1:], F32)
    coupling_hbm, near_hbm, expand_hbm, field_hbm = in_hbm(coupling, nearfield_dense_blocks, expand, field_in)

    back = VMEM((8, 128), jnp.int32)
    coeffs = call(
        compress_kernel,
        state,
        [HBM] * 2,
        scratch=[VMEM(field_in.shape, F32), VMEM(compress.shape, F32), DMA((1 + blocks // 2,))],
    )(*in_hbm(field_in, compress))
    weights = {}

    def ahead(position, coeffs, levels=(), whole=()):
        parts = list(levels) + [None] * len(whole)
        sources = [coupling_hbm] * len(levels) + list(whole)
        shapes = [level_weights] * len(levels) + [VMEM(array.shape, array.dtype) for array in whole]
        ready, other, places, *got = call(
            functools.partial(ahead_kernel, position, parts),
            [state, wide, back] + shapes,
            [VMEM] * 3 + [HBM] * len(sources),
            [VMEM] * (3 + len(shapes)),
            [DMA((max(len(parts), 1),))],
        )(coeffs, weights[position], names, *sources)
        weights.update(dict(zip(levels, got)))
        return ready, other, places, got[len(levels) :]

    def prepared(weight, after):
        return call(prepare_kernel, [wide, wide], [VMEM, ANY], [VMEM] * 2)(weight, after)

    def prepared_sorted(position, weight, after):
        return call(
            functools.partial(sorted_kernel, position), [wide, wide, back], [VMEM, VMEM, ANY], [VMEM] * 3
        )(weight, names, after)

    def near_piece(number, after):
        begin, count = NEAR_PARTS[number]
        return call(
            functools.partial(near_kernel, begin), VMEM((count, 2 * rhs, 128), F32), [SMEM] * 4 + [VMEM] * 5 + [ANY]
        )(*indices, field, core, far, both, dense, after)

    def own_part(own, wide_own):
        return call(own_kernel, state, [VMEM] * 2)(own, wide_own)

    def own_sorted(position, own, wide_own):
        return call(functools.partial(own_sorted_kernel, position), state, [VMEM] * 3)(own, wide_own, names)

    def level_of(places, other, wide_other, ready, extra):
        return call(level_kernel, state, [VMEM] * 4 + [ANY] * len(extra))(places, other, wide_other, ready, *extra)

    extra_levels = {1: (3,), 2: (4,), 4: (5, 7), 5: ()}
    extra_whole = {4: (near_hbm, field_hbm, expand_hbm)}
    for position, (axis, mask) in enumerate(plan[:-2]):
        other = flipped(coeffs, axis, mask)
        extra = []
        if position == 0:
            far = flipped(tied(field_in, coeffs), "sub", 2)
            ready, wide_other, places, names, packed, weights[1], weights[2] = call(
                functools.partial(first_kernel, 6),
                [
                    state,
                    wide,
                    back,
                    VMEM(roster.shape, jnp.int32),
                    VMEM((blocks + 1,) + coupling.shape[2:], F32),
                    level_weights,
                    level_weights,
                ],
                [VMEM, HBM, HBM],
                [VMEM] * 7,
                [level_weights, DMA((4 + blocks // 4,))],
            )(coeffs, coupling_hbm, *in_hbm(roster))
        elif position == 3:
            ready = own_sorted(3, coeffs, third[0])
            wide_other, places = third[1:]
        else:
            ready, wide_other, places, got = ahead(
                position, coeffs, extra_levels[position], extra_whole.get(position, ())
            )
        if position == 1:
            away = flipped(tied(packed, coeffs), "leaf", top)
        if position == 2:
            third = prepared_sorted(3, weights[3], coeffs)
            extra.append(third[0])
        if position == 4:
            dense, field, expand_ready = got
            core = flipped(tied(field_in, coeffs), "sub", 1)
            both = flipped(tied(far, coeffs), "sub", 1)
            sixth = prepared_sorted(6, packed, coeffs)
            extra.append(sixth[0])
        if position == 5:
            last = call(spread_kernel, wide, [VMEM, ANY])(expand_ready, coeffs)
            seventh = prepared(weights[7], coeffs)
            pieces = [near_piece(0, coeffs)]
            extra += [last, seventh[0], pieces[0]]
        coeffs = level_of(places, other, wide_other, ready, extra)
    side = flipped(coeffs, "leaf", top // 2)
    corner = flipped(coeffs, "leaf", top // 2 + top)
    cross = flipped(coeffs, "leaf", top)
    pieces.append(near_piece(1, coeffs))
    ready = own_sorted(6, coeffs, sixth[0])
    here = level_of(sixth[2], side, sixth[1], ready, [pieces[1]])
    ready = own_part(here, seventh[0])
    away_wide = prepared(away, ready)
    beside = call(corner_kernel, state, [VMEM] * 3)(away, corner, away_wide[1])
    return call(
        functools.partial(last_kernel, 7),
        jax.ShapeDtypeStruct(field_in.shape, F32),
        [VMEM] * (7 + len(pieces)),
        HBM,
        [state, VMEM(field_in.shape, F32), DMA((3,))],
    )(names, cross, away_wide[0], beside, seventh[1], ready, last, *pieces)


def solution(mesh):
    return jax.shard_map(
        on_device,
        mesh=mesh,
        in_specs=(
            P(None, None, ("leaf", "sub")),
            P(("leaf", "sub"), None, None, None),
            P(None, ("leaf", "sub"), None, None, None),
            P(None, ("leaf", "sub"), None),
            P(("leaf", "sub"), None, None, None),
            P(("leaf", "sub"), None, None, None, None),
            P(("leaf", "sub"), None),
            P(("leaf", "sub"), None),
            P(("leaf", "sub"), None),
            P(("leaf", "sub"), None, None),
        ),
        out_specs=P(None, None, ("leaf", "sub")),
        check_vma=False,
    )
```

```python
import functools

import jax
import jax.numpy as jnp
from jax import lax
from jax.experimental import pallas as pl
from jax.experimental.pallas import tpu as pltpu
from jax.sharding import PartitionSpec as P


VMEM = pltpu.VMEM
SMEM = pltpu.SMEM
ANY = pl.ANY
HBM = pltpu.HBM
DMA = pltpu.SemaphoreType.DMA
BF = jnp.bfloat16
F32 = jnp.float32
NT = (((1,), (1,)), ((), ()))
NN = (((1,), (0,)), ((), ()))
NEAR_PARTS = ((0, 4), (4, 8))


def split(value):
    high = value.astype(BF)
    return high, (value - high.astype(F32)).astype(BF)


def widened(rows):
    high, low = split(rows)
    return jnp.concatenate(
        [
            jnp.concatenate([high, high], axis=1),
            jnp.concatenate([low, jnp.zeros_like(low)], axis=1),
        ],
        axis=0,
    )


def folded(result):
    count = result.shape[0] // 2
    return result[:count] + result[count:]


def product(rows, weights):
    wide = jnp.concatenate(split(weights), axis=1)
    return folded(lax.dot_general(widened(rows), wide, NT, preferred_element_type=F32))


def times(rows, wide):
    return folded(lax.dot_general(widened(rows), wide, NN, preferred_element_type=F32))


def lane_low(shape):
    return lax.broadcasted_iota(jnp.int32, shape, 1) < 64


def joined(result):
    rhs = result.shape[0] // 2
    turned = pltpu.roll(result[rhs:], 64, axis=1)
    return result[:rhs] + jnp.where(lane_low(turned.shape), -turned, turned)


def filled(upper):
    turned = pltpu.roll(upper, 64, axis=1)
    lower = jnp.where(lane_low(turned.shape), -turned, turned)
    return jnp.concatenate(split(jnp.concatenate([upper, lower], axis=0)), axis=0)


def halves(block):
    flat = block.T
    return flat[:64], flat[64:]


def started(pairs, sems):
    copies = [pltpu.make_async_copy(source, out, sems.at[n]) for n, (source, out) in enumerate(pairs)]
    for copy in copies:
        copy.start()
    return copies


def finish(copies):
    for copy in copies:
        copy.wait()


def compress_kernel(field_hbm, weight_hbm, out_ref, field_ref, weight_ref, sems):
    blocks = out_ref.shape[0]
    half = blocks // 2
    parts = [pl.ds(0, half), pl.ds(half, blocks - half)]
    copies = started(
        [(field_hbm, field_ref)] + [(weight_hbm.at[part], weight_ref.at[part]) for part in parts], sems
    )
    copies[0].wait()
    for k in range(blocks):
        if k % half == 0:
            copies[1 + k // half].wait()
        lanes = pl.ds(128 * k, 128)
        rows = jnp.concatenate([field_ref[0, :, lanes], field_ref[1, :, lanes]], axis=0)
        out_ref[k] = joined(product(rows, weight_ref[k].reshape(128, 128)))


def entries(row, count):
    return [row[0, k].astype(jnp.int32) for k in range(count)]


def slots(row, count, back_ref):
    places = entries(row, count)
    lane = lax.broadcasted_iota(jnp.int32, back_ref.shape, 1)
    back = jnp.zeros(back_ref.shape, jnp.int32)
    for k, place in enumerate(places):
        back = jnp.where(lane == place, k, back)
    back_ref[...] = back
    return places


def put_row(packed_ref, row):
    blocks = row.shape[1]
    packed_ref[blocks, 0:8, 0:blocks] = jnp.broadcast_to(row.astype(F32), (8, blocks))


def packed_row(packed_ref):
    blocks = packed_ref.shape[0] - 1
    return entries(packed_ref[blocks, 0:8, 0:blocks], blocks)


def prepare_block(k, place, weight_ref, own_out, other_out, packed_ref=None):
    own_half, other_half = halves(weight_ref[k].reshape(128, 128))
    own_out[k] = filled(own_half)
    other_out[place] = filled(other_half)
    if packed_ref is not None:
        packed_ref[k] = other_half


def first_kernel(own_ref, coupling_hbm, roster_hbm, *refs):
    ready_out, other_out, back_ref, roster_ref, own_4, other_4, packed_4, weight_1, weight_2, *rest = refs
    weight_0, weight_4, sems = rest
    blocks = own_ref.shape[0]
    copies = started(
        [(roster_hbm, roster_ref)]
        + [(coupling_hbm.at[n], out) for n, out in ((0, weight_0), (4, weight_4), (1, weight_1), (2, weight_2))],
        sems,
    )
    copies[0].wait()
    places = slots(roster_ref[0], blocks, back_ref)
    put_row(packed_4, roster_ref[4])
    copies[1].wait()
    for k, place in enumerate(places):
        own_half, other_half = halves(weight_0[k].reshape(128, 128))
        other_out[place] = filled(other_half)
        ready_out[place] = times(own_ref[k], filled(own_half))
    copies[2].wait()
    for k in range(blocks):
        prepare_block(k, k, weight_4, own_4, other_4, packed_4)
    finish(copies[3:])


def ahead_kernel(level, own_ref, weight_ref, roster_ref, coupling_hbm, *refs):
    ready_out, other_out, back_ref, weight_3, weight_6, sems = refs
    copies = started([(coupling_hbm.at[3], weight_3), (coupling_hbm.at[6], weight_6)], sems)
    for k, place in enumerate(slots(roster_ref[level], own_ref.shape[0], back_ref)):
        own_half, other_half = halves(weight_ref[k].reshape(128, 128))
        other_out[place] = filled(other_half)
        ready_out[place] = times(own_ref[k], filled(own_half))
    finish(copies)


def sorted_kernel(level, weight_ref, roster_ref, after_ref, own_out, other_out, back_ref):
    for k, place in enumerate(slots(roster_ref[level], own_out.shape[0], back_ref)):
        prepare_block(k, place, weight_ref, own_out, other_out)


def packed_kernel(level, weight_ref, roster_ref, after_ref, own_out, other_out, packed_ref):
    put_row(packed_ref, roster_ref[level])
    for k in range(own_out.shape[0]):
        prepare_block(k, k, weight_ref, own_out, other_out, packed_ref)


def fetch_kernel(levels, coupling_hbm, after_ref, *refs):
    count = len(levels)
    outs, weights, sems = refs[: 2 * count], refs[2 * count : -1], refs[-1]
    copies = started([(coupling_hbm.at[level], out) for level, out in zip(levels, weights)], sems)
    for n in range(count):
        copies[n].wait()
        for k in range(weights[n].shape[0]):
            prepare_block(k, k, weights[n], outs[2 * n], outs[2 * n + 1])


def unpack_kernel(packed_ref, after_ref, out_ref):
    for k in range(out_ref.shape[0]):
        out_ref[k] = filled(packed_ref[k])


def spread_kernel(weight_ref, after_ref, out_ref):
    for k in range(out_ref.shape[0]):
        out_ref[k] = jnp.concatenate(split(weight_ref[k].reshape(128, 128)), axis=0)


def own_kernel(own_ref, wide_ref, out_ref):
    for k in range(out_ref.shape[0]):
        out_ref[k] = times(own_ref[k], wide_ref[k])


def own_sorted_kernel(level, own_ref, wide_ref, roster_ref, out_ref):
    for k, place in enumerate(entries(roster_ref[level], out_ref.shape[0])):
        out_ref[place] = times(own_ref[k], wide_ref[k])


def level_kernel(back_ref, other_ref, wide_ref, ready_ref, *rest):
    out_ref = rest[-1]
    for place, k in enumerate(entries(back_ref[0:1, :], out_ref.shape[0])):
        out_ref[k] = ready_ref[place] + times(other_ref[place], wide_ref[place])


def plain_kernel(level, roster_ref, other_ref, wide_ref, ready_ref, *rest):
    out_ref = rest[-1]
    for k, place in enumerate(entries(roster_ref[level], out_ref.shape[0])):
        out_ref[k] = ready_ref[k] + times(other_ref[place], wide_ref[k])


def side_kernel(level, roster_ref, packed_ref, corner_ref, away_ref, beside_ref, wide_ref, out_ref, there_ref):
    blocks = out_ref.shape[0]
    for k, place in enumerate(packed_row(packed_ref)):
        there_ref[k] = beside_ref[k] + times(corner_ref[place], away_ref[k])
    for k, place in enumerate(entries(roster_ref[level], blocks)):
        out_ref[k] = times(there_ref[place], wide_ref[k])


def double_kernel(level, roster_ref, other_ref, wide_ref, ready_ref, next_ref, side_ref, *rest):
    out_ref, here_ref = rest[-2:]
    for k, place in enumerate(entries(roster_ref[level], out_ref.shape[0])):
        here_ref[k] = ready_ref[k] + times(other_ref[place], wide_ref[k])
    for k in range(out_ref.shape[0]):
        out_ref[k] = side_ref[k] + times(here_ref[k], next_ref[k])


def corner_kernel(packed_ref, other_ref, wide_ref, out_ref):
    for k, place in enumerate(packed_row(packed_ref)):
        out_ref[k] = times(other_ref[place], wide_ref[k])


def last_kernel(level, roster_ref, beside_ref, corner_ref, wide_ref, ready_ref, expand_ref, *rest):
    near_refs, (out_hbm, out_ref, sems) = rest[:-3], rest[-3:]
    blocks = beside_ref.shape[0]
    copies = []
    for k, place in enumerate(entries(roster_ref[level], blocks)):
        coeffs = ready_ref[k] + times(beside_ref[place] + corner_ref[place], wide_ref[k])
        signed = jnp.where(lane_low(coeffs.shape), coeffs, -coeffs)
        turned = pltpu.roll(coeffs, 64, axis=1)
        far = times(jnp.concatenate([signed, turned], axis=0), expand_ref[k])
        which = [n for n, (begin, count) in enumerate(NEAR_PARTS) if begin <= k < begin + count][0]
        total = far + near_refs[which][k - NEAR_PARTS[which][0]]
        half = total.shape[0] // 2
        lanes = pl.ds(128 * k, 128)
        out_ref[0, :, lanes] = total[:half]
        out_ref[1, :, lanes] = total[half:]
        if k % 4 == 3:
            part = pl.ds(128 * (k - 3), 512)
            copy = pltpu.make_async_copy(out_ref.at[:, :, part], out_hbm.at[:, :, part], sems.at[k // 4])
            copy.start()
            copies.append(copy)
    finish(copies)


def near_kernel(first, owner_ref, place_ref, valid_ref, pick_ref, own_ref, core_ref, far_ref, both_ref, weight_ref, *rest):
    out_ref = rest[-1]
    me = lax.axis_index("sub")
    for n in range(out_ref.shape[0]):
        k = first + n
        total = None
        for t in range(weight_ref.shape[1]):
            owner = owner_ref[t, k]
            leaf = pick_ref[owner, place_ref[t, k]]
            lanes = pl.ds(pl.multiple_of(leaf * 128, 128), 128)
            which = owner ^ me
            parts = []
            for d in range(2):
                low = jnp.where(which == 1, core_ref[d, :, lanes], own_ref[d, :, lanes])
                high = jnp.where(which == 3, both_ref[d, :, lanes], far_ref[d, :, lanes])
                parts.append(jnp.where(which >= 2, high, low))
            rows = jnp.concatenate(parts, axis=0) * valid_ref[t, k].astype(F32)
            result = product(rows, weight_ref[k, t].reshape(256, 128))
            half = result.shape[0] // 2
            term = jnp.concatenate(
                [result[:half, :128] - result[half:, 128:], result[half:, :128] + result[:half, 128:]], axis=0
            )
            total = term if total is None else total + term
        out_ref[n] = total


def spec(space):
    return pl.BlockSpec(memory_space=space)


def call(kernel, out, spaces, out_spaces=VMEM, scratch=(), flops=2_000_000):
    single = not isinstance(out_spaces, (list, tuple))
    return pl.pallas_call(
        kernel,
        out_shape=out,
        in_specs=[spec(space) for space in spaces],
        out_specs=spec(out_spaces) if single else [spec(space) for space in out_spaces],
        scratch_shapes=list(scratch),
        compiler_params=pltpu.CompilerParams(vmem_limit_bytes=8 << 20),
        cost_estimate=pl.CostEstimate(flops=flops, bytes_accessed=1 << 20, transcendentals=0),
    )


def in_hbm(*arrays):
    return [pltpu.with_memory_space_constraint(array, HBM) for array in arrays]


def flipped(value, leaf_mask, sub_mask):
    sub_count = lax.axis_size("sub")
    mask = leaf_mask * sub_count + sub_mask
    pairs = [(source, source ^ mask) for source in range(lax.axis_size("leaf") * sub_count)]
    return lax.ppermute(value, ("leaf", "sub"), pairs)


def tied(value, after):
    return lax.optimization_barrier((value, after))[0]


def on_device(
    field_in,
    compress,
    coupling,
    roster,
    expand,
    nearfield_dense_blocks,
    slot_owner_index,
    slot_source_position,
    slot_valid_mask,
    near_pick,
):
    blocks = compress.shape[0]
    rhs = field_in.shape[1]
    top = lax.axis_size("leaf") // 2
    pick = near_pick[0]
    indices = (slot_owner_index.T, slot_source_position.T, slot_valid_mask.T, pick)
    state = VMEM((blocks, rhs, 128), F32)
    wide = VMEM((blocks, 256, 128), BF)
    back = VMEM((8, 128), jnp.int32)
    packed = VMEM((blocks + 1, 64, 128), F32)
    level_weights = VMEM(coupling.shape[1:], F32)
    (coupling_hbm, _, roster_hbm) = in_hbm(coupling, field_in, roster)
    field = pltpu.with_memory_space_constraint(field_in, VMEM)
    dense = pltpu.with_memory_space_constraint(nearfield_dense_blocks, VMEM)
    expanding = pltpu.with_memory_space_constraint(expand, VMEM)

    def run(kernel, outs, inputs, after=(), scratch=(), hbm=()):
        spaces = [HBM if n in hbm else VMEM for n in range(len(inputs))] + [ANY] * len(after)
        several = isinstance(outs, list)
        return call(kernel, outs, spaces, [VMEM] * len(outs) if several else VMEM, scratch)(*inputs, *after)

    def near_piece(number, after):
        begin, count = NEAR_PARTS[number]
        return call(
            functools.partial(near_kernel, begin), VMEM((count, 2 * rhs, 128), F32), [SMEM] * 4 + [VMEM] * 5 + [ANY]
        )(*indices, field, core, far, both, dense, after)

    part = functools.partial
    coeffs = run(
        compress_kernel,
        state,
        in_hbm(field_in, compress),
        scratch=[VMEM(field_in.shape, F32), VMEM(compress.shape, F32), DMA((3,))],
        hbm=(0, 1),
    )

    other = flipped(coeffs, top, 0)
    ready, wide_0, back_0, names, own_4, wide_4, packed_4, weight_1, weight_2 = run(
        first_kernel,
        [state, wide, back, VMEM(roster.shape, jnp.int32), wide, wide, packed, level_weights, level_weights],
        [coeffs, coupling_hbm, roster_hbm],
        scratch=[level_weights, level_weights, DMA((5,))],
        hbm=(1, 2),
    )
    away_4 = flipped(packed_4, top // 4, 0)
    own_2, wide_2, back_2 = run(part(sorted_kernel, 2), [wide, wide, back], [weight_2, names], [coeffs])
    coeffs = run(level_kernel, state, [back_0, other, wide_0, ready], [own_2])

    other = flipped(coeffs, top // 2, 0)
    ready, wide_1, back_1, weight_3, weight_6 = run(
        part(ahead_kernel, 1),
        [state, wide, back, level_weights, level_weights],
        [coeffs, weight_1, names, coupling_hbm],
        scratch=[DMA((2,))],
        hbm=(3,),
    )
    own_3, wide_3, back_3 = run(part(sorted_kernel, 3), [wide, wide, back], [weight_3, names], [coeffs])
    own_6, wide_6, packed_6 = run(part(packed_kernel, 6), [wide, wide, packed], [weight_6, names], [coeffs])
    coeffs = run(level_kernel, state, [back_1, other, wide_1, ready], [own_3, own_6])

    other = flipped(coeffs, top // 4, 0)
    far = flipped(tied(field_in, coeffs), 0, 2)
    away_6 = flipped(tied(packed_6, coeffs), top, 0)
    ready = run(part(own_sorted_kernel, 2), state, [coeffs, own_2, names])
    coeffs = run(level_kernel, state, [back_2, other, wide_2, ready])

    other = flipped(coeffs, 0, 1)
    ready = run(part(own_sorted_kernel, 3), state, [coeffs, own_3, names])
    coeffs = run(level_kernel, state, [back_3, other, wide_3, ready])

    corner = flipped(coeffs, top // 4, 2)
    ready = run(own_kernel, state, [coeffs, own_4])
    beside = flipped(ready, top // 4, 0)
    other = flipped(coeffs, 0, 2)
    own_5, wide_5, own_7, wide_7 = run(
        part(fetch_kernel, (5, 7)),
        [wide] * 4,
        [coupling_hbm],
        [coeffs],
        scratch=[level_weights, level_weights, DMA((2,))],
        hbm=(0,),
    )
    core = flipped(tied(field_in, coeffs), 0, 1)
    both = flipped(tied(far, coeffs), 0, 1)
    away = run(unpack_kernel, wide, [away_4], [coeffs])
    side = run(part(side_kernel, 5), state, [names, away_4, corner, away, beside, wide_5], scratch=[state])
    coeffs = run(part(double_kernel, 4), state, [names, other, wide_4, ready, own_5, side], [own_7], scratch=[state])

    other = flipped(coeffs, top // 2, 0)
    ready = run(own_kernel, state, [coeffs, own_6])
    corner = flipped(coeffs, top // 2 + top, 0)
    beside = flipped(ready, top, 0)
    last = run(spread_kernel, wide, [expanding], [coeffs])
    away = run(unpack_kernel, wide, [away_6], [coeffs])
    pieces = [near_piece(n, coeffs) for n in range(len(NEAR_PARTS))]
    here = run(part(plain_kernel, 6), state, [names, other, wide_6, ready], [pieces[0]])
    ready = run(own_kernel, state, [here, own_7])
    corner = run(corner_kernel, state, [away_6, corner, away])
    return call(
        part(last_kernel, 7),
        jax.ShapeDtypeStruct(field_in.shape, F32),
        [VMEM] * (6 + len(pieces)),
        HBM,
        [VMEM(field_in.shape, F32), DMA((3,))],
    )(names, beside, corner, wide_7, ready, last, *pieces)


def solution(mesh):
    return jax.shard_map(
        on_device,
        mesh=mesh,
        in_specs=(
            P(None, None, ("leaf", "sub")),
            P(("leaf", "sub"), None, None, None),
            P(None, ("leaf", "sub"), None, None, None),
            P(None, ("leaf", "sub"), None),
            P(("leaf", "sub"), None, None, None),
            P(("leaf", "sub"), None, None, None, None),
            P(("leaf", "sub"), None),
            P(("leaf", "sub"), None),
            P(("leaf", "sub"), None),
            P(("leaf", "sub"), None, None),
        ),
        out_specs=P(None, None, ("leaf", "sub")),
        check_vma=False,
    )
```

```python
import functools

import jax
import jax.numpy as jnp
from jax import lax
from jax.experimental import pallas as pl
from jax.experimental.pallas import tpu as pltpu
from jax.sharding import PartitionSpec as P


VMEM = pltpu.VMEM
SMEM = pltpu.SMEM
ANY = pl.ANY
HBM = pltpu.HBM
DMA = pltpu.SemaphoreType.DMA
BF = jnp.bfloat16
F32 = jnp.float32
NT = (((1,), (1,)), ((), ()))
NN = (((1,), (0,)), ((), ()))
NEAR_PARTS = ((0, 4), (4, 8))


def split(value):
    high = value.astype(BF)
    return high, (value - high.astype(F32)).astype(BF)


def widened(rows):
    high, low = split(rows)
    return jnp.concatenate(
        [
            jnp.concatenate([high, high], axis=1),
            jnp.concatenate([low, jnp.zeros_like(low)], axis=1),
        ],
        axis=0,
    )


def folded(result):
    count = result.shape[0] // 2
    return result[:count] + result[count:]


def product(rows, weights):
    wide = jnp.concatenate(split(weights), axis=1)
    return folded(lax.dot_general(widened(rows), wide, NT, preferred_element_type=F32))


def times(rows, wide):
    return folded(lax.dot_general(widened(rows), wide, NN, preferred_element_type=F32))


def lane_low(shape):
    return lax.broadcasted_iota(jnp.int32, shape, 1) < 64


def joined(result):
    rhs = result.shape[0] // 2
    turned = pltpu.roll(result[rhs:], 64, axis=1)
    return result[:rhs] + jnp.where(lane_low(turned.shape), -turned, turned)


def filled(upper):
    turned = pltpu.roll(upper, 64, axis=1)
    lower = jnp.where(lane_low(turned.shape), -turned, turned)
    return jnp.concatenate(split(jnp.concatenate([upper, lower], axis=0)), axis=0)


def halves(block):
    flat = block.T
    return flat[:64], flat[64:]


def started(pairs, sems):
    copies = [pltpu.make_async_copy(source, out, sems.at[n]) for n, (source, out) in enumerate(pairs)]
    for copy in copies:
        copy.start()
    return copies


def finish(copies):
    for copy in copies:
        copy.wait()


def compress_kernel(field_hbm, weight_hbm, coupling_hbm, roster_hbm, out_ref, next_ref, roster_ref, field_ref, weight_ref, sems):
    blocks = out_ref.shape[0]
    half = blocks // 2
    parts = [pl.ds(0, half), pl.ds(half, blocks - half)]
    copies = started(
        [(field_hbm, field_ref)]
        + [(weight_hbm.at[part], weight_ref.at[part]) for part in parts]
        + [(roster_hbm, roster_ref), (coupling_hbm.at[0], next_ref)],
        sems,
    )
    copies[0].wait()
    for k in range(blocks):
        if k % half == 0:
            copies[1 + k // half].wait()
        lanes = pl.ds(128 * k, 128)
        rows = jnp.concatenate([field_ref[0, :, lanes], field_ref[1, :, lanes]], axis=0)
        out_ref[k] = joined(product(rows, weight_ref[k].reshape(128, 128)))
    finish(copies[3:])


def entries(row, count):
    return [row[0, k].astype(jnp.int32) for k in range(count)]


def slots(row, count, back_ref):
    places = entries(row, count)
    lane = lax.broadcasted_iota(jnp.int32, back_ref.shape, 1)
    back = jnp.zeros(back_ref.shape, jnp.int32)
    for k, place in enumerate(places):
        back = jnp.where(lane == place, k, back)
    back_ref[...] = back
    return places


def put_row(packed_ref, row):
    blocks = row.shape[1]
    packed_ref[blocks, 0:8, 0:blocks] = jnp.broadcast_to(row.astype(F32), (8, blocks))


def packed_row(packed_ref, blocks):
    return entries(packed_ref[packed_ref.shape[0] - 1, 0:8, 0:blocks], blocks)


def prepare_block(k, place, weight_ref, own_out, other_out, packed_ref=None):
    own_half, other_half = halves(weight_ref[k].reshape(128, 128))
    own_out[k] = filled(own_half)
    other_out[place] = filled(other_half)
    if packed_ref is not None:
        packed_ref[k] = other_half


def start_level(level, own_ref, weight_ref, roster_ref, ready_out, other_out, back_ref):
    for k, place in enumerate(slots(roster_ref[level], own_ref.shape[0], back_ref)):
        own_half, other_half = halves(weight_ref[k].reshape(128, 128))
        other_out[place] = filled(other_half)
        ready_out[place] = times(own_ref[k], filled(own_half))


def first_kernel(own_ref, weight_0, roster_ref, coupling_hbm, *refs):
    ready_out, other_out, back_ref, own_4, other_4, packed_a, packed_b, weight_1, weight_2, weight_4, sems = refs
    blocks = own_ref.shape[0]
    half = packed_b.shape[0]
    copies = started([(coupling_hbm.at[n], out) for n, out in ((4, weight_4), (1, weight_1), (2, weight_2))], sems)
    start_level(0, own_ref, weight_0, roster_ref, ready_out, other_out, back_ref)
    packed_a[half, 0:8, 0:blocks] = jnp.broadcast_to(roster_ref[4].astype(F32), (8, blocks))
    copies[0].wait()
    for k in range(blocks):
        own_half, other_half = halves(weight_4[k].reshape(128, 128))
        own_4[k] = filled(own_half)
        other_4[k] = filled(other_half)
        if k < half:
            packed_a[k] = other_half
        else:
            packed_b[k - half] = other_half
    finish(copies[1:])


def ahead_kernel(level, own_ref, weight_ref, roster_ref, weight_2, coupling_hbm, *refs):
    ready_out, other_out, back_ref, own_2, other_2, back_2, weight_3, weight_6, sems = refs
    copies = started([(coupling_hbm.at[3], weight_3), (coupling_hbm.at[6], weight_6)], sems)
    start_level(level, own_ref, weight_ref, roster_ref, ready_out, other_out, back_ref)
    for k, place in enumerate(slots(roster_ref[level + 1], own_ref.shape[0], back_2)):
        prepare_block(k, place, weight_2, own_2, other_2)
    finish(copies)


def sorted_kernel(level, weight_ref, roster_ref, after_ref, own_out, other_out, back_ref):
    for k, place in enumerate(slots(roster_ref[level], own_out.shape[0], back_ref)):
        prepare_block(k, place, weight_ref, own_out, other_out)


def packed_kernel(level, weight_ref, roster_ref, after_ref, own_out, other_out, packed_ref):
    put_row(packed_ref, roster_ref[level])
    for k in range(own_out.shape[0]):
        prepare_block(k, k, weight_ref, own_out, other_out, packed_ref)


def fetch_kernel(levels, coupling_hbm, after_ref, *refs):
    count = len(levels)
    outs, weights, sems = refs[: 2 * count], refs[2 * count : -1], refs[-1]
    copies = started([(coupling_hbm.at[level], out) for level, out in zip(levels, weights)], sems)
    for n in range(count):
        copies[n].wait()
        for k in range(weights[n].shape[0]):
            prepare_block(k, k, weights[n], outs[2 * n], outs[2 * n + 1])


def unpack_kernel(packed_ref, *rest):
    out_ref = rest[-1]
    for k in range(out_ref.shape[0]):
        half = packed_ref.shape[0] - 1
        out_ref[k] = filled(packed_ref[k] if k < half else rest[0][k - half])


def spread_kernel(weight_ref, after_ref, out_ref):
    for k in range(out_ref.shape[0]):
        out_ref[k] = jnp.concatenate(split(weight_ref[k].reshape(128, 128)), axis=0)


def own_kernel(own_ref, wide_ref, out_ref):
    for k in range(out_ref.shape[0]):
        out_ref[k] = times(own_ref[k], wide_ref[k])


def own_sorted_kernel(level, own_ref, wide_ref, roster_ref, out_ref):
    for k, place in enumerate(entries(roster_ref[level], out_ref.shape[0])):
        out_ref[place] = times(own_ref[k], wide_ref[k])


def level_kernel(back_ref, other_ref, wide_ref, ready_ref, *rest):
    out_ref = rest[-1]
    for place, k in enumerate(entries(back_ref[0:1, :], out_ref.shape[0])):
        out_ref[k] = ready_ref[place] + times(other_ref[place], wide_ref[place])


def plain_kernel(level, roster_ref, other_ref, wide_ref, ready_ref, *rest):
    out_ref = rest[-1]
    for k, place in enumerate(entries(roster_ref[level], out_ref.shape[0])):
        out_ref[k] = ready_ref[k] + times(other_ref[place], wide_ref[k])


def side_kernel(level, roster_ref, packed_ref, corner_ref, away_ref, beside_ref, wide_ref, out_ref, there_ref):
    blocks = out_ref.shape[0]
    for k, place in enumerate(packed_row(packed_ref, out_ref.shape[0])):
        there_ref[k] = beside_ref[k] + times(corner_ref[place], away_ref[k])
    for k, place in enumerate(entries(roster_ref[level], blocks)):
        out_ref[k] = times(there_ref[place], wide_ref[k])


def double_kernel(level, roster_ref, other_ref, wide_ref, ready_ref, next_ref, side_ref, *rest):
    out_ref, here_ref = rest[-2:]
    for k, place in enumerate(entries(roster_ref[level], out_ref.shape[0])):
        here_ref[k] = ready_ref[k] + times(other_ref[place], wide_ref[k])
    for k in range(out_ref.shape[0]):
        out_ref[k] = side_ref[k] + times(here_ref[k], next_ref[k])


def corner_kernel(packed_ref, other_ref, wide_ref, out_ref):
    for k, place in enumerate(packed_row(packed_ref, out_ref.shape[0])):
        out_ref[k] = times(other_ref[place], wide_ref[k])


def last_kernel(level, roster_ref, beside_ref, corner_ref, wide_ref, ready_ref, expand_ref, *rest):
    near_refs, (out_hbm, out_ref, sems) = rest[:-3], rest[-3:]
    blocks = beside_ref.shape[0]
    copies = []
    for k, place in enumerate(entries(roster_ref[level], blocks)):
        coeffs = ready_ref[k] + times(beside_ref[place] + corner_ref[place], wide_ref[k])
        signed = jnp.where(lane_low(coeffs.shape), coeffs, -coeffs)
        turned = pltpu.roll(coeffs, 64, axis=1)
        far = times(jnp.concatenate([signed, turned], axis=0), expand_ref[k])
        which = [n for n, (begin, count) in enumerate(NEAR_PARTS) if begin <= k < begin + count][0]
        total = far + near_refs[which][k - NEAR_PARTS[which][0]]
        half = total.shape[0] // 2
        lanes = pl.ds(128 * k, 128)
        out_ref[0, :, lanes] = total[:half]
        out_ref[1, :, lanes] = total[half:]
        if k % 4 == 3:
            part = pl.ds(128 * (k - 3), 512)
            copy = pltpu.make_async_copy(out_ref.at[:, :, part], out_hbm.at[:, :, part], sems.at[k // 4])
            copy.start()
            copies.append(copy)
    finish(copies)


def near_kernel(first, owner_ref, place_ref, valid_ref, pick_ref, own_ref, core_ref, far_ref, both_ref, weight_ref, *rest):
    out_ref = rest[-1]
    me = lax.axis_index("sub")
    for n in range(out_ref.shape[0]):
        k = first + n
        total = None
        for t in range(weight_ref.shape[1]):
            owner = owner_ref[t, k]
            leaf = pick_ref[owner, place_ref[t, k]]
            lanes = pl.ds(pl.multiple_of(leaf * 128, 128), 128)
            which = owner ^ me
            parts = []
            for d in range(2):
                low = jnp.where(which == 1, core_ref[d, :, lanes], own_ref[d, :, lanes])
                high = jnp.where(which == 3, both_ref[d, :, lanes], far_ref[d, :, lanes])
                parts.append(jnp.where(which >= 2, high, low))
            rows = jnp.concatenate(parts, axis=0) * valid_ref[t, k].astype(F32)
            result = product(rows, weight_ref[k, t].reshape(256, 128))
            half = result.shape[0] // 2
            term = jnp.concatenate(
                [result[:half, :128] - result[half:, 128:], result[half:, :128] + result[:half, 128:]], axis=0
            )
            total = term if total is None else total + term
        out_ref[n] = total


def spec(space):
    return pl.BlockSpec(memory_space=space)


def call(kernel, out, spaces, out_spaces=VMEM, scratch=(), flops=2_000_000):
    single = not isinstance(out_spaces, (list, tuple))
    return pl.pallas_call(
        kernel,
        out_shape=out,
        in_specs=[spec(space) for space in spaces],
        out_specs=spec(out_spaces) if single else [spec(space) for space in out_spaces],
        scratch_shapes=list(scratch),
        compiler_params=pltpu.CompilerParams(vmem_limit_bytes=8 << 20),
        cost_estimate=pl.CostEstimate(flops=flops, bytes_accessed=1 << 20, transcendentals=0),
    )


def in_hbm(*arrays):
    return [pltpu.with_memory_space_constraint(array, HBM) for array in arrays]


def flipped(value, leaf_mask, sub_mask):
    sub_count = lax.axis_size("sub")
    mask = leaf_mask * sub_count + sub_mask
    pairs = [(source, source ^ mask) for source in range(lax.axis_size("leaf") * sub_count)]
    return lax.ppermute(value, ("leaf", "sub"), pairs)


def tied(value, after):
    return lax.optimization_barrier((value, after))[0]


def on_device(
    field_in,
    compress,
    coupling,
    roster,
    expand,
    nearfield_dense_blocks,
    slot_owner_index,
    slot_source_position,
    slot_valid_mask,
    near_pick,
):
    blocks = compress.shape[0]
    rhs = field_in.shape[1]
    top = lax.axis_size("leaf") // 2
    pick = near_pick[0]
    indices = (slot_owner_index.T, slot_source_position.T, slot_valid_mask.T, pick)
    state = VMEM((blocks, rhs, 128), F32)
    wide = VMEM((blocks, 256, 128), BF)
    back = VMEM((8, 128), jnp.int32)
    packed = VMEM((blocks + 1, 64, 128), F32)
    level_weights = VMEM(coupling.shape[1:], F32)
    (coupling_hbm, _, roster_hbm) = in_hbm(coupling, field_in, roster)
    field = pltpu.with_memory_space_constraint(field_in, VMEM)
    dense = pltpu.with_memory_space_constraint(nearfield_dense_blocks, VMEM)
    expanding = pltpu.with_memory_space_constraint(expand, VMEM)

    def run(kernel, outs, inputs, after=(), scratch=(), hbm=()):
        spaces = [HBM if n in hbm else VMEM for n in range(len(inputs))] + [ANY] * len(after)
        several = isinstance(outs, list)
        return call(kernel, outs, spaces, [VMEM] * len(outs) if several else VMEM, scratch)(*inputs, *after)

    def near_piece(number, after):
        begin, count = NEAR_PARTS[number]
        return call(
            functools.partial(near_kernel, begin), VMEM((count, 2 * rhs, 128), F32), [SMEM] * 4 + [VMEM] * 5 + [ANY]
        )(*indices, field, core, far, both, dense, after)

    part = functools.partial
    coeffs, weight_0, names = run(
        compress_kernel,
        [state, level_weights, VMEM(roster.shape, jnp.int32)],
        [*in_hbm(field_in, compress), coupling_hbm, roster_hbm],
        scratch=[VMEM(field_in.shape, F32), VMEM(compress.shape, F32), DMA((5,))],
        hbm=(0, 1, 2, 3),
    )

    other = flipped(coeffs, top, 0)
    half = blocks // 2
    ready, wide_0, back_0, own_4, wide_4, packed_4, packed_more, weight_1, weight_2 = run(
        first_kernel,
        [
            state,
            wide,
            back,
            wide,
            wide,
            VMEM((half + 1, 64, 128), F32),
            VMEM((blocks - half, 64, 128), F32),
            level_weights,
            level_weights,
        ],
        [coeffs, weight_0, names, coupling_hbm],
        scratch=[level_weights, DMA((3,))],
        hbm=(3,),
    )
    away_4 = flipped(packed_4, top // 4, 0)
    far = flipped(tied(field_in, wide_4), 0, 2)
    coeffs = run(level_kernel, state, [back_0, other, wide_0, ready])

    other = flipped(coeffs, top // 2, 0)
    ready, wide_1, back_1, own_2, wide_2, back_2, weight_3, weight_6 = run(
        part(ahead_kernel, 1),
        [state, wide, back, wide, wide, back, level_weights, level_weights],
        [coeffs, weight_1, names, weight_2, coupling_hbm],
        scratch=[DMA((2,))],
        hbm=(4,),
    )
    own_3, wide_3, back_3 = run(part(sorted_kernel, 3), [wide, wide, back], [weight_3, names], [coeffs])
    own_6, wide_6, packed_6 = run(part(packed_kernel, 6), [wide, wide, packed], [weight_6, names], [coeffs])
    coeffs = run(level_kernel, state, [back_1, other, wide_1, ready], [own_3, own_6])

    other = flipped(coeffs, top // 4, 0)
    away_more = flipped(tied(packed_more, coeffs), top // 4, 0)
    away_6 = flipped(tied(packed_6, coeffs), top, 0)
    ready = run(part(own_sorted_kernel, 2), state, [coeffs, own_2, names])
    coeffs = run(level_kernel, state, [back_2, other, wide_2, ready])

    other = flipped(coeffs, 0, 1)
    ready = run(part(own_sorted_kernel, 3), state, [coeffs, own_3, names])
    coeffs = run(level_kernel, state, [back_3, other, wide_3, ready])

    corner = flipped(coeffs, top // 4, 2)
    ready = run(own_kernel, state, [coeffs, own_4])
    beside = flipped(ready, top // 4, 0)
    other = flipped(coeffs, 0, 2)
    own_5, wide_5, own_7, wide_7 = run(
        part(fetch_kernel, (5, 7)),
        [wide] * 4,
        [coupling_hbm],
        [coeffs],
        scratch=[level_weights, level_weights, DMA((2,))],
        hbm=(0,),
    )
    core = flipped(tied(field_in, coeffs), 0, 1)
    both = flipped(tied(far, coeffs), 0, 1)
    away = run(unpack_kernel, wide, [away_4, away_more], [coeffs])
    side = run(part(side_kernel, 5), state, [names, away_4, corner, away, beside, wide_5], scratch=[state])
    coeffs = run(part(double_kernel, 4), state, [names, other, wide_4, ready, own_5, side], [own_7], scratch=[state])

    other = flipped(coeffs, top // 2, 0)
    ready = run(own_kernel, state, [coeffs, own_6])
    corner = flipped(coeffs, top // 2 + top, 0)
    beside = flipped(ready, top, 0)
    last = run(spread_kernel, wide, [expanding], [coeffs])
    away = run(unpack_kernel, wide, [away_6], [coeffs])
    pieces = [near_piece(n, coeffs) for n in range(len(NEAR_PARTS))]
    here = run(part(plain_kernel, 6), state, [names, other, wide_6, ready], [pieces[0]])
    ready = run(own_kernel, state, [here, own_7])
    corner = run(corner_kernel, state, [away_6, corner, away])
    return call(
        part(last_kernel, 7),
        jax.ShapeDtypeStruct(field_in.shape, F32),
        [VMEM] * (6 + len(pieces)),
        HBM,
        [VMEM(field_in.shape, F32), DMA((3,))],
    )(names, beside, corner, wide_7, ready, last, *pieces)


def solution(mesh):
    return jax.shard_map(
        on_device,
        mesh=mesh,
        in_specs=(
            P(None, None, ("leaf", "sub")),
            P(("leaf", "sub"), None, None, None),
            P(None, ("leaf", "sub"), None, None, None),
            P(None, ("leaf", "sub"), None),
            P(("leaf", "sub"), None, None, None),
            P(("leaf", "sub"), None, None, None, None),
            P(("leaf", "sub"), None),
            P(("leaf", "sub"), None),
            P(("leaf", "sub"), None),
            P(("leaf", "sub"), None, None),
        ),
        out_specs=P(None, None, ("leaf", "sub")),
        check_vma=False,
    )
```

```python
import functools

import jax
import jax.numpy as jnp
from jax import lax
from jax.experimental import pallas as pl
from jax.experimental.pallas import tpu as pltpu
from jax.sharding import PartitionSpec as P


VMEM = pltpu.VMEM
SMEM = pltpu.SMEM
ANY = pl.ANY
HBM = pltpu.HBM
DMA = pltpu.SemaphoreType.DMA
BF = jnp.bfloat16
F32 = jnp.float32
NT = (((1,), (1,)), ((), ()))
NN = (((1,), (0,)), ((), ()))
NEAR_PARTS = ((0, 4), (4, 8))


def split(value):
    high = value.astype(BF)
    return high, (value - high.astype(F32)).astype(BF)


def widened(rows):
    high, low = split(rows)
    return jnp.concatenate(
        [
            jnp.concatenate([high, high], axis=1),
            jnp.concatenate([low, jnp.zeros_like(low)], axis=1),
        ],
        axis=0,
    )


def folded(result):
    count = result.shape[0] // 2
    return result[:count] + result[count:]


def product(rows, weights):
    wide = jnp.concatenate(split(weights), axis=1)
    return folded(lax.dot_general(widened(rows), wide, NT, preferred_element_type=F32))


def times(rows, wide):
    return folded(lax.dot_general(widened(rows), wide, NN, preferred_element_type=F32))


def lane_low(shape):
    return lax.broadcasted_iota(jnp.int32, shape, 1) < 64


def joined(result):
    rhs = result.shape[0] // 2
    turned = pltpu.roll(result[rhs:], 64, axis=1)
    return result[:rhs] + jnp.where(lane_low(turned.shape), -turned, turned)


def filled(upper):
    turned = pltpu.roll(upper, 64, axis=1)
    lower = jnp.where(lane_low(turned.shape), -turned, turned)
    return jnp.concatenate(split(jnp.concatenate([upper, lower], axis=0)), axis=0)


def halves(block):
    flat = block.T
    return flat[:64], flat[64:]


def started(pairs, sems):
    copies = [pltpu.make_async_copy(source, out, sems.at[n]) for n, (source, out) in enumerate(pairs)]
    for copy in copies:
        copy.start()
    return copies


def finish(copies):
    for copy in copies:
        copy.wait()


def compress_kernel(field_hbm, weight_hbm, coupling_hbm, roster_hbm, out_ref, next_ref, roster_ref, field_ref, weight_ref, sems):
    blocks = out_ref.shape[0]
    half = blocks // 2
    parts = [pl.ds(0, half), pl.ds(half, blocks - half)]
    copies = started(
        [(field_hbm, field_ref)]
        + [(weight_hbm.at[part], weight_ref.at[part]) for part in parts]
        + [(roster_hbm, roster_ref), (coupling_hbm.at[0], next_ref)],
        sems,
    )
    copies[0].wait()
    for k in range(blocks):
        if k % half == 0:
            copies[1 + k // half].wait()
        lanes = pl.ds(128 * k, 128)
        rows = jnp.concatenate([field_ref[0, :, lanes], field_ref[1, :, lanes]], axis=0)
        out_ref[k] = joined(product(rows, weight_ref[k].reshape(128, 128)))
    finish(copies[3:])


def entries(row, count):
    return [row[0, k].astype(jnp.int32) for k in range(count)]


def slots(row, count, back_ref):
    places = entries(row, count)
    lane = lax.broadcasted_iota(jnp.int32, back_ref.shape, 1)
    back = jnp.zeros(back_ref.shape, jnp.int32)
    for k, place in enumerate(places):
        back = jnp.where(lane == place, k, back)
    back_ref[...] = back
    return places


def put_row(packed_ref, row):
    blocks = row.shape[1]
    packed_ref[blocks, 0:8, 0:blocks] = jnp.broadcast_to(row.astype(F32), (8, blocks))


def packed_row(packed_ref, blocks):
    return entries(packed_ref[packed_ref.shape[0] - 1, 0:8, 0:blocks], blocks)


def prepare_block(k, place, weight_ref, own_out, other_out, packed_ref=None):
    own_half, other_half = halves(weight_ref[k].reshape(128, 128))
    own_out[k] = filled(own_half)
    other_out[place] = filled(other_half)
    if packed_ref is not None:
        packed_ref[k] = other_half


def start_level(level, own_ref, weight_ref, roster_ref, ready_out, other_out, back_ref):
    for k, place in enumerate(slots(roster_ref[level], own_ref.shape[0], back_ref)):
        own_half, other_half = halves(weight_ref[k].reshape(128, 128))
        other_out[place] = filled(other_half)
        ready_out[place] = times(own_ref[k], filled(own_half))


def first_kernel(own_ref, weight_0, roster_ref, coupling_hbm, *refs):
    ready_out, other_out, back_ref, own_4, other_4, packed_a, packed_b, weight_1, weight_2, weight_4, sems = refs
    blocks = own_ref.shape[0]
    half = packed_b.shape[0]
    copies = started([(coupling_hbm.at[n], out) for n, out in ((4, weight_4), (1, weight_1), (2, weight_2))], sems)
    start_level(0, own_ref, weight_0, roster_ref, ready_out, other_out, back_ref)
    packed_a[half, 0:8, 0:blocks] = jnp.broadcast_to(roster_ref[4].astype(F32), (8, blocks))
    copies[0].wait()
    for k in range(blocks):
        own_half, other_half = halves(weight_4[k].reshape(128, 128))
        own_4[k] = filled(own_half)
        other_4[k] = filled(other_half)
        if k < half:
            packed_a[k] = other_half
        else:
            packed_b[k - half] = other_half
    finish(copies[1:])


def ahead_kernel(level, own_ref, weight_ref, roster_ref, weight_2, coupling_hbm, *refs):
    ready_out, other_out, back_ref, own_2, other_2, back_2, weight_3, weight_6, sems = refs
    copies = started([(coupling_hbm.at[3], weight_3), (coupling_hbm.at[6], weight_6)], sems)
    start_level(level, own_ref, weight_ref, roster_ref, ready_out, other_out, back_ref)
    for k, place in enumerate(slots(roster_ref[level + 1], own_ref.shape[0], back_2)):
        prepare_block(k, place, weight_2, own_2, other_2)
    finish(copies)


def sorted_kernel(level, weight_ref, roster_ref, after_ref, own_out, other_out, back_ref):
    for k, place in enumerate(slots(roster_ref[level], own_out.shape[0], back_ref)):
        prepare_block(k, place, weight_ref, own_out, other_out)


def packed_kernel(level, weight_ref, roster_ref, after_ref, own_out, other_out, packed_ref):
    put_row(packed_ref, roster_ref[level])
    for k in range(own_out.shape[0]):
        prepare_block(k, k, weight_ref, own_out, other_out, packed_ref)


def fetch_kernel(levels, coupling_ref, after_ref, *outs):
    for n, level in enumerate(levels):
        for k in range(coupling_ref.shape[1]):
            prepare_block(k, k, coupling_ref.at[level], outs[2 * n], outs[2 * n + 1])


def unpack_kernel(packed_ref, *rest):
    out_ref = rest[-1]
    for k in range(out_ref.shape[0]):
        half = packed_ref.shape[0] - 1
        out_ref[k] = filled(packed_ref[k] if k < half else rest[0][k - half])


def spread_kernel(weight_ref, after_ref, out_ref):
    for k in range(out_ref.shape[0]):
        out_ref[k] = jnp.concatenate(split(weight_ref[k].reshape(128, 128)), axis=0)


def own_kernel(own_ref, wide_ref, *rest):
    out_ref = rest[-1]
    for k in range(out_ref.shape[0]):
        out_ref[k] = times(own_ref[k], wide_ref[k])


def own_sorted_kernel(level, own_ref, wide_ref, roster_ref, out_ref):
    for k, place in enumerate(entries(roster_ref[level], out_ref.shape[0])):
        out_ref[place] = times(own_ref[k], wide_ref[k])


def level_kernel(back_ref, other_ref, wide_ref, ready_ref, *rest):
    out_ref = rest[-1]
    for place, k in enumerate(entries(back_ref[0:1, :], out_ref.shape[0])):
        out_ref[k] = ready_ref[place] + times(other_ref[place], wide_ref[place])


def plain_kernel(level, roster_ref, other_ref, wide_ref, ready_ref, *rest):
    out_ref = rest[-1]
    for k, place in enumerate(entries(roster_ref[level], out_ref.shape[0])):
        out_ref[k] = ready_ref[k] + times(other_ref[place], wide_ref[k])


def side_kernel(level, roster_ref, packed_ref, corner_ref, away_ref, beside_ref, wide_ref, out_ref, there_ref):
    blocks = out_ref.shape[0]
    for k, place in enumerate(packed_row(packed_ref, out_ref.shape[0])):
        there_ref[k] = beside_ref[k] + times(corner_ref[place], away_ref[k])
    for k, place in enumerate(entries(roster_ref[level], blocks)):
        out_ref[k] = times(there_ref[place], wide_ref[k])


def double_kernel(level, roster_ref, other_ref, wide_ref, ready_ref, next_ref, side_ref, *rest):
    out_ref, here_ref = rest[-2:]
    for k, place in enumerate(entries(roster_ref[level], out_ref.shape[0])):
        here_ref[k] = ready_ref[k] + times(other_ref[place], wide_ref[k])
    for k in range(out_ref.shape[0]):
        out_ref[k] = side_ref[k] + times(here_ref[k], next_ref[k])


def corner_kernel(packed_ref, other_ref, wide_ref, out_ref):
    for k, place in enumerate(packed_row(packed_ref, out_ref.shape[0])):
        out_ref[k] = times(other_ref[place], wide_ref[k])


def last_kernel(level, roster_ref, beside_ref, corner_ref, wide_ref, ready_ref, expand_ref, *rest):
    near_refs, (out_hbm, out_ref, sems) = rest[:-3], rest[-3:]
    blocks = beside_ref.shape[0]
    copies = []
    for k, place in enumerate(entries(roster_ref[level], blocks)):
        coeffs = ready_ref[k] + times(beside_ref[place] + corner_ref[place], wide_ref[k])
        signed = jnp.where(lane_low(coeffs.shape), coeffs, -coeffs)
        turned = pltpu.roll(coeffs, 64, axis=1)
        far = times(jnp.concatenate([signed, turned], axis=0), expand_ref[k])
        which = [n for n, (begin, count) in enumerate(NEAR_PARTS) if begin <= k < begin + count][0]
        total = far + near_refs[which][k - NEAR_PARTS[which][0]]
        half = total.shape[0] // 2
        lanes = pl.ds(128 * k, 128)
        out_ref[0, :, lanes] = total[:half]
        out_ref[1, :, lanes] = total[half:]
        if k % 4 == 3:
            part = pl.ds(128 * (k - 3), 512)
            copy = pltpu.make_async_copy(out_ref.at[:, :, part], out_hbm.at[:, :, part], sems.at[k // 4])
            copy.start()
            copies.append(copy)
    finish(copies)


def near_kernel(first, owner_ref, place_ref, valid_ref, pick_ref, own_ref, core_ref, far_ref, both_ref, weight_ref, *rest):
    out_ref = rest[-1]
    me = lax.axis_index("sub")
    for n in range(out_ref.shape[0]):
        k = first + n
        total = None
        for t in range(weight_ref.shape[1]):
            owner = owner_ref[t, k]
            leaf = pick_ref[owner, place_ref[t, k]]
            lanes = pl.ds(pl.multiple_of(leaf * 128, 128), 128)
            which = owner ^ me
            parts = []
            for d in range(2):
                low = jnp.where(which == 1, core_ref[d, :, lanes], own_ref[d, :, lanes])
                high = jnp.where(which == 3, both_ref[d, :, lanes], far_ref[d, :, lanes])
                parts.append(jnp.where(which >= 2, high, low))
            rows = jnp.concatenate(parts, axis=0) * valid_ref[t, k].astype(F32)
            result = product(rows, weight_ref[k, t].reshape(256, 128))
            half = result.shape[0] // 2
            term = jnp.concatenate(
                [result[:half, :128] - result[half:, 128:], result[half:, :128] + result[:half, 128:]], axis=0
            )
            total = term if total is None else total + term
        out_ref[n] = total


def spec(space):
    return pl.BlockSpec(memory_space=space)


def call(kernel, out, spaces, out_spaces=VMEM, scratch=(), flops=2_000_000):
    single = not isinstance(out_spaces, (list, tuple))
    return pl.pallas_call(
        kernel,
        out_shape=out,
        in_specs=[spec(space) for space in spaces],
        out_specs=spec(out_spaces) if single else [spec(space) for space in out_spaces],
        scratch_shapes=list(scratch),
        compiler_params=pltpu.CompilerParams(vmem_limit_bytes=8 << 20),
        cost_estimate=pl.CostEstimate(flops=flops, bytes_accessed=1 << 20, transcendentals=0),
    )


def in_hbm(*arrays):
    return [pltpu.with_memory_space_constraint(array, HBM) for array in arrays]


def flipped(value, leaf_mask, sub_mask):
    sub_count = lax.axis_size("sub")
    mask = leaf_mask * sub_count + sub_mask
    pairs = [(source, source ^ mask) for source in range(lax.axis_size("leaf") * sub_count)]
    return lax.ppermute(value, ("leaf", "sub"), pairs)


def tied(value, after):
    return lax.optimization_barrier((value, after))[0]


def on_device(
    field_in,
    compress,
    coupling,
    roster,
    expand,
    nearfield_dense_blocks,
    slot_owner_index,
    slot_source_position,
    slot_valid_mask,
    near_pick,
):
    blocks = compress.shape[0]
    rhs = field_in.shape[1]
    top = lax.axis_size("leaf") // 2
    pick = near_pick[0]
    indices = (slot_owner_index.T, slot_source_position.T, slot_valid_mask.T, pick)
    state = VMEM((blocks, rhs, 128), F32)
    wide = VMEM((blocks, 256, 128), BF)
    back = VMEM((8, 128), jnp.int32)
    packed = VMEM((blocks + 1, 64, 128), F32)
    level_weights = VMEM(coupling.shape[1:], F32)
    (coupling_hbm, _, roster_hbm) = in_hbm(coupling, field_in, roster)
    field = pltpu.with_memory_space_constraint(field_in, VMEM)
    dense = pltpu.with_memory_space_constraint(nearfield_dense_blocks, VMEM)
    expanding = pltpu.with_memory_space_constraint(expand, VMEM)

    def run(kernel, outs, inputs, after=(), scratch=(), hbm=()):
        spaces = [HBM if n in hbm else VMEM for n in range(len(inputs))] + [ANY] * len(after)
        several = isinstance(outs, list)
        return call(kernel, outs, spaces, [VMEM] * len(outs) if several else VMEM, scratch)(*inputs, *after)

    def near_piece(number, after):
        begin, count = NEAR_PARTS[number]
        return call(
            functools.partial(near_kernel, begin), VMEM((count, 2 * rhs, 128), F32), [SMEM] * 4 + [VMEM] * 5 + [ANY]
        )(*indices, field, core, far, both, dense, after)

    part = functools.partial
    coeffs, weight_0, names = run(
        compress_kernel,
        [state, level_weights, VMEM(roster.shape, jnp.int32)],
        [*in_hbm(field_in, compress), coupling_hbm, roster_hbm],
        scratch=[VMEM(field_in.shape, F32), VMEM(compress.shape, F32), DMA((5,))],
        hbm=(0, 1, 2, 3),
    )

    other = flipped(coeffs, top, 0)
    half = blocks // 2
    ready, wide_0, back_0, own_4, wide_4, packed_4, packed_more, weight_1, weight_2 = run(
        first_kernel,
        [
            state,
            wide,
            back,
            wide,
            wide,
            VMEM((half + 1, 64, 128), F32),
            VMEM((blocks - half, 64, 128), F32),
            level_weights,
            level_weights,
        ],
        [coeffs, weight_0, names, coupling_hbm],
        scratch=[level_weights, DMA((3,))],
        hbm=(3,),
    )
    away_4 = flipped(packed_4, top // 4, 0)
    coeffs = run(level_kernel, state, [back_0, other, wide_0, ready])

    other = flipped(coeffs, top // 2, 0)
    ready, wide_1, back_1, own_2, wide_2, back_2, weight_3, weight_6 = run(
        part(ahead_kernel, 1),
        [state, wide, back, wide, wide, back, level_weights, level_weights],
        [coeffs, weight_1, names, weight_2, coupling_hbm],
        scratch=[DMA((2,))],
        hbm=(4,),
    )
    own_3, wide_3, back_3 = run(part(sorted_kernel, 3), [wide, wide, back], [weight_3, names], [coeffs])
    own_6, wide_6, packed_6 = run(part(packed_kernel, 6), [wide, wide, packed], [weight_6, names], [coeffs])
    coeffs = run(level_kernel, state, [back_1, other, wide_1, ready], [own_3, own_6])

    other = flipped(coeffs, top // 4, 0)
    away_more = flipped(tied(packed_more, coeffs), top // 4, 0)
    away_6 = flipped(tied(packed_6, coeffs), top, 0)
    ready = run(part(own_sorted_kernel, 2), state, [coeffs, own_2, names])
    coeffs = run(level_kernel, state, [back_2, other, wide_2, ready])

    other = flipped(coeffs, 0, 1)
    ready = run(part(own_sorted_kernel, 3), state, [coeffs, own_3, names])
    coeffs = run(level_kernel, state, [back_3, other, wide_3, ready])

    corner = flipped(coeffs, top // 4, 2)
    ready = run(own_kernel, state, [coeffs, own_4])
    beside = flipped(ready, top // 4, 0)
    other = flipped(coeffs, 0, 2)
    own_5, wide_5, own_7, wide_7 = run(
        part(fetch_kernel, (5, 7)), [wide] * 4, [pltpu.with_memory_space_constraint(coupling, VMEM)], [coeffs]
    )
    far = flipped(tied(field_in, coeffs), 0, 2)
    away = run(unpack_kernel, wide, [away_4, away_more], [coeffs])
    side = run(part(side_kernel, 5), state, [names, away_4, corner, away, beside, wide_5], scratch=[state])
    coeffs = run(part(double_kernel, 4), state, [names, other, wide_4, ready, own_5, side], [own_7], scratch=[state])

    other = flipped(coeffs, top // 2, 0)
    ready = run(own_kernel, state, [coeffs, own_6])
    corner = flipped(coeffs, top // 2 + top, 0)
    beside = flipped(ready, top, 0)
    last = run(spread_kernel, wide, [expanding], [coeffs])
    away = run(unpack_kernel, wide, [away_6], [coeffs])
    core = flipped(tied(field_in, coeffs), 0, 1)
    both = flipped(tied(far, coeffs), 0, 1)
    here = run(part(plain_kernel, 6), state, [names, other, wide_6, ready], [last])
    ready = run(own_kernel, state, [here, own_7], [away])
    pieces = [near_piece(n, ready) for n in range(len(NEAR_PARTS))]
    corner = run(corner_kernel, state, [away_6, corner, away])
    return call(
        part(last_kernel, 7),
        jax.ShapeDtypeStruct(field_in.shape, F32),
        [VMEM] * (6 + len(pieces)),
        HBM,
        [VMEM(field_in.shape, F32), DMA((3,))],
    )(names, beside, corner, wide_7, ready, last, *pieces)


def solution(mesh):
    return jax.shard_map(
        on_device,
        mesh=mesh,
        in_specs=(
            P(None, None, ("leaf", "sub")),
            P(("leaf", "sub"), None, None, None),
            P(None, ("leaf", "sub"), None, None, None),
            P(None, ("leaf", "sub"), None),
            P(("leaf", "sub"), None, None, None),
            P(("leaf", "sub"), None, None, None, None),
            P(("leaf", "sub"), None),
            P(("leaf", "sub"), None),
            P(("leaf", "sub"), None),
            P(("leaf", "sub"), None, None),
        ),
        out_specs=P(None, None, ("leaf", "sub")),
        check_vma=False,
    )
```

```python
import functools

import jax
import jax.numpy as jnp
from jax import lax
from jax.experimental import pallas as pl
from jax.experimental.pallas import tpu as pltpu
from jax.sharding import PartitionSpec as P


VMEM = pltpu.VMEM
SMEM = pltpu.SMEM
ANY = pl.ANY
HBM = pltpu.HBM
DMA = pltpu.SemaphoreType.DMA
BF = jnp.bfloat16
F32 = jnp.float32
NT = (((1,), (1,)), ((), ()))
NN = (((1,), (0,)), ((), ()))
NEAR_PARTS = ((0, 4), (4, 8))


def split(value):
    high = value.astype(BF)
    return high, (value - high.astype(F32)).astype(BF)


def widened(rows):
    high, low = split(rows)
    return jnp.concatenate(
        [
            jnp.concatenate([high, high], axis=1),
            jnp.concatenate([low, jnp.zeros_like(low)], axis=1),
        ],
        axis=0,
    )


def folded(result):
    count = result.shape[0] // 2
    return result[:count] + result[count:]


def product(rows, weights):
    wide = jnp.concatenate(split(weights), axis=1)
    return folded(lax.dot_general(widened(rows), wide, NT, preferred_element_type=F32))


def times(rows, wide):
    return folded(lax.dot_general(widened(rows), wide, NN, preferred_element_type=F32))


def lane_low(shape):
    return lax.broadcasted_iota(jnp.int32, shape, 1) < 64


def joined(result):
    rhs = result.shape[0] // 2
    turned = pltpu.roll(result[rhs:], 64, axis=1)
    return result[:rhs] + jnp.where(lane_low(turned.shape), -turned, turned)


def filled(upper):
    turned = pltpu.roll(upper, 64, axis=1)
    lower = jnp.where(lane_low(turned.shape), -turned, turned)
    return jnp.concatenate(split(jnp.concatenate([upper, lower], axis=0)), axis=0)


def halves(block):
    flat = block.T
    return flat[:64], flat[64:]


def started(pairs, sems):
    copies = [pltpu.make_async_copy(source, out, sems.at[n]) for n, (source, out) in enumerate(pairs)]
    for copy in copies:
        copy.start()
    return copies


def finish(copies):
    for copy in copies:
        copy.wait()


def compress_kernel(field_hbm, weight_hbm, coupling_hbm, roster_hbm, out_ref, next_ref, roster_ref, field_ref, weight_ref, sems):
    blocks = out_ref.shape[0]
    half = blocks // 2
    parts = [pl.ds(0, half), pl.ds(half, blocks - half)]
    copies = started(
        [(field_hbm, field_ref)]
        + [(weight_hbm.at[part], weight_ref.at[part]) for part in parts]
        + [(roster_hbm, roster_ref), (coupling_hbm.at[0], next_ref)],
        sems,
    )
    copies[0].wait()
    for k in range(blocks):
        if k % half == 0:
            copies[1 + k // half].wait()
        lanes = pl.ds(128 * k, 128)
        rows = jnp.concatenate([field_ref[0, :, lanes], field_ref[1, :, lanes]], axis=0)
        out_ref[k] = joined(product(rows, weight_ref[k].reshape(128, 128)))
    finish(copies[3:])


def entries(row, count):
    return [row[0, k].astype(jnp.int32) for k in range(count)]


def slots(row, count, back_ref):
    places = entries(row, count)
    lane = lax.broadcasted_iota(jnp.int32, back_ref.shape, 1)
    back = jnp.zeros(back_ref.shape, jnp.int32)
    for k, place in enumerate(places):
        back = jnp.where(lane == place, k, back)
    back_ref[...] = back
    return places


def put_row(packed_ref, row):
    blocks = row.shape[1]
    packed_ref[blocks, 0:8, 0:blocks] = jnp.broadcast_to(row.astype(F32), (8, blocks))


def packed_row(packed_ref, blocks):
    return entries(packed_ref[packed_ref.shape[0] - 1, 0:8, 0:blocks], blocks)


def prepare_block(k, place, weight_ref, own_out, other_out, packed_ref=None):
    own_half, other_half = halves(weight_ref[k].reshape(128, 128))
    own_out[k] = filled(own_half)
    other_out[place] = filled(other_half)
    if packed_ref is not None:
        packed_ref[k] = other_half


def start_level(level, own_ref, weight_ref, roster_ref, ready_out, other_out, back_ref):
    for k, place in enumerate(slots(roster_ref[level], own_ref.shape[0], back_ref)):
        own_half, other_half = halves(weight_ref[k].reshape(128, 128))
        other_out[place] = filled(other_half)
        ready_out[place] = times(own_ref[k], filled(own_half))


def first_kernel(own_ref, weight_0, roster_ref, coupling_hbm, *refs):
    ready_out, other_out, back_ref, weight_1, weight_2, sems = refs
    copies = started([(coupling_hbm.at[n], out) for n, out in ((1, weight_1), (2, weight_2))], sems)
    start_level(0, own_ref, weight_0, roster_ref, ready_out, other_out, back_ref)
    finish(copies)


def middle_kernel(level, own_ref, coupling_ref, roster_ref, *outs):
    start_level(level, own_ref, coupling_ref.at[level], roster_ref, *outs)


def ahead_kernel(level, own_ref, weight_ref, roster_ref, weight_2, coupling_hbm, *refs):
    ready_out, other_out, back_ref, own_2, other_2, back_2, weight_3, weight_6, sems = refs
    copies = started([(coupling_hbm.at[3], weight_3), (coupling_hbm.at[6], weight_6)], sems)
    start_level(level, own_ref, weight_ref, roster_ref, ready_out, other_out, back_ref)
    for k, place in enumerate(slots(roster_ref[level + 1], own_ref.shape[0], back_2)):
        prepare_block(k, place, weight_2, own_2, other_2)
    finish(copies)


def sorted_kernel(level, weight_ref, roster_ref, after_ref, own_out, other_out, back_ref):
    for k, place in enumerate(slots(roster_ref[level], own_out.shape[0], back_ref)):
        prepare_block(k, place, weight_ref, own_out, other_out)


def packed_kernel(level, weight_ref, roster_ref, after_ref, own_out, other_out, packed_ref):
    put_row(packed_ref, roster_ref[level])
    for k in range(own_out.shape[0]):
        prepare_block(k, k, weight_ref, own_out, other_out, packed_ref)


def fetch_kernel(coupling_ref, roster_ref, after_ref, own_5, other_5, back_5, own_7, other_7):
    for k, place in enumerate(slots(roster_ref[5], coupling_ref.shape[1], back_5)):
        prepare_block(k, place, coupling_ref.at[5], own_5, other_5)
    for k in range(coupling_ref.shape[1]):
        prepare_block(k, k, coupling_ref.at[7], own_7, other_7)


def unpack_kernel(packed_ref, after_ref, out_ref):
    for k in range(out_ref.shape[0]):
        out_ref[k] = filled(packed_ref[k])


def spread_kernel(weight_ref, after_ref, out_ref):
    for k in range(out_ref.shape[0]):
        out_ref[k] = jnp.concatenate(split(weight_ref[k].reshape(128, 128)), axis=0)


def own_kernel(own_ref, wide_ref, *rest):
    out_ref = rest[-1]
    for k in range(out_ref.shape[0]):
        out_ref[k] = times(own_ref[k], wide_ref[k])


def own_sorted_kernel(level, own_ref, wide_ref, roster_ref, out_ref):
    for k, place in enumerate(entries(roster_ref[level], out_ref.shape[0])):
        out_ref[place] = times(own_ref[k], wide_ref[k])


def level_kernel(back_ref, other_ref, wide_ref, ready_ref, *rest):
    out_ref = rest[-1]
    for place, k in enumerate(entries(back_ref[0:1, :], out_ref.shape[0])):
        out_ref[k] = ready_ref[place] + times(other_ref[place], wide_ref[place])


def plain_kernel(level, roster_ref, other_ref, wide_ref, ready_ref, *rest):
    out_ref = rest[-1]
    for k, place in enumerate(entries(roster_ref[level], out_ref.shape[0])):
        out_ref[k] = ready_ref[k] + times(other_ref[place], wide_ref[k])


def corner_kernel(packed_ref, other_ref, wide_ref, out_ref):
    for k, place in enumerate(packed_row(packed_ref, out_ref.shape[0])):
        out_ref[k] = times(other_ref[place], wide_ref[k])


def last_kernel(level, roster_ref, beside_ref, corner_ref, wide_ref, ready_ref, expand_ref, *rest):
    near_refs, (out_hbm, out_ref, sems) = rest[:-3], rest[-3:]
    blocks = beside_ref.shape[0]
    copies = []
    for k, place in enumerate(entries(roster_ref[level], blocks)):
        coeffs = ready_ref[k] + times(beside_ref[place] + corner_ref[place], wide_ref[k])
        signed = jnp.where(lane_low(coeffs.shape), coeffs, -coeffs)
        turned = pltpu.roll(coeffs, 64, axis=1)
        far = times(jnp.concatenate([signed, turned], axis=0), expand_ref[k])
        which = [n for n, (begin, count) in enumerate(NEAR_PARTS) if begin <= k < begin + count][0]
        total = far + near_refs[which][k - NEAR_PARTS[which][0]]
        half = total.shape[0] // 2
        lanes = pl.ds(128 * k, 128)
        out_ref[0, :, lanes] = total[:half]
        out_ref[1, :, lanes] = total[half:]
        if k % 4 == 3:
            part = pl.ds(128 * (k - 3), 512)
            copy = pltpu.make_async_copy(out_ref.at[:, :, part], out_hbm.at[:, :, part], sems.at[k // 4])
            copy.start()
            copies.append(copy)
    finish(copies)


def near_kernel(first, owner_ref, place_ref, valid_ref, pick_ref, own_ref, core_ref, far_ref, both_ref, weight_ref, *rest):
    out_ref = rest[-1]
    me = lax.axis_index("sub")
    for n in range(out_ref.shape[0]):
        k = first + n
        total = None
        for t in range(weight_ref.shape[1]):
            owner = owner_ref[t, k]
            leaf = pick_ref[owner, place_ref[t, k]]
            lanes = pl.ds(pl.multiple_of(leaf * 128, 128), 128)
            which = owner ^ me
            parts = []
            for d in range(2):
                low = jnp.where(which == 1, core_ref[d, :, lanes], own_ref[d, :, lanes])
                high = jnp.where(which == 3, both_ref[d, :, lanes], far_ref[d, :, lanes])
                parts.append(jnp.where(which >= 2, high, low))
            rows = jnp.concatenate(parts, axis=0) * valid_ref[t, k].astype(F32)
            result = product(rows, weight_ref[k, t].reshape(256, 128))
            half = result.shape[0] // 2
            term = jnp.concatenate(
                [result[:half, :128] - result[half:, 128:], result[half:, :128] + result[:half, 128:]], axis=0
            )
            total = term if total is None else total + term
        out_ref[n] = total


def spec(space):
    return pl.BlockSpec(memory_space=space)


def call(kernel, out, spaces, out_spaces=VMEM, scratch=(), flops=2_000_000):
    single = not isinstance(out_spaces, (list, tuple))
    return pl.pallas_call(
        kernel,
        out_shape=out,
        in_specs=[spec(space) for space in spaces],
        out_specs=spec(out_spaces) if single else [spec(space) for space in out_spaces],
        scratch_shapes=list(scratch),
        compiler_params=pltpu.CompilerParams(vmem_limit_bytes=8 << 20),
        cost_estimate=pl.CostEstimate(flops=flops, bytes_accessed=1 << 20, transcendentals=0),
    )


def in_hbm(*arrays):
    return [pltpu.with_memory_space_constraint(array, HBM) for array in arrays]


def flipped(value, leaf_mask, sub_mask):
    sub_count = lax.axis_size("sub")
    mask = leaf_mask * sub_count + sub_mask
    pairs = [(source, source ^ mask) for source in range(lax.axis_size("leaf") * sub_count)]
    return lax.ppermute(value, ("leaf", "sub"), pairs)


def tied(value, after):
    return lax.optimization_barrier((value, after))[0]


def on_device(
    field_in,
    compress,
    coupling,
    roster,
    expand,
    nearfield_dense_blocks,
    slot_owner_index,
    slot_source_position,
    slot_valid_mask,
    near_pick,
):
    blocks = compress.shape[0]
    rhs = field_in.shape[1]
    top = lax.axis_size("leaf") // 2
    pick = near_pick[0]
    indices = (slot_owner_index.T, slot_source_position.T, slot_valid_mask.T, pick)
    state = VMEM((blocks, rhs, 128), F32)
    wide = VMEM((blocks, 256, 128), BF)
    back = VMEM((8, 128), jnp.int32)
    packed = VMEM((blocks + 1, 64, 128), F32)
    level_weights = VMEM(coupling.shape[1:], F32)
    (coupling_hbm, _, roster_hbm) = in_hbm(coupling, field_in, roster)
    field = pltpu.with_memory_space_constraint(field_in, VMEM)
    dense = pltpu.with_memory_space_constraint(nearfield_dense_blocks, VMEM)
    expanding = pltpu.with_memory_space_constraint(expand, VMEM)

    def run(kernel, outs, inputs, after=(), scratch=(), hbm=()):
        spaces = [HBM if n in hbm else VMEM for n in range(len(inputs))] + [ANY] * len(after)
        several = isinstance(outs, list)
        return call(kernel, outs, spaces, [VMEM] * len(outs) if several else VMEM, scratch)(*inputs, *after)

    def near_piece(number, after):
        begin, count = NEAR_PARTS[number]
        return call(
            functools.partial(near_kernel, begin), VMEM((count, 2 * rhs, 128), F32), [SMEM] * 4 + [VMEM] * 5 + [ANY]
        )(*indices, field, core, far, both, dense, after)

    part = functools.partial
    coeffs, weight_0, names = run(
        compress_kernel,
        [state, level_weights, VMEM(roster.shape, jnp.int32)],
        [*in_hbm(field_in, compress), coupling_hbm, roster_hbm],
        scratch=[VMEM(field_in.shape, F32), VMEM(compress.shape, F32), DMA((5,))],
        hbm=(0, 1, 2, 3),
    )

    other = flipped(coeffs, top, 0)
    far = flipped(tied(field_in, coeffs), 0, 2)
    ready, wide_0, back_0, weight_1, weight_2 = run(
        first_kernel,
        [state, wide, back, level_weights, level_weights],
        [coeffs, weight_0, names, coupling_hbm],
        scratch=[DMA((2,))],
        hbm=(3,),
    )
    coeffs = run(level_kernel, state, [back_0, other, wide_0, ready])

    other = flipped(coeffs, top // 2, 0)
    ready, wide_1, back_1, own_2, wide_2, back_2, weight_3, weight_6 = run(
        part(ahead_kernel, 1),
        [state, wide, back, wide, wide, back, level_weights, level_weights],
        [coeffs, weight_1, names, weight_2, coupling_hbm],
        scratch=[DMA((2,))],
        hbm=(4,),
    )
    own_6, wide_6, packed_6 = run(part(packed_kernel, 6), [wide, wide, packed], [weight_6, names], [coeffs])
    coeffs = run(level_kernel, state, [back_1, other, wide_1, ready], [own_6])

    other = flipped(coeffs, top // 4, 0)
    away_6 = flipped(tied(packed_6, coeffs), top, 0)
    ready = run(part(own_sorted_kernel, 2), state, [coeffs, own_2, names])
    own_3, wide_3, back_3 = run(part(sorted_kernel, 3), [wide, wide, back], [weight_3, names], [coeffs])
    coeffs = run(level_kernel, state, [back_2, other, wide_2, ready], [own_3])

    other = flipped(coeffs, 0, 1)
    ready = run(part(own_sorted_kernel, 3), state, [coeffs, own_3, names])
    coeffs = run(level_kernel, state, [back_3, other, wide_3, ready])

    other = flipped(coeffs, 0, 2)
    core = flipped(tied(field_in, coeffs), 0, 1)
    both = flipped(tied(far, coeffs), 0, 1)
    everything = pltpu.with_memory_space_constraint(coupling, VMEM)
    ready, wide_4, back_4 = run(part(middle_kernel, 4), [state, wide, back], [coeffs, everything, names])
    own_5, wide_5, back_5, own_7, wide_7 = run(
        fetch_kernel, [wide, wide, back, wide, wide], [everything, names], [coeffs]
    )
    coeffs = run(level_kernel, state, [back_4, other, wide_4, ready], [own_7])

    other = flipped(coeffs, top // 4, 0)
    ready = run(part(own_sorted_kernel, 5), state, [coeffs, own_5, names])
    pieces = [near_piece(n, coeffs) for n in range(len(NEAR_PARTS))]
    coeffs = run(level_kernel, state, [back_5, other, wide_5, ready], pieces)

    other = flipped(coeffs, top // 2, 0)
    ready = run(own_kernel, state, [coeffs, own_6])
    corner = flipped(coeffs, top // 2 + top, 0)
    beside = flipped(ready, top, 0)
    last = run(spread_kernel, wide, [expanding], [coeffs])
    away = run(unpack_kernel, wide, [away_6], [coeffs])
    here = run(part(plain_kernel, 6), state, [names, other, wide_6, ready], [last])
    ready = run(own_kernel, state, [here, own_7], [away])
    corner = run(corner_kernel, state, [away_6, corner, away])
    return call(
        part(last_kernel, 7),
        jax.ShapeDtypeStruct(field_in.shape, F32),
        [VMEM] * (6 + len(pieces)),
        HBM,
        [VMEM(field_in.shape, F32), DMA((3,))],
    )(names, beside, corner, wide_7, ready, last, *pieces)


def solution(mesh):
    return jax.shard_map(
        on_device,
        mesh=mesh,
        in_specs=(
            P(None, None, ("leaf", "sub")),
            P(("leaf", "sub"), None, None, None),
            P(None, ("leaf", "sub"), None, None, None),
            P(None, ("leaf", "sub"), None),
            P(("leaf", "sub"), None, None, None),
            P(("leaf", "sub"), None, None, None, None),
            P(("leaf", "sub"), None),
            P(("leaf", "sub"), None),
            P(("leaf", "sub"), None),
            P(("leaf", "sub"), None, None),
        ),
        out_specs=P(None, None, ("leaf", "sub")),
        check_vma=False,
    )
```

```python
import functools

import jax
import jax.numpy as jnp
from jax import lax
from jax.experimental import pallas as pl
from jax.experimental.pallas import tpu as pltpu
from jax.sharding import PartitionSpec as P


VMEM = pltpu.VMEM
SMEM = pltpu.SMEM
ANY = pl.ANY
HBM = pltpu.HBM
DMA = pltpu.SemaphoreType.DMA
BF = jnp.bfloat16
F32 = jnp.float32
NT = (((1,), (1,)), ((), ()))
NN = (((1,), (0,)), ((), ()))
NEAR_PARTS = ((0, 4), (4, 8))


def split(value):
    high = value.astype(BF)
    return high, (value - high.astype(F32)).astype(BF)


def widened(rows):
    high, low = split(rows)
    return jnp.concatenate(
        [
            jnp.concatenate([high, high], axis=1),
            jnp.concatenate([low, jnp.zeros_like(low)], axis=1),
        ],
        axis=0,
    )


def folded(result):
    count = result.shape[0] // 2
    return result[:count] + result[count:]


def product(rows, weights):
    wide = jnp.concatenate(split(weights), axis=1)
    return folded(lax.dot_general(widened(rows), wide, NT, preferred_element_type=F32))


def times(rows, wide):
    return folded(lax.dot_general(widened(rows), wide, NN, preferred_element_type=F32))


def lane_low(shape):
    return lax.broadcasted_iota(jnp.int32, shape, 1) < 64


def joined(result):
    rhs = result.shape[0] // 2
    turned = pltpu.roll(result[rhs:], 64, axis=1)
    return result[:rhs] + jnp.where(lane_low(turned.shape), -turned, turned)


def filled(upper):
    turned = pltpu.roll(upper, 64, axis=1)
    lower = jnp.where(lane_low(turned.shape), -turned, turned)
    return jnp.concatenate(split(jnp.concatenate([upper, lower], axis=0)), axis=0)


def halves(block):
    flat = block.T
    return flat[:64], flat[64:]


def started(pairs, sems):
    copies = [pltpu.make_async_copy(source, out, sems.at[n]) for n, (source, out) in enumerate(pairs)]
    for copy in copies:
        copy.start()
    return copies


def finish(copies):
    for copy in copies:
        copy.wait()


def compress_kernel(field_hbm, weight_hbm, coupling_hbm, roster_hbm, out_ref, next_ref, roster_ref, field_ref, weight_ref, sems):
    blocks = out_ref.shape[0]
    half = blocks // 2
    parts = [pl.ds(0, half), pl.ds(half, blocks - half)]
    copies = started(
        [(field_hbm, field_ref)]
        + [(weight_hbm.at[part], weight_ref.at[part]) for part in parts]
        + [(roster_hbm, roster_ref), (coupling_hbm.at[4], next_ref)],
        sems,
    )
    copies[0].wait()
    for k in range(blocks):
        if k % half == 0:
            copies[1 + k // half].wait()
        lanes = pl.ds(128 * k, 128)
        rows = jnp.concatenate([field_ref[0, :, lanes], field_ref[1, :, lanes]], axis=0)
        out_ref[k] = joined(product(rows, weight_ref[k].reshape(128, 128)))
    finish(copies[3:])


def entries(row, count):
    return [row[0, k].astype(jnp.int32) for k in range(count)]


def slots(row, count, back_ref):
    places = entries(row, count)
    lane = lax.broadcasted_iota(jnp.int32, back_ref.shape, 1)
    back = jnp.zeros(back_ref.shape, jnp.int32)
    for k, place in enumerate(places):
        back = jnp.where(lane == place, k, back)
    back_ref[...] = back
    return places


def put_row(packed_ref, row):
    blocks = row.shape[1]
    packed_ref[blocks, 0:8, 0:blocks] = jnp.broadcast_to(row.astype(F32), (8, blocks))


def packed_row(packed_ref, blocks):
    return entries(packed_ref[packed_ref.shape[0] - 1, 0:8, 0:blocks], blocks)


def prepare_block(k, place, weight_ref, own_out, other_out, packed_ref=None):
    own_half, other_half = halves(weight_ref[k].reshape(128, 128))
    own_out[k] = filled(own_half)
    other_out[place] = filled(other_half)
    if packed_ref is not None:
        packed_ref[k] = other_half


def start_level(level, own_ref, weight_ref, roster_ref, ready_out, other_out, back_ref):
    for k, place in enumerate(slots(roster_ref[level], own_ref.shape[0], back_ref)):
        own_half, other_half = halves(weight_ref[k].reshape(128, 128))
        other_out[place] = filled(other_half)
        ready_out[place] = times(own_ref[k], filled(own_half))


def pack_kernel(level, weight_ref, roster_ref, out_ref):
    put_row(out_ref, roster_ref[level])
    for k in range(weight_ref.shape[0]):
        out_ref[k] = halves(weight_ref[k].reshape(128, 128))[1]


def first_kernel(own_ref, weight_4, roster_ref, coupling_hbm, *refs):
    ready_out, other_out, back_ref, own_4, other_4, weight_1, weight_2, weight_0, sems = refs
    copies = started([(coupling_hbm.at[n], out) for n, out in enumerate((weight_0, weight_1, weight_2))], sems)
    for k in range(own_ref.shape[0]):
        prepare_block(k, k, weight_4, own_4, other_4)
    copies[0].wait()
    start_level(0, own_ref, weight_0, roster_ref, ready_out, other_out, back_ref)
    finish(copies[1:])


def ahead_kernel(level, own_ref, weight_ref, roster_ref, weight_2, coupling_hbm, *refs):
    ready_out, other_out, back_ref, own_2, other_2, back_2, weight_3, weight_6, sems = refs
    copies = started([(coupling_hbm.at[3], weight_3), (coupling_hbm.at[6], weight_6)], sems)
    start_level(level, own_ref, weight_ref, roster_ref, ready_out, other_out, back_ref)
    for k, place in enumerate(slots(roster_ref[level + 1], own_ref.shape[0], back_2)):
        prepare_block(k, place, weight_2, own_2, other_2)
    finish(copies)


def sorted_kernel(level, weight_ref, roster_ref, after_ref, own_out, other_out, back_ref):
    for k, place in enumerate(slots(roster_ref[level], own_out.shape[0], back_ref)):
        prepare_block(k, place, weight_ref, own_out, other_out)


def packed_kernel(level, weight_ref, roster_ref, after_ref, own_out, other_out, packed_ref):
    put_row(packed_ref, roster_ref[level])
    for k in range(own_out.shape[0]):
        prepare_block(k, k, weight_ref, own_out, other_out, packed_ref)


def fetch_kernel(levels, coupling_ref, after_ref, *outs):
    for n, level in enumerate(levels):
        for k in range(coupling_ref.shape[1]):
            prepare_block(k, k, coupling_ref.at[level], outs[2 * n], outs[2 * n + 1])


def unpack_kernel(packed_ref, after_ref, out_ref):
    for k in range(out_ref.shape[0]):
        out_ref[k] = filled(packed_ref[k])


def spread_kernel(weight_ref, after_ref, out_ref):
    for k in range(out_ref.shape[0]):
        out_ref[k] = jnp.concatenate(split(weight_ref[k].reshape(128, 128)), axis=0)


def own_kernel(own_ref, wide_ref, *rest):
    out_ref = rest[-1]
    for k in range(out_ref.shape[0]):
        out_ref[k] = times(own_ref[k], wide_ref[k])


def own_sorted_kernel(level, own_ref, wide_ref, roster_ref, out_ref):
    for k, place in enumerate(entries(roster_ref[level], out_ref.shape[0])):
        out_ref[place] = times(own_ref[k], wide_ref[k])


def level_kernel(back_ref, other_ref, wide_ref, ready_ref, *rest):
    out_ref = rest[-1]
    for place, k in enumerate(entries(back_ref[0:1, :], out_ref.shape[0])):
        out_ref[k] = ready_ref[place] + times(other_ref[place], wide_ref[place])


def plain_kernel(level, roster_ref, other_ref, wide_ref, ready_ref, *rest):
    out_ref = rest[-1]
    for k, place in enumerate(entries(roster_ref[level], out_ref.shape[0])):
        out_ref[k] = ready_ref[k] + times(other_ref[place], wide_ref[k])


def side_kernel(level, roster_ref, packed_ref, corner_ref, away_ref, beside_ref, wide_ref, out_ref, there_ref):
    blocks = out_ref.shape[0]
    for k, place in enumerate(packed_row(packed_ref, out_ref.shape[0])):
        there_ref[k] = beside_ref[k] + times(corner_ref[place], away_ref[k])
    for k, place in enumerate(entries(roster_ref[level], blocks)):
        out_ref[k] = times(there_ref[place], wide_ref[k])


def double_kernel(level, roster_ref, other_ref, wide_ref, ready_ref, next_ref, side_ref, *rest):
    out_ref, here_ref = rest[-2:]
    for k, place in enumerate(entries(roster_ref[level], out_ref.shape[0])):
        here_ref[k] = ready_ref[k] + times(other_ref[place], wide_ref[k])
    for k in range(out_ref.shape[0]):
        out_ref[k] = side_ref[k] + times(here_ref[k], next_ref[k])


def corner_kernel(packed_ref, other_ref, wide_ref, out_ref):
    for k, place in enumerate(packed_row(packed_ref, out_ref.shape[0])):
        out_ref[k] = times(other_ref[place], wide_ref[k])


def last_kernel(level, roster_ref, beside_ref, corner_ref, wide_ref, ready_ref, expand_ref, *rest):
    near_refs, (out_hbm, out_ref, sems) = rest[:-3], rest[-3:]
    blocks = beside_ref.shape[0]
    copies = []
    for k, place in enumerate(entries(roster_ref[level], blocks)):
        coeffs = ready_ref[k] + times(beside_ref[place] + corner_ref[place], wide_ref[k])
        signed = jnp.where(lane_low(coeffs.shape), coeffs, -coeffs)
        turned = pltpu.roll(coeffs, 64, axis=1)
        far = times(jnp.concatenate([signed, turned], axis=0), expand_ref[k])
        which = [n for n, (begin, count) in enumerate(NEAR_PARTS) if begin <= k < begin + count][0]
        total = far + near_refs[which][k - NEAR_PARTS[which][0]]
        half = total.shape[0] // 2
        lanes = pl.ds(128 * k, 128)
        out_ref[0, :, lanes] = total[:half]
        out_ref[1, :, lanes] = total[half:]
        if k % 4 == 3:
            part = pl.ds(128 * (k - 3), 512)
            copy = pltpu.make_async_copy(out_ref.at[:, :, part], out_hbm.at[:, :, part], sems.at[k // 4])
            copy.start()
            copies.append(copy)
    finish(copies)


def near_kernel(first, owner_ref, place_ref, valid_ref, pick_ref, own_ref, core_ref, far_ref, both_ref, weight_ref, *rest):
    out_ref = rest[-1]
    me = lax.axis_index("sub")
    for n in range(out_ref.shape[0]):
        k = first + n
        total = None
        for t in range(weight_ref.shape[1]):
            owner = owner_ref[t, k]
            leaf = pick_ref[owner, place_ref[t, k]]
            lanes = pl.ds(pl.multiple_of(leaf * 128, 128), 128)
            which = owner ^ me
            parts = []
            for d in range(2):
                low = jnp.where(which == 1, core_ref[d, :, lanes], own_ref[d, :, lanes])
                high = jnp.where(which == 3, both_ref[d, :, lanes], far_ref[d, :, lanes])
                parts.append(jnp.where(which >= 2, high, low))
            rows = jnp.concatenate(parts, axis=0) * valid_ref[t, k].astype(F32)
            result = product(rows, weight_ref[k, t].reshape(256, 128))
            half = result.shape[0] // 2
            term = jnp.concatenate(
                [result[:half, :128] - result[half:, 128:], result[half:, :128] + result[:half, 128:]], axis=0
            )
            total = term if total is None else total + term
        out_ref[n] = total


def spec(space):
    return pl.BlockSpec(memory_space=space)


def call(kernel, out, spaces, out_spaces=VMEM, scratch=(), flops=2_000_000):
    single = not isinstance(out_spaces, (list, tuple))
    return pl.pallas_call(
        kernel,
        out_shape=out,
        in_specs=[spec(space) for space in spaces],
        out_specs=spec(out_spaces) if single else [spec(space) for space in out_spaces],
        scratch_shapes=list(scratch),
        compiler_params=pltpu.CompilerParams(vmem_limit_bytes=8 << 20),
        cost_estimate=pl.CostEstimate(flops=flops, bytes_accessed=1 << 20, transcendentals=0),
    )


def in_hbm(*arrays):
    return [pltpu.with_memory_space_constraint(array, HBM) for array in arrays]


def flipped(value, leaf_mask, sub_mask):
    sub_count = lax.axis_size("sub")
    mask = leaf_mask * sub_count + sub_mask
    pairs = [(source, source ^ mask) for source in range(lax.axis_size("leaf") * sub_count)]
    return lax.ppermute(value, ("leaf", "sub"), pairs)


def tied(value, after):
    return lax.optimization_barrier((value, after))[0]


def on_device(
    field_in,
    compress,
    coupling,
    roster,
    expand,
    nearfield_dense_blocks,
    slot_owner_index,
    slot_source_position,
    slot_valid_mask,
    near_pick,
):
    blocks = compress.shape[0]
    rhs = field_in.shape[1]
    top = lax.axis_size("leaf") // 2
    pick = near_pick[0]
    indices = (slot_owner_index.T, slot_source_position.T, slot_valid_mask.T, pick)
    state = VMEM((blocks, rhs, 128), F32)
    wide = VMEM((blocks, 256, 128), BF)
    back = VMEM((8, 128), jnp.int32)
    packed = VMEM((blocks + 1, 64, 128), F32)
    level_weights = VMEM(coupling.shape[1:], F32)
    (coupling_hbm, _, roster_hbm) = in_hbm(coupling, field_in, roster)
    field = pltpu.with_memory_space_constraint(field_in, VMEM)
    dense = pltpu.with_memory_space_constraint(nearfield_dense_blocks, VMEM)
    expanding = pltpu.with_memory_space_constraint(expand, VMEM)

    def run(kernel, outs, inputs, after=(), scratch=(), hbm=()):
        spaces = [HBM if n in hbm else VMEM for n in range(len(inputs))] + [ANY] * len(after)
        several = isinstance(outs, list)
        return call(kernel, outs, spaces, [VMEM] * len(outs) if several else VMEM, scratch)(*inputs, *after)

    def near_piece(number, after):
        begin, count = NEAR_PARTS[number]
        return call(
            functools.partial(near_kernel, begin), VMEM((count, 2 * rhs, 128), F32), [SMEM] * 4 + [VMEM] * 5 + [ANY]
        )(*indices, field, core, far, both, dense, after)

    part = functools.partial
    coeffs, weight_4, names = run(
        compress_kernel,
        [state, level_weights, VMEM(roster.shape, jnp.int32)],
        [*in_hbm(field_in, compress), coupling_hbm, roster_hbm],
        scratch=[VMEM(field_in.shape, F32), VMEM(compress.shape, F32), DMA((5,))],
        hbm=(0, 1, 2, 3),
    )

    other = flipped(coeffs, top, 0)
    packed_4 = run(part(pack_kernel, 4), packed, [weight_4, names])
    away_4 = flipped(packed_4, top // 4, 0)
    ready, wide_0, back_0, own_4, wide_4, weight_1, weight_2 = run(
        first_kernel,
        [state, wide, back, wide, wide, level_weights, level_weights],
        [coeffs, weight_4, names, coupling_hbm],
        scratch=[level_weights, DMA((3,))],
        hbm=(3,),
    )
    coeffs = run(level_kernel, state, [back_0, other, wide_0, ready])

    other = flipped(coeffs, top // 2, 0)
    ready, wide_1, back_1, own_2, wide_2, back_2, weight_3, weight_6 = run(
        part(ahead_kernel, 1),
        [state, wide, back, wide, wide, back, level_weights, level_weights],
        [coeffs, weight_1, names, weight_2, coupling_hbm],
        scratch=[DMA((2,))],
        hbm=(4,),
    )
    own_3, wide_3, back_3 = run(part(sorted_kernel, 3), [wide, wide, back], [weight_3, names], [coeffs])
    own_6, wide_6, packed_6 = run(part(packed_kernel, 6), [wide, wide, packed], [weight_6, names], [coeffs])
    coeffs = run(level_kernel, state, [back_1, other, wide_1, ready], [own_3, own_6])

    other = flipped(coeffs, top // 4, 0)
    far = flipped(tied(field_in, coeffs), 0, 2)
    away_6 = flipped(tied(packed_6, coeffs), top, 0)
    ready = run(part(own_sorted_kernel, 2), state, [coeffs, own_2, names])
    coeffs = run(level_kernel, state, [back_2, other, wide_2, ready])

    other = flipped(coeffs, 0, 1)
    ready = run(part(own_sorted_kernel, 3), state, [coeffs, own_3, names])
    coeffs = run(level_kernel, state, [back_3, other, wide_3, ready])

    corner = flipped(coeffs, top // 4, 2)
    ready = run(own_kernel, state, [coeffs, own_4])
    beside = flipped(ready, top // 4, 0)
    other = flipped(coeffs, 0, 2)
    own_5, wide_5, own_7, wide_7 = run(
        part(fetch_kernel, (5, 7)), [wide] * 4, [pltpu.with_memory_space_constraint(coupling, VMEM)], [coeffs]
    )
    core = flipped(tied(field_in, coeffs), 0, 1)
    both = flipped(tied(far, coeffs), 0, 1)
    away = run(unpack_kernel, wide, [away_4], [coeffs])
    side = run(part(side_kernel, 5), state, [names, away_4, corner, away, beside, wide_5], scratch=[state])
    coeffs = run(part(double_kernel, 4), state, [names, other, wide_4, ready, own_5, side], [own_7], scratch=[state])

    other = flipped(coeffs, top // 2, 0)
    ready = run(own_kernel, state, [coeffs, own_6])
    corner = flipped(coeffs, top // 2 + top, 0)
    beside = flipped(ready, top, 0)
    last = run(spread_kernel, wide, [expanding], [coeffs])
    away = run(unpack_kernel, wide, [away_6], [coeffs])
    pieces = [near_piece(0, coeffs)]
    here = run(part(plain_kernel, 6), state, [names, other, wide_6, ready], [last, pieces[0]])
    ready = run(own_kernel, state, [here, own_7], [away])
    pieces.append(near_piece(1, ready))
    corner = run(corner_kernel, state, [away_6, corner, away])
    return call(
        part(last_kernel, 7),
        jax.ShapeDtypeStruct(field_in.shape, F32),
        [VMEM] * (6 + len(pieces)),
        HBM,
        [VMEM(field_in.shape, F32), DMA((3,))],
    )(names, beside, corner, wide_7, ready, last, *pieces)


def solution(mesh):
    return jax.shard_map(
        on_device,
        mesh=mesh,
        in_specs=(
            P(None, None, ("leaf", "sub")),
            P(("leaf", "sub"), None, None, None),
            P(None, ("leaf", "sub"), None, None, None),
            P(None, ("leaf", "sub"), None),
            P(("leaf", "sub"), None, None, None),
            P(("leaf", "sub"), None, None, None, None),
            P(("leaf", "sub"), None),
            P(("leaf", "sub"), None),
            P(("leaf", "sub"), None),
            P(("leaf", "sub"), None, None),
        ),
        out_specs=P(None, None, ("leaf", "sub")),
        check_vma=False,
    )
```

```python
import functools

import jax
import jax.numpy as jnp
from jax import lax
from jax.experimental import pallas as pl
from jax.experimental.pallas import tpu as pltpu
from jax.sharding import PartitionSpec as P


VMEM = pltpu.VMEM
SMEM = pltpu.SMEM
ANY = pl.ANY
HBM = pltpu.HBM
DMA = pltpu.SemaphoreType.DMA
BF = jnp.bfloat16
F32 = jnp.float32
NT = (((1,), (1,)), ((), ()))
NN = (((1,), (0,)), ((), ()))
NEAR_PARTS = ((0, 4), (4, 8))


def split(value):
    high = value.astype(BF)
    return high, (value - high.astype(F32)).astype(BF)


def widened(rows):
    high, low = split(rows)
    return jnp.concatenate(
        [
            jnp.concatenate([high, high], axis=1),
            jnp.concatenate([low, jnp.zeros_like(low)], axis=1),
        ],
        axis=0,
    )


def folded(result):
    count = result.shape[0] // 2
    return result[:count] + result[count:]


def product(rows, weights):
    wide = jnp.concatenate(split(weights), axis=1)
    return folded(lax.dot_general(widened(rows), wide, NT, preferred_element_type=F32))


def times(rows, wide):
    return folded(lax.dot_general(widened(rows), wide, NN, preferred_element_type=F32))


def lane_low(shape):
    return lax.broadcasted_iota(jnp.int32, shape, 1) < 64


def joined(result):
    rhs = result.shape[0] // 2
    turned = pltpu.roll(result[rhs:], 64, axis=1)
    return result[:rhs] + jnp.where(lane_low(turned.shape), -turned, turned)


def filled(upper):
    turned = pltpu.roll(upper, 64, axis=1)
    lower = jnp.where(lane_low(turned.shape), -turned, turned)
    return jnp.concatenate(split(jnp.concatenate([upper, lower], axis=0)), axis=0)


def halves(block):
    flat = block.T
    return flat[:64], flat[64:]


def started(pairs, sems):
    copies = [pltpu.make_async_copy(source, out, sems.at[n]) for n, (source, out) in enumerate(pairs)]
    for copy in copies:
        copy.start()
    return copies


def finish(copies):
    for copy in copies:
        copy.wait()


def compress_kernel(field_hbm, weight_hbm, coupling_hbm, roster_hbm, out_ref, next_ref, roster_ref, field_ref, weight_ref, sems):
    blocks = out_ref.shape[0]
    half = blocks // 2
    parts = [pl.ds(0, half), pl.ds(half, blocks - half)]
    copies = started(
        [(field_hbm, field_ref)]
        + [(weight_hbm.at[part], weight_ref.at[part]) for part in parts]
        + [(roster_hbm, roster_ref), (coupling_hbm.at[4], next_ref)],
        sems,
    )
    copies[0].wait()
    for k in range(blocks):
        if k % half == 0:
            copies[1 + k // half].wait()
        lanes = pl.ds(128 * k, 128)
        rows = jnp.concatenate([field_ref[0, :, lanes], field_ref[1, :, lanes]], axis=0)
        out_ref[k] = joined(product(rows, weight_ref[k].reshape(128, 128)))
    finish(copies[3:])


def entries(row, count):
    return [row[0, k].astype(jnp.int32) for k in range(count)]


def slots(row, count, back_ref):
    places = entries(row, count)
    lane = lax.broadcasted_iota(jnp.int32, back_ref.shape, 1)
    back = jnp.zeros(back_ref.shape, jnp.int32)
    for k, place in enumerate(places):
        back = jnp.where(lane == place, k, back)
    back_ref[...] = back
    return places


def put_row(packed_ref, row):
    blocks = row.shape[1]
    packed_ref[blocks, 0:8, 0:blocks] = jnp.broadcast_to(row.astype(F32), (8, blocks))


def packed_row(packed_ref, blocks):
    return entries(packed_ref[packed_ref.shape[0] - 1, 0:8, 0:blocks], blocks)


def prepare_block(k, place, weight_ref, own_out, other_out, packed_ref=None):
    own_half, other_half = halves(weight_ref[k].reshape(128, 128))
    own_out[k] = filled(own_half)
    other_out[place] = filled(other_half)
    if packed_ref is not None:
        packed_ref[k] = other_half


def start_level(level, own_ref, weight_ref, roster_ref, ready_out, other_out, back_ref):
    for k, place in enumerate(slots(roster_ref[level], own_ref.shape[0], back_ref)):
        own_half, other_half = halves(weight_ref[k].reshape(128, 128))
        other_out[place] = filled(other_half)
        ready_out[place] = times(own_ref[k], filled(own_half))


def pack_kernel(level, weight_ref, roster_ref, out_ref):
    put_row(out_ref, roster_ref[level])
    for k in range(weight_ref.shape[0]):
        out_ref[k] = halves(weight_ref[k].reshape(128, 128))[1]


def first_kernel(own_ref, weight_4, roster_ref, coupling_hbm, *refs):
    ready_out, other_out, back_ref, own_4, other_4, *outs, weight_0, sems = refs
    pairs = zip((0, 1, 2, 6, 3), [weight_0] + outs)
    copies = started([(coupling_hbm.at[n], out) for n, out in pairs], sems)
    for k in range(own_ref.shape[0]):
        prepare_block(k, k, weight_4, own_4, other_4)
    copies[0].wait()
    start_level(0, own_ref, weight_0, roster_ref, ready_out, other_out, back_ref)
    finish(copies[1:])


def ahead_kernel(level, own_ref, weight_ref, roster_ref, weight_2, *refs):
    ready_out, other_out, back_ref, own_2, other_2, back_2 = refs
    start_level(level, own_ref, weight_ref, roster_ref, ready_out, other_out, back_ref)
    for k, place in enumerate(slots(roster_ref[level + 1], own_ref.shape[0], back_2)):
        prepare_block(k, place, weight_2, own_2, other_2)


def sorted_kernel(level, weight_ref, roster_ref, after_ref, own_out, other_out, back_ref):
    for k, place in enumerate(slots(roster_ref[level], own_out.shape[0], back_ref)):
        prepare_block(k, place, weight_ref, own_out, other_out)


def packed_kernel(level, weight_ref, roster_ref, after_ref, own_out, other_out, packed_ref):
    put_row(packed_ref, roster_ref[level])
    for k in range(own_out.shape[0]):
        prepare_block(k, k, weight_ref, own_out, other_out, packed_ref)


def fetch_kernel(levels, coupling_hbm, after_ref, *refs):
    count = len(levels)
    outs, weights, sems = refs[: 2 * count], refs[2 * count : -1], refs[-1]
    copies = started([(coupling_hbm.at[level], out) for level, out in zip(levels, weights)], sems)
    for n in range(count):
        copies[n].wait()
        for k in range(weights[n].shape[0]):
            prepare_block(k, k, weights[n], outs[2 * n], outs[2 * n + 1])


def unpack_kernel(packed_ref, after_ref, out_ref):
    for k in range(out_ref.shape[0]):
        out_ref[k] = filled(packed_ref[k])


def spread_kernel(weight_ref, after_ref, out_ref):
    for k in range(out_ref.shape[0]):
        out_ref[k] = jnp.concatenate(split(weight_ref[k].reshape(128, 128)), axis=0)


def own_kernel(own_ref, wide_ref, *rest):
    out_ref = rest[-1]
    for k in range(out_ref.shape[0]):
        out_ref[k] = times(own_ref[k], wide_ref[k])


def own_sorted_kernel(level, own_ref, wide_ref, roster_ref, out_ref):
    for k, place in enumerate(entries(roster_ref[level], out_ref.shape[0])):
        out_ref[place] = times(own_ref[k], wide_ref[k])


def level_kernel(back_ref, other_ref, wide_ref, ready_ref, *rest):
    out_ref = rest[-1]
    for place, k in enumerate(entries(back_ref[0:1, :], out_ref.shape[0])):
        out_ref[k] = ready_ref[place] + times(other_ref[place], wide_ref[place])


def plain_kernel(level, roster_ref, other_ref, wide_ref, ready_ref, *rest):
    out_ref = rest[-1]
    for k, place in enumerate(entries(roster_ref[level], out_ref.shape[0])):
        out_ref[k] = ready_ref[k] + times(other_ref[place], wide_ref[k])


def side_kernel(level, roster_ref, packed_ref, corner_ref, away_ref, beside_ref, wide_ref, out_ref, there_ref):
    blocks = out_ref.shape[0]
    for k, place in enumerate(packed_row(packed_ref, out_ref.shape[0])):
        there_ref[k] = beside_ref[k] + times(corner_ref[place], away_ref[k])
    for k, place in enumerate(entries(roster_ref[level], blocks)):
        out_ref[k] = times(there_ref[place], wide_ref[k])


def double_kernel(level, roster_ref, other_ref, wide_ref, ready_ref, next_ref, side_ref, *rest):
    out_ref, here_ref = rest[-2:]
    for k, place in enumerate(entries(roster_ref[level], out_ref.shape[0])):
        here_ref[k] = ready_ref[k] + times(other_ref[place], wide_ref[k])
    for k in range(out_ref.shape[0]):
        out_ref[k] = side_ref[k] + times(here_ref[k], next_ref[k])


def corner_kernel(packed_ref, other_ref, wide_ref, out_ref):
    for k, place in enumerate(packed_row(packed_ref, out_ref.shape[0])):
        out_ref[k] = times(other_ref[place], wide_ref[k])


def last_kernel(level, roster_ref, beside_ref, corner_ref, wide_ref, ready_ref, expand_ref, *rest):
    near_refs, (out_hbm, out_ref, sems) = rest[:-3], rest[-3:]
    blocks = beside_ref.shape[0]
    copies = []
    for k, place in enumerate(entries(roster_ref[level], blocks)):
        coeffs = ready_ref[k] + times(beside_ref[place] + corner_ref[place], wide_ref[k])
        signed = jnp.where(lane_low(coeffs.shape), coeffs, -coeffs)
        turned = pltpu.roll(coeffs, 64, axis=1)
        far = times(jnp.concatenate([signed, turned], axis=0), expand_ref[k])
        which = [n for n, (begin, count) in enumerate(NEAR_PARTS) if begin <= k < begin + count][0]
        total = far + near_refs[which][k - NEAR_PARTS[which][0]]
        half = total.shape[0] // 2
        lanes = pl.ds(128 * k, 128)
        out_ref[0, :, lanes] = total[:half]
        out_ref[1, :, lanes] = total[half:]
        if k % 4 == 3:
            part = pl.ds(128 * (k - 3), 512)
            copy = pltpu.make_async_copy(out_ref.at[:, :, part], out_hbm.at[:, :, part], sems.at[k // 4])
            copy.start()
            copies.append(copy)
    finish(copies)


def near_kernel(first, owner_ref, place_ref, valid_ref, pick_ref, own_ref, core_ref, far_ref, both_ref, weight_ref, *rest):
    out_ref = rest[-1]
    me = lax.axis_index("sub")
    for n in range(out_ref.shape[0]):
        k = first + n
        total = None
        for t in range(weight_ref.shape[1]):
            owner = owner_ref[t, k]
            leaf = pick_ref[owner, place_ref[t, k]]
            lanes = pl.ds(pl.multiple_of(leaf * 128, 128), 128)
            which = owner ^ me
            parts = []
            for d in range(2):
                low = jnp.where(which == 1, core_ref[d, :, lanes], own_ref[d, :, lanes])
                high = jnp.where(which == 3, both_ref[d, :, lanes], far_ref[d, :, lanes])
                parts.append(jnp.where(which >= 2, high, low))
            rows = jnp.concatenate(parts, axis=0) * valid_ref[t, k].astype(F32)
            result = product(rows, weight_ref[k, t].reshape(256, 128))
            half = result.shape[0] // 2
            term = jnp.concatenate(
                [result[:half, :128] - result[half:, 128:], result[half:, :128] + result[:half, 128:]], axis=0
            )
            total = term if total is None else total + term
        out_ref[n] = total


def spec(space):
    return pl.BlockSpec(memory_space=space)


def call(kernel, out, spaces, out_spaces=VMEM, scratch=(), flops=2_000_000):
    single = not isinstance(out_spaces, (list, tuple))
    return pl.pallas_call(
        kernel,
        out_shape=out,
        in_specs=[spec(space) for space in spaces],
        out_specs=spec(out_spaces) if single else [spec(space) for space in out_spaces],
        scratch_shapes=list(scratch),
        compiler_params=pltpu.CompilerParams(vmem_limit_bytes=8 << 20),
        cost_estimate=pl.CostEstimate(flops=flops, bytes_accessed=1 << 20, transcendentals=0),
    )


def in_hbm(*arrays):
    return [pltpu.with_memory_space_constraint(array, HBM) for array in arrays]


def flipped(value, leaf_mask, sub_mask):
    sub_count = lax.axis_size("sub")
    mask = leaf_mask * sub_count + sub_mask
    pairs = [(source, source ^ mask) for source in range(lax.axis_size("leaf") * sub_count)]
    return lax.ppermute(value, ("leaf", "sub"), pairs)


def tied(value, after):
    return lax.optimization_barrier((value, after))[0]


def on_device(
    field_in,
    compress,
    coupling,
    roster,
    expand,
    nearfield_dense_blocks,
    slot_owner_index,
    slot_source_position,
    slot_valid_mask,
    near_pick,
):
    blocks = compress.shape[0]
    rhs = field_in.shape[1]
    top = lax.axis_size("leaf") // 2
    pick = near_pick[0]
    indices = (slot_owner_index.T, slot_source_position.T, slot_valid_mask.T, pick)
    state = VMEM((blocks, rhs, 128), F32)
    wide = VMEM((blocks, 256, 128), BF)
    back = VMEM((8, 128), jnp.int32)
    packed = VMEM((blocks + 1, 64, 128), F32)
    level_weights = VMEM(coupling.shape[1:], F32)
    (coupling_hbm, _, roster_hbm) = in_hbm(coupling, field_in, roster)
    field = pltpu.with_memory_space_constraint(field_in, VMEM)
    dense = pltpu.with_memory_space_constraint(nearfield_dense_blocks, VMEM)
    expanding = pltpu.with_memory_space_constraint(expand, VMEM)

    def run(kernel, outs, inputs, after=(), scratch=(), hbm=()):
        spaces = [HBM if n in hbm else VMEM for n in range(len(inputs))] + [ANY] * len(after)
        several = isinstance(outs, list)
        return call(kernel, outs, spaces, [VMEM] * len(outs) if several else VMEM, scratch)(*inputs, *after)

    def near_piece(number, after):
        begin, count = NEAR_PARTS[number]
        return call(
            functools.partial(near_kernel, begin), VMEM((count, 2 * rhs, 128), F32), [SMEM] * 4 + [VMEM] * 5 + [ANY]
        )(*indices, field, core, far, both, dense, after)

    part = functools.partial
    coeffs, weight_4, names = run(
        compress_kernel,
        [state, level_weights, VMEM(roster.shape, jnp.int32)],
        [*in_hbm(field_in, compress), coupling_hbm, roster_hbm],
        scratch=[VMEM(field_in.shape, F32), VMEM(compress.shape, F32), DMA((5,))],
        hbm=(0, 1, 2, 3),
    )

    other = flipped(coeffs, top, 0)
    packed_4 = run(part(pack_kernel, 4), packed, [weight_4, names])
    away_4 = flipped(packed_4, top // 4, 0)
    ready, wide_0, back_0, own_4, wide_4, weight_1, weight_2, weight_6, weight_3 = run(
        first_kernel,
        [state, wide, back, wide, wide] + [level_weights] * 4,
        [coeffs, weight_4, names, coupling_hbm],
        scratch=[level_weights, DMA((5,))],
        hbm=(3,),
    )
    coeffs = run(level_kernel, state, [back_0, other, wide_0, ready])

    other = flipped(coeffs, top // 2, 0)
    ready, wide_1, back_1, own_2, wide_2, back_2 = run(
        part(ahead_kernel, 1), [state, wide, back, wide, wide, back], [coeffs, weight_1, names, weight_2]
    )
    own_6, wide_6, packed_6 = run(part(packed_kernel, 6), [wide, wide, packed], [weight_6, names], [ready])
    away_6 = flipped(tied(packed_6, coeffs), top, 0)
    coeffs = run(level_kernel, state, [back_1, other, wide_1, ready], [own_6])

    other = flipped(coeffs, top // 4, 0)
    far = flipped(tied(field_in, coeffs), 0, 2)
    ready = run(part(own_sorted_kernel, 2), state, [coeffs, own_2, names])
    own_3, wide_3, back_3 = run(part(sorted_kernel, 3), [wide, wide, back], [weight_3, names], [coeffs])
    coeffs = run(level_kernel, state, [back_2, other, wide_2, ready], [own_3])

    other = flipped(coeffs, 0, 1)
    ready = run(part(own_sorted_kernel, 3), state, [coeffs, own_3, names])
    coeffs = run(level_kernel, state, [back_3, other, wide_3, ready])

    corner = flipped(coeffs, top // 4, 2)
    ready = run(own_kernel, state, [coeffs, own_4])
    beside = flipped(ready, top // 4, 0)
    other = flipped(coeffs, 0, 2)
    own_5, wide_5, own_7, wide_7 = run(
        part(fetch_kernel, (5, 7)),
        [wide] * 4,
        [coupling_hbm],
        [coeffs],
        scratch=[level_weights, level_weights, DMA((2,))],
        hbm=(0,),
    )
    core = flipped(tied(field_in, coeffs), 0, 1)
    both = flipped(tied(far, coeffs), 0, 1)
    away = run(unpack_kernel, wide, [away_4], [coeffs])
    side = run(part(side_kernel, 5), state, [names, away_4, corner, away, beside, wide_5], scratch=[state])
    coeffs = run(part(double_kernel, 4), state, [names, other, wide_4, ready, own_5, side], [own_7], scratch=[state])

    other = flipped(coeffs, top // 2, 0)
    ready = run(own_kernel, state, [coeffs, own_6])
    corner = flipped(coeffs, top // 2 + top, 0)
    beside = flipped(ready, top, 0)
    last = run(spread_kernel, wide, [expanding], [coeffs])
    away = run(unpack_kernel, wide, [away_6], [coeffs])
    pieces = [near_piece(0, coeffs)]
    here = run(part(plain_kernel, 6), state, [names, other, wide_6, ready], [last, pieces[0]])
    ready = run(own_kernel, state, [here, own_7], [away])
    pieces.append(near_piece(1, ready))
    corner = run(corner_kernel, state, [away_6, corner, away])
    return call(
        part(last_kernel, 7),
        jax.ShapeDtypeStruct(field_in.shape, F32),
        [VMEM] * (6 + len(pieces)),
        HBM,
        [VMEM(field_in.shape, F32), DMA((3,))],
    )(names, beside, corner, wide_7, ready, last, *pieces)


def solution(mesh):
    return jax.shard_map(
        on_device,
        mesh=mesh,
        in_specs=(
            P(None, None, ("leaf", "sub")),
            P(("leaf", "sub"), None, None, None),
            P(None, ("leaf", "sub"), None, None, None),
            P(None, ("leaf", "sub"), None),
            P(("leaf", "sub"), None, None, None),
            P(("leaf", "sub"), None, None, None, None),
            P(("leaf", "sub"), None),
            P(("leaf", "sub"), None),
            P(("leaf", "sub"), None),
            P(("leaf", "sub"), None, None),
        ),
        out_specs=P(None, None, ("leaf", "sub")),
        check_vma=False,
    )
```

```python
import functools

import jax
import jax.numpy as jnp
from jax import lax
from jax.experimental import pallas as pl
from jax.experimental.pallas import tpu as pltpu
from jax.sharding import PartitionSpec as P


VMEM = pltpu.VMEM
SMEM = pltpu.SMEM
ANY = pl.ANY
HBM = pltpu.HBM
DMA = pltpu.SemaphoreType.DMA
BF = jnp.bfloat16
F32 = jnp.float32
NT = (((1,), (1,)), ((), ()))
NN = (((1,), (0,)), ((), ()))
NEAR_PARTS = ((0, 4), (4, 8))


def split(value):
    high = value.astype(BF)
    return high, (value - high.astype(F32)).astype(BF)


def widened(rows):
    high, low = split(rows)
    return jnp.concatenate(
        [
            jnp.concatenate([high, high], axis=1),
            jnp.concatenate([low, jnp.zeros_like(low)], axis=1),
        ],
        axis=0,
    )


def folded(result):
    count = result.shape[0] // 2
    return result[:count] + result[count:]


def product(rows, weights):
    wide = jnp.concatenate(split(weights), axis=1)
    return folded(lax.dot_general(widened(rows), wide, NT, preferred_element_type=F32))


def times(rows, wide):
    return folded(lax.dot_general(widened(rows), wide, NN, preferred_element_type=F32))


def lane_low(shape):
    return lax.broadcasted_iota(jnp.int32, shape, 1) < 64


def joined(result):
    rhs = result.shape[0] // 2
    turned = pltpu.roll(result[rhs:], 64, axis=1)
    return result[:rhs] + jnp.where(lane_low(turned.shape), -turned, turned)


def filled(upper):
    turned = pltpu.roll(upper, 64, axis=1)
    lower = jnp.where(lane_low(turned.shape), -turned, turned)
    return jnp.concatenate(split(jnp.concatenate([upper, lower], axis=0)), axis=0)


def halves(block):
    flat = block.T
    return flat[:64], flat[64:]


def started(pairs, sems):
    copies = [pltpu.make_async_copy(source, out, sems.at[n]) for n, (source, out) in enumerate(pairs)]
    for copy in copies:
        copy.start()
    return copies


def finish(copies):
    for copy in copies:
        copy.wait()


def compress_kernel(field_hbm, weight_hbm, coupling_hbm, roster_hbm, out_ref, next_ref, roster_ref, field_ref, weight_ref, sems):
    blocks = out_ref.shape[0]
    half = blocks // 2
    parts = [pl.ds(0, half), pl.ds(half, blocks - half)]
    copies = started(
        [(field_hbm, field_ref)]
        + [(weight_hbm.at[part], weight_ref.at[part]) for part in parts]
        + [(roster_hbm, roster_ref), (coupling_hbm.at[4], next_ref)],
        sems,
    )
    copies[0].wait()
    for k in range(blocks):
        if k % half == 0:
            copies[1 + k // half].wait()
        lanes = pl.ds(128 * k, 128)
        rows = jnp.concatenate([field_ref[0, :, lanes], field_ref[1, :, lanes]], axis=0)
        out_ref[k] = joined(product(rows, weight_ref[k].reshape(128, 128)))
    finish(copies[3:])


def entries(row, count):
    return [row[0, k].astype(jnp.int32) for k in range(count)]


def slots(row, count, back_ref):
    places = entries(row, count)
    lane = lax.broadcasted_iota(jnp.int32, back_ref.shape, 1)
    back = jnp.zeros(back_ref.shape, jnp.int32)
    for k, place in enumerate(places):
        back = jnp.where(lane == place, k, back)
    back_ref[...] = back
    return places


def put_row(packed_ref, row):
    blocks = row.shape[1]
    packed_ref[blocks, 0:8, 0:blocks] = jnp.broadcast_to(row.astype(F32), (8, blocks))


def packed_row(packed_ref, blocks):
    return entries(packed_ref[packed_ref.shape[0] - 1, 0:8, 0:blocks], blocks)


def prepare_block(k, place, weight_ref, own_out, other_out, packed_ref=None):
    own_half, other_half = halves(weight_ref[k].reshape(128, 128))
    own_out[k] = filled(own_half)
    other_out[place] = filled(other_half)
    if packed_ref is not None:
        packed_ref[k] = other_half


def start_level(level, own_ref, weight_ref, roster_ref, ready_out, other_out, back_ref):
    for k, place in enumerate(slots(roster_ref[level], own_ref.shape[0], back_ref)):
        own_half, other_half = halves(weight_ref[k].reshape(128, 128))
        other_out[place] = filled(other_half)
        ready_out[place] = times(own_ref[k], filled(own_half))


def pack_kernel(level, weight_ref, roster_ref, out_ref):
    put_row(out_ref, roster_ref[level])
    for k in range(weight_ref.shape[0]):
        out_ref[k] = halves(weight_ref[k].reshape(128, 128))[1]


def plain_weights_kernel(weight_ref, after_ref, own_out, other_out):
    for k in range(own_out.shape[0]):
        prepare_block(k, k, weight_ref, own_out, other_out)


def first_kernel(own_ref, roster_ref, coupling_hbm, *refs):
    ready_out, other_out, back_ref, *outs, weight_0, sems = refs
    pairs = zip((0, 1, 2, 6, 3), [weight_0] + outs)
    copies = started([(coupling_hbm.at[n], out) for n, out in pairs], sems)
    copies[0].wait()
    start_level(0, own_ref, weight_0, roster_ref, ready_out, other_out, back_ref)
    finish(copies[1:])


def ahead_kernel(level, own_ref, weight_ref, roster_ref, weight_2, *refs):
    ready_out, other_out, back_ref, own_2, other_2, back_2 = refs
    start_level(level, own_ref, weight_ref, roster_ref, ready_out, other_out, back_ref)
    for k, place in enumerate(slots(roster_ref[level + 1], own_ref.shape[0], back_2)):
        prepare_block(k, place, weight_2, own_2, other_2)


def sorted_kernel(level, weight_ref, roster_ref, after_ref, own_out, other_out, back_ref):
    for k, place in enumerate(slots(roster_ref[level], own_out.shape[0], back_ref)):
        prepare_block(k, place, weight_ref, own_out, other_out)


def packed_kernel(level, weight_ref, roster_ref, after_ref, own_out, other_out, packed_ref):
    put_row(packed_ref, roster_ref[level])
    for k in range(own_out.shape[0]):
        prepare_block(k, k, weight_ref, own_out, other_out, packed_ref)


def fetch_kernel(levels, coupling_hbm, after_ref, *refs):
    count = len(levels)
    outs, weights, sems = refs[: 2 * count], refs[2 * count : -1], refs[-1]
    copies = started([(coupling_hbm.at[level], out) for level, out in zip(levels, weights)], sems)
    for n in range(count):
        copies[n].wait()
        for k in range(weights[n].shape[0]):
            prepare_block(k, k, weights[n], outs[2 * n], outs[2 * n + 1])


def unpack_kernel(packed_ref, after_ref, out_ref):
    for k in range(out_ref.shape[0]):
        out_ref[k] = filled(packed_ref[k])


def spread_kernel(weight_ref, after_ref, out_ref):
    for k in range(out_ref.shape[0]):
        out_ref[k] = jnp.concatenate(split(weight_ref[k].reshape(128, 128)), axis=0)


def own_kernel(own_ref, wide_ref, *rest):
    out_ref = rest[-1]
    for k in range(out_ref.shape[0]):
        out_ref[k] = times(own_ref[k], wide_ref[k])


def own_sorted_kernel(level, own_ref, wide_ref, roster_ref, out_ref):
    for k, place in enumerate(entries(roster_ref[level], out_ref.shape[0])):
        out_ref[place] = times(own_ref[k], wide_ref[k])


def level_kernel(back_ref, other_ref, wide_ref, ready_ref, *rest):
    out_ref = rest[-1]
    for place, k in enumerate(entries(back_ref[0:1, :], out_ref.shape[0])):
        out_ref[k] = ready_ref[place] + times(other_ref[place], wide_ref[place])


def plain_kernel(level, roster_ref, other_ref, wide_ref, ready_ref, *rest):
    out_ref = rest[-1]
    for k, place in enumerate(entries(roster_ref[level], out_ref.shape[0])):
        out_ref[k] = ready_ref[k] + times(other_ref[place], wide_ref[k])


def side_kernel(level, roster_ref, packed_ref, corner_ref, away_ref, beside_ref, wide_ref, out_ref, there_ref):
    blocks = out_ref.shape[0]
    for k, place in enumerate(packed_row(packed_ref, out_ref.shape[0])):
        there_ref[k] = beside_ref[k] + times(corner_ref[place], away_ref[k])
    for k, place in enumerate(entries(roster_ref[level], blocks)):
        out_ref[k] = times(there_ref[place], wide_ref[k])


def double_kernel(level, roster_ref, other_ref, wide_ref, ready_ref, next_ref, side_ref, *rest):
    out_ref, here_ref = rest[-2:]
    for k, place in enumerate(entries(roster_ref[level], out_ref.shape[0])):
        here_ref[k] = ready_ref[k] + times(other_ref[place], wide_ref[k])
    for k in range(out_ref.shape[0]):
        out_ref[k] = side_ref[k] + times(here_ref[k], next_ref[k])


def corner_kernel(packed_ref, other_ref, wide_ref, out_ref):
    for k, place in enumerate(packed_row(packed_ref, out_ref.shape[0])):
        out_ref[k] = times(other_ref[place], wide_ref[k])


def last_kernel(level, roster_ref, beside_ref, corner_ref, wide_ref, ready_ref, expand_ref, *rest):
    near_refs, (out_hbm, out_ref, sems) = rest[:-3], rest[-3:]
    blocks = beside_ref.shape[0]
    copies = []
    for k, place in enumerate(entries(roster_ref[level], blocks)):
        coeffs = ready_ref[k] + times(beside_ref[place] + corner_ref[place], wide_ref[k])
        signed = jnp.where(lane_low(coeffs.shape), coeffs, -coeffs)
        turned = pltpu.roll(coeffs, 64, axis=1)
        far = times(jnp.concatenate([signed, turned], axis=0), expand_ref[k])
        which = [n for n, (begin, count) in enumerate(NEAR_PARTS) if begin <= k < begin + count][0]
        total = far + near_refs[which][k - NEAR_PARTS[which][0]]
        half = total.shape[0] // 2
        lanes = pl.ds(128 * k, 128)
        out_ref[0, :, lanes] = total[:half]
        out_ref[1, :, lanes] = total[half:]
        if k % 4 == 3:
            part = pl.ds(128 * (k - 3), 512)
            copy = pltpu.make_async_copy(out_ref.at[:, :, part], out_hbm.at[:, :, part], sems.at[k // 4])
            copy.start()
            copies.append(copy)
    finish(copies)


def near_kernel(first, owner_ref, place_ref, valid_ref, pick_ref, own_ref, core_ref, far_ref, both_ref, weight_ref, *rest):
    out_ref = rest[-1]
    me = lax.axis_index("sub")
    for n in range(out_ref.shape[0]):
        k = first + n
        total = None
        for t in range(weight_ref.shape[1]):
            owner = owner_ref[t, k]
            leaf = pick_ref[owner, place_ref[t, k]]
            lanes = pl.ds(pl.multiple_of(leaf * 128, 128), 128)
            which = owner ^ me
            parts = []
            for d in range(2):
                low = jnp.where(which == 1, core_ref[d, :, lanes], own_ref[d, :, lanes])
                high = jnp.where(which == 3, both_ref[d, :, lanes], far_ref[d, :, lanes])
                parts.append(jnp.where(which >= 2, high, low))
            rows = jnp.concatenate(parts, axis=0) * valid_ref[t, k].astype(F32)
            result = product(rows, weight_ref[k, t].reshape(256, 128))
            half = result.shape[0] // 2
            term = jnp.concatenate(
                [result[:half, :128] - result[half:, 128:], result[half:, :128] + result[:half, 128:]], axis=0
            )
            total = term if total is None else total + term
        out_ref[n] = total


def spec(space):
    return pl.BlockSpec(memory_space=space)


def call(kernel, out, spaces, out_spaces=VMEM, scratch=(), flops=2_000_000):
    single = not isinstance(out_spaces, (list, tuple))
    return pl.pallas_call(
        kernel,
        out_shape=out,
        in_specs=[spec(space) for space in spaces],
        out_specs=spec(out_spaces) if single else [spec(space) for space in out_spaces],
        scratch_shapes=list(scratch),
        compiler_params=pltpu.CompilerParams(vmem_limit_bytes=8 << 20),
        cost_estimate=pl.CostEstimate(flops=flops, bytes_accessed=1 << 20, transcendentals=0),
    )


def in_hbm(*arrays):
    return [pltpu.with_memory_space_constraint(array, HBM) for array in arrays]


def flipped(value, leaf_mask, sub_mask):
    sub_count = lax.axis_size("sub")
    mask = leaf_mask * sub_count + sub_mask
    pairs = [(source, source ^ mask) for source in range(lax.axis_size("leaf") * sub_count)]
    return lax.ppermute(value, ("leaf", "sub"), pairs)


def tied(value, after):
    return lax.optimization_barrier((value, after))[0]


def on_device(
    field_in,
    compress,
    coupling,
    roster,
    expand,
    nearfield_dense_blocks,
    slot_owner_index,
    slot_source_position,
    slot_valid_mask,
    near_pick,
):
    blocks = compress.shape[0]
    rhs = field_in.shape[1]
    top = lax.axis_size("leaf") // 2
    pick = near_pick[0]
    indices = (slot_owner_index.T, slot_source_position.T, slot_valid_mask.T, pick)
    state = VMEM((blocks, rhs, 128), F32)
    wide = VMEM((blocks, 256, 128), BF)
    back = VMEM((8, 128), jnp.int32)
    packed = VMEM((blocks + 1, 64, 128), F32)
    level_weights = VMEM(coupling.shape[1:], F32)
    (coupling_hbm, _, roster_hbm) = in_hbm(coupling, field_in, roster)
    field = pltpu.with_memory_space_constraint(field_in, VMEM)
    dense = pltpu.with_memory_space_constraint(nearfield_dense_blocks, VMEM)
    expanding = pltpu.with_memory_space_constraint(expand, VMEM)

    def run(kernel, outs, inputs, after=(), scratch=(), hbm=()):
        spaces = [HBM if n in hbm else VMEM for n in range(len(inputs))] + [ANY] * len(after)
        several = isinstance(outs, list)
        return call(kernel, outs, spaces, [VMEM] * len(outs) if several else VMEM, scratch)(*inputs, *after)

    def near_piece(number, after):
        begin, count = NEAR_PARTS[number]
        return call(
            functools.partial(near_kernel, begin), VMEM((count, 2 * rhs, 128), F32), [SMEM] * 4 + [VMEM] * 5 + [ANY]
        )(*indices, field, core, far, both, dense, after)

    part = functools.partial
    coeffs, weight_4, names = run(
        compress_kernel,
        [state, level_weights, VMEM(roster.shape, jnp.int32)],
        [*in_hbm(field_in, compress), coupling_hbm, roster_hbm],
        scratch=[VMEM(field_in.shape, F32), VMEM(compress.shape, F32), DMA((5,))],
        hbm=(0, 1, 2, 3),
    )

    other = flipped(coeffs, top, 0)
    packed_4 = run(part(pack_kernel, 4), packed, [weight_4, names])
    away_4 = flipped(packed_4, top // 4, 0)
    ready, wide_0, back_0, weight_1, weight_2, weight_6, weight_3 = run(
        first_kernel,
        [state, wide, back] + [level_weights] * 4,
        [coeffs, names, coupling_hbm],
        scratch=[level_weights, DMA((5,))],
        hbm=(2,),
    )
    coeffs = run(level_kernel, state, [back_0, other, wide_0, ready])

    other = flipped(coeffs, top // 2, 0)
    ready, wide_1, back_1, own_2, wide_2, back_2 = run(
        part(ahead_kernel, 1), [state, wide, back, wide, wide, back], [coeffs, weight_1, names, weight_2]
    )
    own_6, wide_6, packed_6 = run(part(packed_kernel, 6), [wide, wide, packed], [weight_6, names], [ready])
    away_6 = flipped(tied(packed_6, coeffs), top, 0)
    coeffs = run(level_kernel, state, [back_1, other, wide_1, ready], [own_6])

    other = flipped(coeffs, top // 4, 0)
    far = flipped(tied(field_in, coeffs), 0, 2)
    ready = run(part(own_sorted_kernel, 2), state, [coeffs, own_2, names])
    own_4, wide_4 = run(plain_weights_kernel, [wide, wide], [weight_4], [coeffs])
    own_3, wide_3, back_3 = run(part(sorted_kernel, 3), [wide, wide, back], [weight_3, names], [coeffs])
    coeffs = run(level_kernel, state, [back_2, other, wide_2, ready], [own_3, own_4])

    other = flipped(coeffs, 0, 1)
    ready = run(part(own_sorted_kernel, 3), state, [coeffs, own_3, names])
    coeffs = run(level_kernel, state, [back_3, other, wide_3, ready])

    corner = flipped(coeffs, top // 4, 2)
    ready = run(own_kernel, state, [coeffs, own_4])
    beside = flipped(ready, top // 4, 0)
    other = flipped(coeffs, 0, 2)
    own_5, wide_5, own_7, wide_7 = run(
        part(fetch_kernel, (5, 7)),
        [wide] * 4,
        [coupling_hbm],
        [coeffs],
        scratch=[level_weights, level_weights, DMA((2,))],
        hbm=(0,),
    )
    core = flipped(tied(field_in, coeffs), 0, 1)
    both = flipped(tied(far, coeffs), 0, 1)
    away = run(unpack_kernel, wide, [away_4], [coeffs])
    side = run(part(side_kernel, 5), state, [names, away_4, corner, away, beside, wide_5], scratch=[state])
    coeffs = run(part(double_kernel, 4), state, [names, other, wide_4, ready, own_5, side], [own_7], scratch=[state])

    other = flipped(coeffs, top // 2, 0)
    ready = run(own_kernel, state, [coeffs, own_6])
    corner = flipped(coeffs, top // 2 + top, 0)
    beside = flipped(ready, top, 0)
    last = run(spread_kernel, wide, [expanding], [coeffs])
    away = run(unpack_kernel, wide, [away_6], [coeffs])
    pieces = [near_piece(0, coeffs)]
    here = run(part(plain_kernel, 6), state, [names, other, wide_6, ready], [last, pieces[0]])
    ready = run(own_kernel, state, [here, own_7], [away])
    pieces.append(near_piece(1, ready))
    corner = run(corner_kernel, state, [away_6, corner, away])
    return call(
        part(last_kernel, 7),
        jax.ShapeDtypeStruct(field_in.shape, F32),
        [VMEM] * (6 + len(pieces)),
        HBM,
        [VMEM(field_in.shape, F32), DMA((3,))],
    )(names, beside, corner, wide_7, ready, last, *pieces)


def solution(mesh):
    return jax.shard_map(
        on_device,
        mesh=mesh,
        in_specs=(
            P(None, None, ("leaf", "sub")),
            P(("leaf", "sub"), None, None, None),
            P(None, ("leaf", "sub"), None, None, None),
            P(None, ("leaf", "sub"), None),
            P(("leaf", "sub"), None, None, None),
            P(("leaf", "sub"), None, None, None, None),
            P(("leaf", "sub"), None),
            P(("leaf", "sub"), None),
            P(("leaf", "sub"), None),
            P(("leaf", "sub"), None, None),
        ),
        out_specs=P(None, None, ("leaf", "sub")),
        check_vma=False,
    )
```
